128 devices in a mesh: segment: 2 (over y_lo), ctx: 8 (over y_hi, z), tp: 8 (over x, core).
Axes of the slice: x: 4, y: 4 (y_hi: 2, y_lo: 2; y = y_hi * 2 + y_lo), z: 4, core: 2. Of those that a mesh axis runs over, the one named last changes fastest.
Arguments:
- stash_inputs: bfloat16 [2, 4, 2048, 3840], P('segment', None, ('ctx', 'tp')), may hold values from -12 to 12
- stash_grads: bfloat16 [2, 4, 2048, 3840], P('segment', None, ('ctx', 'tp')), may hold values from -6 to 6
- plan: int32 [2, 4], P('segment'), may hold values from 0 to 3, each once within a row
- query_weight: bfloat16 [2, 2, 3840, 4096], P('segment', None, None, 'tp'), may hold values from -0.1 to 0.1
- key_weight: bfloat16 [2, 2, 3840, 2048], P('segment', None, None, 'tp'), may hold values from -0.1 to 0.1
- value_weight: bfloat16 [2, 2, 3840, 2048], P('segment', None, None, 'tp'), may hold values from -0.09375 to 0.09375
- out_weight: bfloat16 [2, 2, 4096, 3840], P('segment', None, 'tp'), may hold values from -0.09375 to 0.09375
- input_gain: float32 [2, 2, 3840], P('segment'), may hold values from 0.1 to 1.9
- output_gain: float32 [2, 2, 3840], P('segment'), may hold values from 0.1 to 1.9
- query_gain: float32 [2, 2, 256], P('segment'), may hold values from 0.5 to 6
- key_gain: float32 [2, 2, 256], P('segment'), may hold values from 0.5 to 6
Outputs:
- arrived_act: bfloat16 [2, 2048, 3840], P('segment', ('ctx', 'tp'))
- arrived_grad: bfloat16 [2, 2048, 3840], P('segment', ('ctx', 'tp'))
The draws below stay inside these ranges and needn't reach their ends.
Inputs may be any that keep to these rules, and one draw needn't show every extreme that they name: `plan`: row s names each of the 4 micro-batches once; its first entry is run forward and its second through its input gradient.
All inputs are finite; a program needn't handle non-finite values.
Results may differ from the reference program's by a relative error of at most 0.019.
The reference program's roundings to bfloat16 on the way count: a program that leaves them out, or rounds other values in their place, can miss the bound.
Values may be sent and summed in bfloat16 or wider, within the bound.
A program may use at most 128 MiB of HBM per device.

```python
import math
import jax
import jax.numpy as jnp
from jax import lax

D = 3840
HEADS = 16
KV_HEADS = 8
HEAD_DIM = 256
WINDOW = 1024
TOK_DEV = 256
MICRO = 4
LEGS = 2
SEGMENTS = 2
TOKENS = 2048
N_CTX = 8
N_TP = 8


def draw_stash_inputs(key, part):
    base_key = jax.random.fold_in(key, 505)
    first_key, second_key = jax.random.split(base_key)
    shape = (SEGMENTS, MICRO, TOKENS, D)
    base = jax.random.normal(first_key, shape, jnp.float32)
    scales = 0.3 * jnp.exp(jax.random.uniform(second_key, (SEGMENTS, MICRO, TOKENS, 1), jnp.float32, 0.0, math.log(10.0)))
    return jnp.clip(base * scales, -12.0, 12.0).astype(jnp.bfloat16)


def query_base(key):
    base_key = jax.random.fold_in(key, 101)
    shape = (SEGMENTS, LEGS, D, HEADS * HEAD_DIM)
    base = jax.random.normal(base_key, shape, jnp.float32)
    return base * D ** (-0.5)


def draw_query_weight(key, part):
    return jnp.clip(query_base(key), -0.09, 0.09).astype(jnp.bfloat16)


def draw_key_weight(key, part):
    noise_key = jax.random.fold_in(key, 202)
    shape = (SEGMENTS, LEGS, D, KV_HEADS * HEAD_DIM)
    result = jax.random.normal(noise_key, shape, jnp.float32) * D ** (-0.5)
    return jnp.clip(result, -0.09, 0.09).astype(jnp.bfloat16)


def gain_values(key, salt):
    gain_key = jax.random.fold_in(key, salt)
    shape = (SEGMENTS, LEGS, HEAD_DIM)
    return jnp.exp(jax.random.uniform(gain_key, shape, jnp.float32, math.log(0.5), math.log(2.0)))


def draw_query_gain(key, part):
    return gain_values(key, 303)


def draw_key_gain(key, part):
    return gain_values(key, 404)


def shard_levels(rng, extent, shards, smallest, largest):
    def one(axis_at, parts):
        steps = jax.random.uniform(jax.random.fold_in(jax.random.fold_in(rng, 6), axis_at), (parts,), jnp.float32, smallest / len(shards), largest / len(shards))
        return jnp.repeat(jnp.exp(steps), extent[axis_at] // parts).reshape((-1,) + (1,) * (len(extent) - axis_at - 1))

    level = one(*shards[0])
    for cut in shards[1:]:
        level = level * one(*cut)
    return level


def normal_values(rng, dims, spread, limit, shards=(), kind=jnp.bfloat16):
    values = jax.random.normal(rng, dims, jnp.float32) * spread
    if len(shards) > 0:
        values = shard_levels(rng, dims, shards, -0.22, 0.18) * values
    return jnp.clip(values, min=-limit, max=limit).astype(kind)


def setup_inputs(seed: int = 0) -> dict:
    arg_keys = jax.random.split(jax.random.key(seed), 12)
    stash_inputs = draw_stash_inputs(jax.random.fold_in(arg_keys[11], 71), 0)
    stash_grads = normal_values(arg_keys[1], (SEGMENTS, MICRO, TOKENS, D), 1.0, 6.0, ((0, 2), (2, 64)))
    plan = jax.vmap(lambda own: jax.random.permutation(own, MICRO))(jax.random.split(arg_keys[2], SEGMENTS)).reshape((SEGMENTS, MICRO)).astype(jnp.int32)
    query_weight = draw_query_weight(jax.random.fold_in(arg_keys[11], 71), 0)
    key_weight = draw_key_weight(jax.random.fold_in(arg_keys[11], 71), 0)
    value_weight = normal_values(arg_keys[5], (SEGMENTS, LEGS, D, KV_HEADS * HEAD_DIM), D ** -0.5, 0.09375, ((0, 2), (3, 8)))
    out_weight = normal_values(arg_keys[6], (SEGMENTS, LEGS, HEADS * HEAD_DIM, D), (HEADS * HEAD_DIM) ** -0.5, 0.09375, ((0, 2), (2, 8)))
    input_gain = jnp.clip(1.0 + 0.18 * jax.random.normal(arg_keys[7], (SEGMENTS, LEGS, D), jnp.float32), 0.1, 1.9)
    output_gain = jnp.clip(1.0 + 0.18 * jax.random.normal(arg_keys[8], (SEGMENTS, LEGS, D), jnp.float32), 0.1, 1.9)
    query_gain = draw_query_gain(jax.random.fold_in(arg_keys[11], 71), 0)
    key_gain = draw_key_gain(jax.random.fold_in(arg_keys[11], 71), 0)
    return {"stash_inputs": stash_inputs, "stash_grads": stash_grads, "plan": plan, "query_weight": query_weight, "key_weight": key_weight, "value_weight": value_weight, "out_weight": out_weight, "input_gain": input_gain, "output_gain": output_gain, "query_gain": query_gain, "key_gain": key_gain}


epsilon = 1e-06
rope_base = 10000.0
masked_score = -1e+30

def rms_scale(operand, gain):
    return operand * lax.rsqrt(lax.optimization_barrier(jnp.mean(operand * operand, axis=-1, keepdims=True)) + epsilon) * gain

def rotate(normed, positions):
    half_width = normed.shape[-1] // 2
    frequency = rope_base ** (-(jnp.arange(half_width).astype(normed.dtype) * 2.0 / normed.shape[-1]))
    angles = positions.astype(normed.dtype)[:, None] * frequency[None, :]
    cosine = jnp.cos(angles)[:, None, :]
    sines = jnp.sin(angles)[:, None, :]
    front_half = normed[..., :half_width]
    back_half = normed[..., half_width:]
    return jnp.concatenate([front_half * cosine - back_half * sines, back_half * cosine + front_half * sines], axis=-1)

def head_norm(raw_heads, gain, positions):
    return rotate(rms_scale(raw_heads, gain), positions)

def block_probs(query_block, key_block, query_place, key_place):
    groups = HEADS // KV_HEADS
    grouped = query_block.reshape(query_block.shape[0], KV_HEADS, groups, HEAD_DIM).astype(jnp.float32)
    scores = jnp.einsum('tkgd,skd->kgts', grouped, key_block.astype(jnp.float32)) * HEAD_DIM ** (-0.5)
    visible = (key_place[None, :] >= 0) & (key_place[None, :] <= query_place[:, None]) & (key_place[None, :] > query_place[:, None] - WINDOW)
    scores = jnp.where(visible, scores, masked_score)
    highest = lax.optimization_barrier(jnp.max(scores, axis=-1, keepdims=True))
    raised = jnp.exp(scores - highest)
    return raised / lax.optimization_barrier(jnp.sum(raised, axis=-1, keepdims=True))

def padded(rows_in):
    return jnp.concatenate([jnp.zeros((WINDOW, KV_HEADS, HEAD_DIM), rows_in.dtype), rows_in], axis=0)

def block_slices(queries, key_pad, value_pad, start):
    query_block = lax.dynamic_slice_in_dim(queries, start, TOK_DEV, 0)
    key_block = lax.dynamic_slice_in_dim(key_pad, start, WINDOW + TOK_DEV, 0)
    value_block = lax.dynamic_slice_in_dim(value_pad, start, WINDOW + TOK_DEV, 0)
    query_place = start + jnp.arange(TOK_DEV, dtype=jnp.int32)
    key_place = start - WINDOW + jnp.arange(WINDOW + TOK_DEV, dtype=jnp.int32)
    return (query_block, key_block, value_block, query_place, key_place)

def attention_out(queries, keys, values):
    key_pad = padded(keys)
    value_pad = padded(values)
    starts = jnp.arange(N_CTX, dtype=jnp.int32) * TOK_DEV

    def per_block(start):
        query_block, key_block, value_block, query_place, key_place = block_slices(queries, key_pad, value_pad, start)
        probs = block_probs(query_block, key_block, query_place, key_place)
        weighting_low = lax.optimization_barrier(probs.astype(jnp.bfloat16)).astype(jnp.float32)
        context = jnp.einsum('kgts,skd->tkgd', weighting_low, value_block.astype(jnp.float32))
        return context.astype(jnp.bfloat16).reshape(TOK_DEV, HEADS * HEAD_DIM)
    blocks = lax.map(per_block, starts)
    return blocks.reshape(N_CTX * TOK_DEV, HEADS * HEAD_DIM)

def attention_back(queries, keys, values, context_grad):
    key_pad = padded(keys)
    value_pad = padded(values)
    groups = HEADS // KV_HEADS
    grad_grouped = context_grad.reshape(context_grad.shape[0], KV_HEADS, groups, HEAD_DIM)
    starts = jnp.arange(N_CTX, dtype=jnp.int32) * TOK_DEV

    def per_block(carried, start):
        key_acc, value_acc = carried
        query_block, key_block, value_block, query_place, key_place = block_slices(queries, key_pad, value_pad, start)
        grad_block = lax.dynamic_slice_in_dim(grad_grouped, start, TOK_DEV, 0).astype(jnp.float32)
        probs = block_probs(query_block, key_block, query_place, key_place)
        weighting_low = lax.optimization_barrier(probs.astype(jnp.bfloat16)).astype(jnp.float32)
        weight_grad = jnp.einsum('tkgd,skd->kgts', grad_block, value_block.astype(jnp.float32))
        score_grad = probs * (weight_grad - lax.optimization_barrier(jnp.sum(weight_grad * probs, axis=-1, keepdims=True))) * HEAD_DIM ** (-0.5)
        score_grad = lax.optimization_barrier(score_grad.astype(jnp.bfloat16)).astype(jnp.float32)
        grouped = query_block.reshape(TOK_DEV, KV_HEADS, groups, HEAD_DIM).astype(jnp.float32)
        query_grad = jnp.einsum('kgts,skd->tkgd', score_grad, key_block.astype(jnp.float32)).reshape(TOK_DEV, HEADS, HEAD_DIM)
        key_grad = jnp.einsum('kgts,tkgd->skd', score_grad, grouped)
        value_grad = jnp.einsum('kgts,tkgd->skd', weighting_low, grad_block)
        key_acc = lax.dynamic_update_slice_in_dim(key_acc, lax.dynamic_slice_in_dim(key_acc, start, WINDOW + TOK_DEV, 0) + key_grad, start, 0)
        value_acc = lax.dynamic_update_slice_in_dim(value_acc, lax.dynamic_slice_in_dim(value_acc, start, WINDOW + TOK_DEV, 0) + value_grad, start, 0)
        return ((key_acc, value_acc), query_grad)
    zeros_pad = jnp.zeros((WINDOW + N_CTX * TOK_DEV, KV_HEADS, HEAD_DIM), jnp.float32)
    (key_acc, value_acc), query_grad = lax.scan(per_block, (zeros_pad, zeros_pad), starts)
    return (query_grad.reshape(N_CTX * TOK_DEV, HEADS, HEAD_DIM), key_acc[WINDOW:], value_acc[WINDOW:])

def group_sum(group_term, token_count):

    def add_group(group, running):
        partial_term = group_term(group.astype(jnp.int32))
        return running + lax.optimization_barrier(partial_term.astype(jnp.bfloat16)).astype(jnp.float32)
    return lax.fori_loop(0, N_TP, add_group, jnp.zeros((token_count, D), jnp.float32))

def layer_front(layer_input, query_proj, key_proj, value_proj, in_gain, q_gain, k_gain):
    token_count = layer_input.shape[0]
    wide_input = layer_input.astype(jnp.float32)
    normed = rms_scale(wide_input, in_gain).astype(jnp.bfloat16)
    positions = jnp.arange(token_count, dtype=jnp.int32)
    query_raw = jnp.dot(normed, query_proj, preferred_element_type=jnp.float32).reshape(token_count, HEADS, HEAD_DIM)
    key_raw = jnp.dot(normed, key_proj, preferred_element_type=jnp.float32).reshape(token_count, KV_HEADS, HEAD_DIM)
    values = jnp.dot(normed, value_proj, preferred_element_type=jnp.float32).astype(jnp.bfloat16).reshape(token_count, KV_HEADS, HEAD_DIM)
    queries = head_norm(query_raw, q_gain, positions).astype(jnp.bfloat16)
    keys = head_norm(key_raw, k_gain, positions).astype(jnp.bfloat16)
    return (wide_input, positions, query_raw, key_raw, queries, keys, values)

def out_sum(context, out_proj):
    query_cols = HEADS * HEAD_DIM // N_TP

    def group_term(group):
        return jnp.dot(lax.dynamic_slice_in_dim(context, group * query_cols, query_cols, 1), lax.dynamic_slice_in_dim(out_proj, group * query_cols, query_cols, 0), preferred_element_type=jnp.float32)
    return group_sum(group_term, context.shape[0])

def forward_layer(layer_input, query_proj, key_proj, value_proj, out_proj, in_gain, post_gain, q_gain, k_gain):
    wide_input, positions, query_raw, key_raw, queries, keys, values = layer_front(layer_input, query_proj, key_proj, value_proj, in_gain, q_gain, k_gain)
    projected = out_sum(attention_out(queries, keys, values), out_proj)
    return (wide_input + rms_scale(projected, post_gain)).astype(jnp.bfloat16)

def backward_layer(layer_input, incoming, query_proj, key_proj, value_proj, out_proj, in_gain, post_gain, q_gain, k_gain):
    wide_input, positions, query_raw, key_raw, queries, keys, values = layer_front(layer_input, query_proj, key_proj, value_proj, in_gain, q_gain, k_gain)
    token_count = layer_input.shape[0]
    projected = out_sum(attention_out(queries, keys, values), out_proj)
    wide_grad = incoming.astype(jnp.float32)
    out_grad = jax.vjp(lambda operand: rms_scale(operand, post_gain), projected)[1](wide_grad)[0].astype(jnp.bfloat16)
    context_grad = jnp.dot(out_grad, out_proj.T, preferred_element_type=jnp.float32).astype(jnp.bfloat16)
    query_grad, key_grad, value_grad = attention_back(queries, keys, values, context_grad)
    query_low = jax.vjp(lambda operand: head_norm(operand, q_gain, positions), query_raw)[1](query_grad)[0].astype(jnp.bfloat16).reshape(token_count, HEADS * HEAD_DIM)
    key_low = jax.vjp(lambda operand: head_norm(operand, k_gain, positions), key_raw)[1](key_grad)[0].astype(jnp.bfloat16).reshape(token_count, KV_HEADS * HEAD_DIM)
    value_low = value_grad.astype(jnp.bfloat16).reshape(token_count, KV_HEADS * HEAD_DIM)
    query_cols = HEADS * HEAD_DIM // N_TP
    key_cols = KV_HEADS * HEAD_DIM // N_TP

    def group_term(group):
        summed = jnp.dot(lax.dynamic_slice_in_dim(query_low, group * query_cols, query_cols, 1), lax.dynamic_slice_in_dim(query_proj, group * query_cols, query_cols, 1).T, preferred_element_type=jnp.float32)
        summed = summed + jnp.dot(lax.dynamic_slice_in_dim(key_low, group * key_cols, key_cols, 1), lax.dynamic_slice_in_dim(key_proj, group * key_cols, key_cols, 1).T, preferred_element_type=jnp.float32)
        summed = summed + jnp.dot(lax.dynamic_slice_in_dim(value_low, group * key_cols, key_cols, 1), lax.dynamic_slice_in_dim(value_proj, group * key_cols, key_cols, 1).T, preferred_element_type=jnp.float32)
        return summed
    hidden_grad = group_sum(group_term, token_count)
    outgoing = wide_grad + jax.vjp(lambda operand: rms_scale(operand, in_gain), wide_input)[1](hidden_grad)[0]
    return outgoing.astype(jnp.bfloat16)

def reference(stash_inputs, stash_grads, plan, query_weight, key_weight, value_weight, out_weight, input_gain, output_gain, query_gain, key_gain):
    forward_rows = []
    backward_rows = []
    for segment_index in range(SEGMENTS):
        forward_batch = plan[segment_index, 0]
        backward_batch = plan[segment_index, 1]

        def layer_set(leg_index):
            return (query_weight[segment_index, leg_index], key_weight[segment_index, leg_index], value_weight[segment_index, leg_index], out_weight[segment_index, leg_index], input_gain[segment_index, leg_index], output_gain[segment_index, leg_index], query_gain[segment_index, leg_index], key_gain[segment_index, leg_index])
        forward_in = lax.dynamic_index_in_dim(stash_inputs[segment_index], forward_batch, 0, keepdims=False)
        backward_in = lax.dynamic_index_in_dim(stash_inputs[segment_index], backward_batch, 0, keepdims=False)
        incoming = lax.dynamic_index_in_dim(stash_grads[segment_index], backward_batch, 0, keepdims=False)
        forward_rows.append(forward_layer(forward_in, *layer_set(segment_index)))
        backward_rows.append(backward_layer(backward_in, incoming, *layer_set(1 - segment_index)))
    arrived_act = jnp.stack(forward_rows[::-1])
    arrived_grad = jnp.stack(backward_rows[::-1])
    return (arrived_act, arrived_grad)
```

```python
import jax
import jax.numpy as jnp
from jax import lax
from jax.experimental import pallas as pl
from jax.experimental.pallas import tpu as pltpu
from jax.sharding import PartitionSpec as P

WINDOW = 1024
epsilon = 1e-06
rope_base = 10000.0
masked_score = -1e30

D = 3840
ROWS = 32
TOK = 256
HD = 256
NCH = 3
CW = D // NCH
BACK, FWD, GRAD = 0, 1, 2
f32 = jnp.float32
bf16 = jnp.bfloat16
MESH = pl.DeviceIdType.MESH


def dot(a, b):
    return lax.dot_general(a, b, (((1,), (0,)), ((), ())), preferred_element_type=f32)


def dot_nt(a, b):
    return lax.dot_general(a, b, (((1,), (1,)), ((), ())), preferred_element_type=f32)


def dot_tn(a, b):
    return lax.dot_general(a, b, (((0,), (0,)), ((), ())), preferred_element_type=f32)


def rms_of(x):
    return lax.rsqrt(jnp.mean(x * x, axis=-1, keepdims=True) + epsilon)


def rms_back(x, grad, gain):
    g = grad * gain
    r = rms_of(x)
    return r * (g - x * (r * r * jnp.mean(g * x, axis=-1, keepdims=True)))


def rope(y, cosine, sine):
    a, b = y[:, : HD // 2], y[:, HD // 2 :]
    return jnp.concatenate([a * cosine - b * sine, b * cosine + a * sine], axis=-1)


def rope_back(g, cosine, sine):
    a, b = g[:, : HD // 2], g[:, HD // 2 :]
    return jnp.concatenate([a * cosine + b * sine, b * cosine - a * sine], axis=-1)


def kernel(
    plan, cos_ref, sin_ref, ig, og, qg, kg, si, sg, wq_h, wk_h, wv_h, wo_h,
    act_out, grad_out,
    wq, wk, wv, wo, sti, stg, ag, qs, qraw, kraw, kvs, kvrl, cx, pw, pl_s, dss, cgs,
    ps, pr, sb, rl, fr, own, gs, gr, gacc, lq, fo, go,
    lsem, ags, agr, rss, rsr, kss, ksr, gss, gsr, swap_s, swap_r,
):
    s = lax.axis_index("segment")
    p = lax.axis_index("ctx")
    t = lax.axis_index("tp")
    yh, z = p // 4, p % 4
    y = 2 * yh + s
    x, c = t // 2, t % 2
    legs = (1 - s, s)

    def dev(s_=None, p_=None, t_=None):
        return {
            "segment": s if s_ is None else s_,
            "ctx": p if p_ is None else p_,
            "tp": t if t_ is None else t_,
        }

    t_r, t_l = ((x + 1) % 4) * 2 + c, ((x + 3) % 4) * 2 + c
    t_o = ((x + 2) % 4) * 2 + c
    t_p = 2 * x + 1 - c
    right, left, partner = dev(t_=t_r), dev(t_=t_l), dev(t_=t_p)
    z_up, z_dn = dev(p_=4 * yh + (z + 1) % 4), dev(p_=4 * yh + (z + 3) % 4)
    y_u, y_d = (y + 1) % 4, (y + 3) % 4
    y_up = dev(s_=y_u % 2, p_=(y_u // 2) * 4 + z)
    y_dn = dev(s_=y_d % 2, p_=(y_d // 2) * 4 + z)
    other = dev(s_=1 - s)

    barrier = pltpu.get_barrier_semaphore()
    for device in (right, left, partner, z_up, z_dn, y_up, y_dn):
        pl.semaphore_signal(barrier, inc=1, device_id=device, device_id_type=MESH)

    loads = [
        pltpu.make_async_copy(si, sti, lsem.at[0]),
        pltpu.make_async_copy(sg, stg, lsem.at[1]),
    ]
    for j in range(2):
        loads += [
            pltpu.make_async_copy(wq_h.at[legs[j]], wq.at[j], lsem.at[2 + 4 * j]),
            pltpu.make_async_copy(wk_h.at[legs[j]], wk.at[j], lsem.at[3 + 4 * j]),
            pltpu.make_async_copy(wv_h.at[legs[j]], wv.at[j], lsem.at[4 + 4 * j]),
            pltpu.make_async_copy(wo_h.at[legs[j]], wo.at[j], lsem.at[5 + 4 * j]),
        ]
    for load in loads:
        load.start()

    def gain(ref, j):
        return ref[pl.ds(legs[j], 1), :]

    def rcopy(src, dst, ssem, rsem, device):
        return pltpu.make_async_remote_copy(
            src_ref=src, dst_ref=dst, send_sem=ssem, recv_sem=rsem,
            device_id=device, device_id_type=MESH,
        )

    drains = []

    def when(cond, run):
        if cond is None:
            run()
        else:
            pl.when(cond)(run)

    def send(copy, cond=None):
        when(cond, copy.start)
        drains.append((copy, cond))

    def arrive(dst, rsem, cond=None):
        copy = rcopy(dst, dst, swap_s.at[0], rsem, partner)
        when(cond, copy.wait_recv)

    H0, H1 = pl.ds(0, ROWS // 2), pl.ds(ROWS // 2, ROWS // 2)
    halves = (H0, H1)

    def gather_start(j):
        blk = ag.at[j, t]
        send(rcopy(blk.at[H0], blk.at[H0], ags.at[j, 0], agr.at[j, 0], right))
        send(rcopy(blk.at[H1], blk.at[H1], ags.at[j, 1], agr.at[j, 1], left))
        send(rcopy(blk.at[H1], blk.at[H1], ags.at[j, 2], agr.at[j, 2], right))
        send(rcopy(blk.at[H0], blk.at[H0], ags.at[j, 3], agr.at[j, 3], left))
        send(rcopy(blk, blk, ags.at[j, 6], agr.at[j, 6], partner))

    def across(j, place, half, i):
        part = ag.at[j, place, halves[half]]
        send(rcopy(part, part, ags.at[j, i], agr.at[j, i], partner))

    def gather_relay(j):
        a = ag.at[j, t_l, H0]
        arrive(a, agr.at[j, 0])
        send(rcopy(a, a, ags.at[j, 4], agr.at[j, 4], right))
        b = ag.at[j, t_r, H1]
        arrive(b, agr.at[j, 1])
        send(rcopy(b, b, ags.at[j, 5], agr.at[j, 5], left))
        across(j, t_l, 0, 7)
        across(j, t_r, 1, 8)

    def gather_finish(j):
        arrive(ag.at[j, t_l, H1], agr.at[j, 2])
        across(j, t_l, 1, 9)
        arrive(ag.at[j, t_r, H0], agr.at[j, 3])
        across(j, t_r, 0, 10)
        arrive(ag.at[j, t_o, H0], agr.at[j, 4])
        across(j, t_o, 0, 11)
        arrive(ag.at[j, t_o, H1], agr.at[j, 5])
        across(j, t_o, 1, 12)
        u_r, u_l, u_o = t_r + 1 - 2 * c, t_l + 1 - 2 * c, t_o + 1 - 2 * c
        arrive(ag.at[j, t_p], agr.at[j, 6])
        arrive(ag.at[j, u_l, H0], agr.at[j, 7])
        arrive(ag.at[j, u_r, H1], agr.at[j, 8])
        arrive(ag.at[j, u_l, H1], agr.at[j, 9])
        arrive(ag.at[j, u_r, H0], agr.at[j, 10])
        arrive(ag.at[j, u_o, H0], agr.at[j, 11])
        arrive(ag.at[j, u_o, H1], agr.at[j, 12])

    def cols(n):
        return pl.ds(n * CW, CW)

    def rows_of(ref, parity):
        parts = [ref[2 * ((x + k) % 4) + parity] for k in range(4)]
        return jnp.concatenate(parts, axis=0)

    def scatter_first(r, product, lhs_of):
        lhs = lhs_of(1 - c)
        for n in range(NCH):
            ps[r % 2, :, :, cols(n)] = product(lhs, n).astype(bf16).reshape(4, ROWS, CW)
            send(rcopy(ps.at[r % 2, :, :, cols(n)], pr.at[r, :, :, cols(n)],
                       rss.at[r, n, 0], rsr.at[r, n, 0], partner))

    def scatter_second(r, product, lhs_of):
        lhs = lhs_of(c)
        for n in range(NCH):
            arrive(pr.at[r, :, :, cols(n)], rsr.at[r, n, 0])
            total = product(lhs, n).reshape(4, ROWS, CW) + pr[r, :, :, cols(n)].astype(f32)
            own[r, :, cols(n)] = total[0]
            sb[r, :, :, cols(n)] = total[1:].astype(bf16)
            send(rcopy(sb.at[r, 1, H0, cols(n)], rl.at[r, 0, :, cols(n)],
                       rss.at[r, n, 1], rsr.at[r, n, 1], right))
            send(rcopy(sb.at[r, 1, H1, cols(n)], rl.at[r, 1, :, cols(n)],
                       rss.at[r, n, 2], rsr.at[r, n, 2], left))
            send(rcopy(sb.at[r, 0, H1, cols(n)], fr.at[r, 0, H1, cols(n)],
                       rss.at[r, n, 3], rsr.at[r, n, 3], right))
            send(rcopy(sb.at[r, 2, H0, cols(n)], fr.at[r, 1, H0, cols(n)],
                       rss.at[r, n, 4], rsr.at[r, n, 4], left))

    def scatter_relay(r):
        for n in range(NCH):
            arrive(rl.at[r, 0, :, cols(n)], rsr.at[r, n, 1])
            sb[r, 0, H0, cols(n)] = (
                sb[r, 0, H0, cols(n)].astype(f32) + rl[r, 0, :, cols(n)].astype(f32)
            ).astype(bf16)
            send(rcopy(sb.at[r, 0, H0, cols(n)], fr.at[r, 0, H0, cols(n)],
                       rss.at[r, n, 5], rsr.at[r, n, 5], right))
            arrive(rl.at[r, 1, :, cols(n)], rsr.at[r, n, 2])
            sb[r, 2, H1, cols(n)] = (
                sb[r, 2, H1, cols(n)].astype(f32) + rl[r, 1, :, cols(n)].astype(f32)
            ).astype(bf16)
            send(rcopy(sb.at[r, 2, H1, cols(n)], fr.at[r, 1, H1, cols(n)],
                       rss.at[r, n, 6], rsr.at[r, n, 6], left))

    def scatter_finish(r):
        for n in range(NCH):
            arrive(fr.at[r, 0, H1, cols(n)], rsr.at[r, n, 3])
            arrive(fr.at[r, 1, H0, cols(n)], rsr.at[r, n, 4])
            arrive(fr.at[r, 0, H0, cols(n)], rsr.at[r, n, 5])
            arrive(fr.at[r, 1, H1, cols(n)], rsr.at[r, n, 6])
        return own[r] + fr[r, 0].astype(f32) + fr[r, 1].astype(f32)

    hi, lo = yh == 1, yh == 0
    mid = (z == 1) | (z == 2)

    def kv_start(j):
        k, v = kvs.at[j, 0, 0], kvs.at[j, 1, 0]
        send(rcopy(k, kvrl.at[j], kss.at[j, 6, 0], ksr.at[j, 0, 0], y_up), lo)
        send(rcopy(v, kvrl.at[j], kss.at[j, 6, 1], ksr.at[j, 0, 0], y_dn), lo)
        for i in range(2):
            o = kvs.at[j, i, 0]
            send(rcopy(o, kvs.at[j, i, 1], kss.at[j, 1, i], ksr.at[j, 1, i], z_up), z < 3)
            send(rcopy(o, kvs.at[j, i, 3], kss.at[j, 3, i], ksr.at[j, 3, i], z_dn), z == 0)

    relay_k = (y == 1) | (y == 2)
    relay_v = (y == 0) | (y == 3)

    def kv_relay(j):
        arrive(kvrl.at[j], ksr.at[j, 0, 0])
        send(rcopy(kvrl.at[j], kvs.at[j, 0, 4], kss.at[j, 4, 0], ksr.at[j, 4, 0], y_up), relay_k)
        send(rcopy(kvrl.at[j], kvs.at[j, 1, 4], kss.at[j, 4, 1], ksr.at[j, 4, 1], y_dn), relay_v)

    def kv_second(j):
        for i in range(2):
            b1, b4 = kvs.at[j, i, 1], kvs.at[j, i, 4]
            arrive(b1, ksr.at[j, 1, i], mid)
            send(rcopy(b1, kvs.at[j, i, 2], kss.at[j, 2, i], ksr.at[j, 2, i], z_up), mid)
            arrive(b4, ksr.at[j, 4, i], hi)
            send(rcopy(b4, kvs.at[j, i, 3], kss.at[j, 3, i], ksr.at[j, 3, i], z_dn), hi & (z >= 1))
            send(rcopy(b4, kvs.at[j, i, 1], kss.at[j, 1, i], ksr.at[j, 1, i], z_up), hi & (z == 3))

    def kv_third(j):
        for i in range(2):
            b3 = kvs.at[j, i, 3]
            arrive(b3, ksr.at[j, 3, i], hi & mid)
            send(rcopy(b3, kvs.at[j, i, 2], kss.at[j, 5, i], ksr.at[j, 2, i], z_dn), hi & mid)

    def kv_finish(j):
        for i in range(2):
            arrive(kvs.at[j, i, 1], ksr.at[j, 1, i], (z == 3) | (hi & (z == 0)))
            arrive(kvs.at[j, i, 2], ksr.at[j, 2, i], (z >= 2) | hi)
            arrive(kvs.at[j, i, 3], ksr.at[j, 3, i], (z == 3) | (hi & (z == 0)))

    cosine, sine = cos_ref[...], sin_ref[...]

    def project(j):
        for load in loads[2 + 4 * j : 5 + 4 * j]:
            load.wait()
        xn = ag[j].reshape(TOK, D)
        q_gain, k_gain = gain(qg, j), gain(kg, j)
        kr = dot(xn, wk[j])
        kvs[j, 0, 0] = rope(kr * rms_of(kr) * k_gain, cosine, sine).astype(bf16)
        kvs[j, 1, 0] = dot(xn, wv[j]).astype(bf16)
        kv_start(j)
        if j == BACK:
            kraw[...] = kr
        for h in range(2):
            qr = dot(xn, wq[j, :, h * HD : (h + 1) * HD])
            qs[j, h * TOK : (h + 1) * TOK] = rope(
                qr * rms_of(qr) * q_gain, cosine, sine
            ).astype(bf16)
            if j == BACK:
                qraw[h * TOK : (h + 1) * TOK] = qr

    def attention(j, keep):
        @pl.loop(0, 4)
        def _(ci):
            rows = pl.ds(pl.multiple_of(ci * 128, 128), 128)
            sc = dot_nt(qs[j, rows, :], kvs[j, 0].reshape(5 * TOK, HD)) * (HD ** -0.5)
            col = lax.broadcasted_iota(jnp.int32, (1, 5 * TOK), 1)
            back = (col // TOK) * TOK - col % TOK
            back = jnp.where(col // TOK <= p, back, -4 * WINDOW)
            ii = (ci % 2) * 128 + lax.broadcasted_iota(jnp.int32, (128, 1), 0)
            rel = ii + back
            sc = jnp.where((rel >= 0) & (rel < WINDOW), sc, masked_score)
            e = jnp.exp(sc - jnp.max(sc, axis=-1, keepdims=True))
            w = e / jnp.sum(e, axis=-1, keepdims=True)
            low = w.astype(bf16)
            if keep:
                pw[rows, :] = w
                pl_s[rows, :] = low
            out = dot(low, kvs[j, 1].reshape(5 * TOK, HD)).astype(bf16)
            for h in range(2):
                @pl.when(ci // 2 == h)
                def _():
                    cx[j, pl.ds(4 * (ci % 2), 4), :, h * HD : (h + 1) * HD] = out.reshape(
                        4, ROWS, HD
                    )

    def out_product(j):
        return lambda lhs, n: dot(lhs, wo[j, :, n * CW : (n + 1) * CW])

    def hidden_product(lhs, n):
        w_rows = slice(n * CW, (n + 1) * CW)
        total = dot_nt(lhs[:, : 2 * HD], wq[BACK, w_rows, :])
        total += dot_nt(lhs[:, 2 * HD : 3 * HD], wk[BACK, w_rows, :])
        return total + dot_nt(lhs[:, 3 * HD :], wv[BACK, w_rows, :])

    loads[0].wait()
    x_back = sti[plan[0, 1]].astype(f32)
    ag[BACK, t] = (x_back * rms_of(x_back) * gain(ig, BACK)).astype(bf16)
    for j in range(2):
        for d in range(1, 5):
            @pl.when(d > p)
            def _():
                for i in range(2):
                    kvs[j, i, d] = jnp.zeros((TOK, HD), bf16)
    pl.semaphore_wait(barrier, 7)
    gather_start(BACK)
    x_fwd = sti[plan[0, 0]].astype(f32)
    ag[FWD, t] = (x_fwd * rms_of(x_fwd) * gain(ig, FWD)).astype(bf16)
    gather_relay(BACK)
    gather_start(FWD)
    gather_finish(BACK)
    project(BACK)
    gather_relay(FWD)
    kv_relay(BACK)
    gather_finish(FWD)
    kv_second(BACK)
    project(FWD)
    kv_third(BACK)
    kv_relay(FWD)
    kv_finish(BACK)
    attention(BACK, True)
    loads[5].wait()
    before = len(drains)
    scatter_first(BACK, out_product(BACK), lambda par: rows_of(cx.at[BACK], par))
    kv_second(FWD)
    scatter_second(BACK, out_product(BACK), lambda par: rows_of(cx.at[BACK], par))
    scatter_relay(BACK)
    kv_third(FWD)
    projected = scatter_finish(BACK)
    loads[1].wait()
    incoming = stg[plan[0, 1]].astype(f32)
    ag[GRAD, t] = rms_back(projected, incoming, gain(og, BACK)).astype(bf16)
    gather_start(GRAD)
    kv_finish(FWD)
    attention(FWD, False)
    gather_relay(GRAD)
    loads[9].wait()
    scatter_first(FWD, out_product(FWD), lambda par: rows_of(cx.at[FWD], par))
    gather_finish(GRAD)
    scatter_second(FWD, out_product(FWD), lambda par: rows_of(cx.at[FWD], par))

    og_rows = ag[GRAD].reshape(TOK, D)
    for h in range(2):
        cgs[h * TOK : (h + 1) * TOK] = dot_nt(
            og_rows, wo[BACK, h * HD : (h + 1) * HD, :]
        ).astype(bf16)
    q_gain, k_gain = gain(qg, BACK), gain(kg, BACK)

    @pl.loop(0, 4)
    def _(ci):
        rows = pl.ds(pl.multiple_of(ci * 128, 128), 128)
        w = pw[rows, :]
        wg = dot_nt(cgs[rows, :], kvs[BACK, 1].reshape(5 * TOK, HD))
        delta = jnp.sum(w * wg, axis=-1, keepdims=True)
        dss[rows, :] = (w * (wg - delta) * (HD ** -0.5)).astype(bf16)

    scatter_relay(FWD)

    def grad_block(d):
        ds_d = dss[:, d * TOK : (d + 1) * TOK]
        gacc[0, d] = dot_tn(ds_d, qs[BACK])
        gacc[1, d] = dot_tn(pl_s[:, d * TOK : (d + 1) * TOK], cgs[...])

    R1, R2, R3, R4, R5, RR = 0, 1, 2, 3, 4, 5

    def give(d):
        for i in range(2):
            gs[i, d - 1] = gacc[i, d].astype(bf16)

    def g_send(d, e, se, device, cond, i):
        send(rcopy(gs.at[i, d - 1], gr.at[e, i], gss.at[se, i], gsr.at[e, i], device), cond)

    def g_add(e, d, cond):
        for i in range(2):
            arrive(gr.at[e, i], gsr.at[e, i], cond)

            @pl.when(cond)
            def _():
                gacc[i, d] = gacc[i, d] + gr[e, i].astype(f32)

    grad_block(2)
    give(2)
    for i in range(2):
        g_send(2, R2, 0, z_dn, z >= 2, i)
        g_send(2, R5, 1, z_up, hi & (z <= 1), i)
    grad_block(3)
    grad_block(1)
    g_add(R5, 3, hi & mid)
    give(3)
    for i in range(2):
        g_send(3, R3, 2, z_up, (z == 3) | hi, i)
    g_add(R2, 1, mid)
    give(1)
    for i in range(2):
        g_send(1, R1, 3, z_dn, (z >= 1) | hi, i)
    grad_block(4)
    grad_block(0)
    g_add(R3, 4, hi & (z >= 1))
    g_add(R1, 4, hi & (z == 3))
    give(4)
    send(rcopy(gs.at[0, 3], gr.at[RR, 0], gss.at[4, 0], gsr.at[RR, 0], y_dn), hi)
    send(rcopy(gs.at[1, 3], gr.at[RR, 0], gss.at[4, 1], gsr.at[RR, 0], y_up), hi)

    for h in range(2):
        rows = slice(h * TOK, (h + 1) * TOK)
        dq = dot(dss[rows, :], kvs[BACK, 0].reshape(5 * TOK, HD))
        low = rms_back(qraw[rows], rope_back(dq, cosine, sine), q_gain).astype(bf16)
        lq[:, :, h * HD : (h + 1) * HD] = low.reshape(8, ROWS, HD)

    arrive(gr.at[RR, 0], gsr.at[RR, 0])
    send(rcopy(gr.at[RR, 0], gr.at[R4, 0], gss.at[5, 0], gsr.at[R4, 0], y_dn), relay_k)
    send(rcopy(gr.at[RR, 0], gr.at[R4, 1], gss.at[5, 1], gsr.at[R4, 1], y_up), relay_v)

    fwd_proj = scatter_finish(FWD)
    x_fwd = sti[plan[0, 0]].astype(f32)
    fo[...] = (x_fwd + fwd_proj * rms_of(fwd_proj) * gain(og, FWD)).astype(bf16)
    send(rcopy(fo, act_out, swap_s.at[1], swap_r.at[1], other))

    g_add(R1, 0, z < 3)
    g_add(R3, 0, z == 0)
    g_add(R4, 0, lo)
    key_low = rms_back(kraw[...], rope_back(gacc[0, 0], cosine, sine), k_gain).astype(bf16)
    lq[:, :, 2 * HD : 3 * HD] = key_low.reshape(8, ROWS, HD)
    lq[:, :, 3 * HD :] = gacc[1, 0].astype(bf16).reshape(8, ROWS, HD)

    for copy, _ in drains[before : before + NCH]:
        copy.wait_send()
    del drains[before : before + NCH]
    scatter_first(2, hidden_product, lambda par: rows_of(lq, par))
    scatter_second(2, hidden_product, lambda par: rows_of(lq, par))
    scatter_relay(2)
    hidden = scatter_finish(2)
    x_back = sti[plan[0, 1]].astype(f32)
    incoming = stg[plan[0, 1]].astype(f32)
    go[...] = (incoming + rms_back(x_back, hidden, gain(ig, BACK))).astype(bf16)
    send(rcopy(go, grad_out, swap_s.at[2], swap_r.at[2], other))
    arrive(act_out, swap_r.at[1])
    arrive(grad_out, swap_r.at[2])
    for copy, cond in drains:
        when(cond, copy.wait_send)


def per_device(
    stash_inputs, stash_grads, plan, query_weight, key_weight, value_weight, out_weight,
    input_gain, output_gain, query_gain, key_gain,
):
    block = lax.axis_index("ctx")
    positions = (block * TOK + jnp.arange(TOK, dtype=jnp.int32)).astype(f32)
    frequency = rope_base ** (-(jnp.arange(HD // 2).astype(f32) * 2.0 / HD))
    angles = positions[:, None] * frequency[None, :]
    vmem = pl.BlockSpec(memory_space=pltpu.VMEM)
    hbm = pl.BlockSpec(memory_space=pl.ANY)
    smem = pl.BlockSpec(memory_space=pltpu.SMEM)
    V = pltpu.VMEM
    sem = pltpu.SemaphoreType.DMA
    act, grad = pl.pallas_call(
        kernel,
        out_shape=(jax.ShapeDtypeStruct((ROWS, D), bf16),) * 2,
        in_specs=[smem] + [vmem] * 6 + [hbm] * 6,
        out_specs=(hbm, hbm),
        scratch_shapes=[
            V((2, D, 2 * HD), bf16), V((2, D, HD), bf16), V((2, D, HD), bf16), V((2, 2 * HD, D), bf16),
            V((4, ROWS, D), bf16), V((4, ROWS, D), bf16),
            V((3, 8, ROWS, D), bf16),
            V((2, 2 * TOK, HD), bf16), V((2 * TOK, HD), f32), V((TOK, HD), f32),
            V((2, 2, 5, TOK, HD), bf16), V((2, TOK, HD), bf16),
            V((2, 8, ROWS, 2 * HD), bf16),
            V((2 * TOK, 5 * TOK), f32), V((2 * TOK, 5 * TOK), bf16), V((2 * TOK, 5 * TOK), bf16),
            V((2 * TOK, HD), bf16),
            V((2, 4, ROWS, D), bf16), V((3, 4, ROWS, D), bf16), V((3, 3, ROWS, D), bf16),
            V((3, 2, ROWS // 2, D), bf16), V((3, 2, ROWS, D), bf16), V((3, ROWS, D), f32),
            V((2, 4, TOK, HD), bf16), V((6, 2, TOK, HD), bf16), V((2, 5, TOK, HD), f32),
            V((8, ROWS, 4 * HD), bf16),
            V((ROWS, D), bf16), V((ROWS, D), bf16),
            sem((10,)), sem((3, 13)), sem((3, 13)), sem((3, NCH, 7)), sem((3, NCH, 7)),
            sem((2, 7, 2)), sem((2, 5, 2)), sem((6, 2)), sem((6, 2)), sem((3,)), sem((3,)),
        ],
        compiler_params=pltpu.CompilerParams(
            collective_id=0, has_side_effects=True, vmem_limit_bytes=67043328
        ),
    )(
        plan, jnp.cos(angles), jnp.sin(angles), input_gain[0], output_gain[0], query_gain[0],
        key_gain[0], stash_inputs[0], stash_grads[0], query_weight[0], key_weight[0],
        value_weight[0], out_weight[0],
    )
    return act[None], grad[None]


def solution(mesh):
    return jax.shard_map(
        per_device,
        mesh=mesh,
        in_specs=(
            P("segment", None, ("ctx", "tp"), None),
            P("segment", None, ("ctx", "tp"), None),
            P("segment", None),
            P("segment", None, None, "tp"),
            P("segment", None, None, "tp"),
            P("segment", None, None, "tp"),
            P("segment", None, "tp", None),
            P("segment", None, None),
            P("segment", None, None),
            P("segment", None, None),
            P("segment", None, None),
        ),
        out_specs=(P("segment", ("ctx", "tp"), None), P("segment", ("ctx", "tp"), None)),
        check_vma=False,
    )
```

```python
import jax
import jax.numpy as jnp
from jax import lax
from jax.experimental import pallas as pl
from jax.experimental.pallas import tpu as pltpu
from jax.sharding import PartitionSpec as P

WINDOW = 1024
epsilon = 1e-06
rope_base = 10000.0
masked_score = -1e30

D = 3840
ROWS = 32
TOK = 256
HD = 256
NCH = 3
CW = D // NCH
BACK, FWD, GRAD = 0, 1, 2
f32 = jnp.float32
bf16 = jnp.bfloat16
MESH = pl.DeviceIdType.MESH


def dot(a, b):
    return lax.dot_general(a, b, (((1,), (0,)), ((), ())), preferred_element_type=f32)


def dot_nt(a, b):
    return lax.dot_general(a, b, (((1,), (1,)), ((), ())), preferred_element_type=f32)


def dot_tn(a, b):
    return lax.dot_general(a, b, (((0,), (0,)), ((), ())), preferred_element_type=f32)


def rms_of(x):
    return lax.rsqrt(jnp.mean(x * x, axis=-1, keepdims=True) + epsilon)


def rms_back(x, grad, gain):
    g = grad * gain
    r = rms_of(x)
    return r * (g - x * (r * r * jnp.mean(g * x, axis=-1, keepdims=True)))


def rope(y, cosine, sine):
    a, b = y[:, : HD // 2], y[:, HD // 2 :]
    return jnp.concatenate([a * cosine - b * sine, b * cosine + a * sine], axis=-1)


def rope_back(g, cosine, sine):
    a, b = g[:, : HD // 2], g[:, HD // 2 :]
    return jnp.concatenate([a * cosine + b * sine, b * cosine - a * sine], axis=-1)


def kernel(
    plan, freq, ig, og, qg, kg, si, sg, wq_h, wk_h, wv_h, wo_h,
    act_out, grad_out,
    wq, wk, wv, wo, sti, stg, ag, qs, qraw, kraw, kvs, kvrl, cx, pw, pl_s, dss, cgs,
    ps, pr, sb, rl, fr, own, gs, gr, gacc, lq, fo, go, cos_ref, sin_ref, hq, bo, gb,
    lsem, ags, agr, rss, rsr, kss, ksr, gss, gsr, swap_s, swap_r,
):
    s = lax.axis_index("segment")
    p = lax.axis_index("ctx")
    t = lax.axis_index("tp")
    yh, z = p // 4, p % 4
    y = 2 * yh + s
    x, c = t // 2, t % 2
    legs = (1 - s, s)

    def dev(s_=None, p_=None, t_=None):
        return {
            "segment": s if s_ is None else s_,
            "ctx": p if p_ is None else p_,
            "tp": t if t_ is None else t_,
        }

    t_r, t_l = ((x + 1) % 4) * 2 + c, ((x + 3) % 4) * 2 + c
    t_o = ((x + 2) % 4) * 2 + c
    t_p = 2 * x + 1 - c
    right, left, partner = dev(t_=t_r), dev(t_=t_l), dev(t_=t_p)
    z_up, z_dn = dev(p_=4 * yh + (z + 1) % 4), dev(p_=4 * yh + (z + 3) % 4)
    y_u, y_d = (y + 1) % 4, (y + 3) % 4
    y_up = dev(s_=y_u % 2, p_=(y_u // 2) * 4 + z)
    y_dn = dev(s_=y_d % 2, p_=(y_d // 2) * 4 + z)
    other = dev(s_=1 - s)

    barrier = pltpu.get_barrier_semaphore()
    for device in (right, left, partner, z_up, z_dn, y_up, y_dn):
        pl.semaphore_signal(barrier, inc=1, device_id=device, device_id_type=MESH)

    loads = [
        pltpu.make_async_copy(si, sti, lsem.at[0]),
        pltpu.make_async_copy(sg, stg, lsem.at[1]),
    ]
    for j in range(2):
        loads += [
            pltpu.make_async_copy(wq_h.at[legs[j]], wq.at[j], lsem.at[2 + 4 * j]),
            pltpu.make_async_copy(wk_h.at[legs[j]], wk.at[j], lsem.at[3 + 4 * j]),
            pltpu.make_async_copy(wv_h.at[legs[j]], wv.at[j], lsem.at[4 + 4 * j]),
            pltpu.make_async_copy(wo_h.at[legs[j]], wo.at[j], lsem.at[5 + 4 * j]),
        ]
    for load in loads:
        load.start()

    def gain(ref, j):
        return ref[pl.ds(legs[j], 1), :]

    def rcopy(src, dst, ssem, rsem, device):
        return pltpu.make_async_remote_copy(
            src_ref=src, dst_ref=dst, send_sem=ssem, recv_sem=rsem,
            device_id=device, device_id_type=MESH,
        )

    drains = []

    def when(cond, run):
        if cond is None:
            run()
        else:
            pl.when(cond)(run)

    def send(copy, cond=None):
        when(cond, copy.start)
        drains.append((copy, cond))

    def arrive(dst, rsem, cond=None):
        copy = rcopy(dst, dst, swap_s.at[0], rsem, partner)
        when(cond, copy.wait_recv)

    H0, H1 = pl.ds(0, ROWS // 2), pl.ds(ROWS // 2, ROWS // 2)
    halves = (H0, H1)

    def gather_start(j):
        blk = ag.at[j, t]
        send(rcopy(blk.at[H0], blk.at[H0], ags.at[j, 0], agr.at[j, 0], right))
        send(rcopy(blk.at[H1], blk.at[H1], ags.at[j, 1], agr.at[j, 1], left))
        send(rcopy(blk.at[H1], blk.at[H1], ags.at[j, 2], agr.at[j, 2], right))
        send(rcopy(blk.at[H0], blk.at[H0], ags.at[j, 3], agr.at[j, 3], left))
        send(rcopy(blk, blk, ags.at[j, 6], agr.at[j, 6], partner))

    def across(j, place, half, i):
        part = ag.at[j, place, halves[half]]
        send(rcopy(part, part, ags.at[j, i], agr.at[j, i], partner))

    def gather_relay(j):
        a = ag.at[j, t_l, H0]
        arrive(a, agr.at[j, 0])
        send(rcopy(a, a, ags.at[j, 4], agr.at[j, 4], right))
        b = ag.at[j, t_r, H1]
        arrive(b, agr.at[j, 1])
        send(rcopy(b, b, ags.at[j, 5], agr.at[j, 5], left))
        across(j, t_l, 0, 7)
        across(j, t_r, 1, 8)

    def gather_finish(j):
        arrive(ag.at[j, t_l, H1], agr.at[j, 2])
        across(j, t_l, 1, 9)
        arrive(ag.at[j, t_r, H0], agr.at[j, 3])
        across(j, t_r, 0, 10)
        arrive(ag.at[j, t_o, H0], agr.at[j, 4])
        across(j, t_o, 0, 11)
        arrive(ag.at[j, t_o, H1], agr.at[j, 5])
        across(j, t_o, 1, 12)
        u_r, u_l, u_o = t_r + 1 - 2 * c, t_l + 1 - 2 * c, t_o + 1 - 2 * c
        arrive(ag.at[j, t_p], agr.at[j, 6])
        arrive(ag.at[j, u_l, H0], agr.at[j, 7])
        arrive(ag.at[j, u_r, H1], agr.at[j, 8])
        arrive(ag.at[j, u_l, H1], agr.at[j, 9])
        arrive(ag.at[j, u_r, H0], agr.at[j, 10])
        arrive(ag.at[j, u_o, H0], agr.at[j, 11])
        arrive(ag.at[j, u_o, H1], agr.at[j, 12])

    def cols(n):
        return pl.ds(n * CW, CW)

    def rows_of(ref, parity):
        parts = [ref[2 * ((x + k) % 4) + parity] for k in range(4)]
        return jnp.concatenate(parts, axis=0)

    def rows_all(ref):
        return jnp.concatenate([rows_of(ref, 1 - c), rows_of(ref, c)], axis=0)

    def scatter_first(r, product, lhs):
        for n in range(NCH):
            total = product(lhs, n)
            ps[r % 2, :, :, cols(n)] = total[: 4 * ROWS].astype(bf16).reshape(4, ROWS, CW)
            send(rcopy(ps.at[r % 2, :, :, cols(n)], pr.at[r, :, :, cols(n)],
                       rss.at[r, n, 0], rsr.at[r, n, 0], partner))
            hq[4 * ROWS :, cols(n)] = total[4 * ROWS :]

    def scatter_second(r):
        for n in range(NCH):
            arrive(pr.at[r, :, :, cols(n)], rsr.at[r, n, 0])
            total = hq[4 * ROWS :, cols(n)].reshape(4, ROWS, CW) + pr[r, :, :, cols(n)].astype(f32)
            own[r % 2, :, cols(n)] = total[0]
            sb[r, :, :, cols(n)] = total[1:].astype(bf16)
            send(rcopy(sb.at[r, 1, H0, cols(n)], rl.at[r, 0, :, cols(n)],
                       rss.at[r, n, 1], rsr.at[r, n, 1], right))
            send(rcopy(sb.at[r, 1, H1, cols(n)], rl.at[r, 1, :, cols(n)],
                       rss.at[r, n, 2], rsr.at[r, n, 2], left))
            send(rcopy(sb.at[r, 0, H1, cols(n)], fr.at[r, 0, H1, cols(n)],
                       rss.at[r, n, 3], rsr.at[r, n, 3], right))
            send(rcopy(sb.at[r, 2, H0, cols(n)], fr.at[r, 1, H0, cols(n)],
                       rss.at[r, n, 4], rsr.at[r, n, 4], left))

    def scatter_relay(r):
        for n in range(NCH):
            arrive(rl.at[r, 0, :, cols(n)], rsr.at[r, n, 1])
            sb[r, 0, H0, cols(n)] = (
                sb[r, 0, H0, cols(n)].astype(f32) + rl[r, 0, :, cols(n)].astype(f32)
            ).astype(bf16)
            send(rcopy(sb.at[r, 0, H0, cols(n)], fr.at[r, 0, H0, cols(n)],
                       rss.at[r, n, 5], rsr.at[r, n, 5], right))
            arrive(rl.at[r, 1, :, cols(n)], rsr.at[r, n, 2])
            sb[r, 2, H1, cols(n)] = (
                sb[r, 2, H1, cols(n)].astype(f32) + rl[r, 1, :, cols(n)].astype(f32)
            ).astype(bf16)
            send(rcopy(sb.at[r, 2, H1, cols(n)], fr.at[r, 1, H1, cols(n)],
                       rss.at[r, n, 6], rsr.at[r, n, 6], left))

    def scatter_part(r, n):
        arrive(fr.at[r, 0, H1, cols(n)], rsr.at[r, n, 3])
        arrive(fr.at[r, 1, H0, cols(n)], rsr.at[r, n, 4])
        arrive(fr.at[r, 0, H0, cols(n)], rsr.at[r, n, 5])
        arrive(fr.at[r, 1, H1, cols(n)], rsr.at[r, n, 6])
        return own[r % 2, :, cols(n)] + (
            fr[r, 0, :, cols(n)].astype(f32) + fr[r, 1, :, cols(n)].astype(f32)
        )

    def scatter_finish(r):
        return jnp.concatenate([scatter_part(r, n) for n in range(NCH)], axis=-1)

    hi, lo = yh == 1, yh == 0
    mid = (z == 1) | (z == 2)

    def kv_start(j):
        k, v = kvs.at[j, 0, 0], kvs.at[j, 1, 0]
        send(rcopy(k, kvrl.at[j], kss.at[j, 6, 0], ksr.at[j, 0, 0], y_up), lo)
        send(rcopy(v, kvrl.at[j], kss.at[j, 6, 1], ksr.at[j, 0, 0], y_dn), lo)
        for i in range(2):
            o = kvs.at[j, i, 0]
            send(rcopy(o, kvs.at[j, i, 1], kss.at[j, 1, i], ksr.at[j, 1, i], z_up), z < 3)
            send(rcopy(o, kvs.at[j, i, 3], kss.at[j, 3, i], ksr.at[j, 3, i], z_dn), z == 0)

    relay_k = (y == 1) | (y == 2)
    relay_v = (y == 0) | (y == 3)

    def kv_relay(j):
        arrive(kvrl.at[j], ksr.at[j, 0, 0])
        send(rcopy(kvrl.at[j], kvs.at[j, 0, 4], kss.at[j, 4, 0], ksr.at[j, 4, 0], y_up), relay_k)
        send(rcopy(kvrl.at[j], kvs.at[j, 1, 4], kss.at[j, 4, 1], ksr.at[j, 4, 1], y_dn), relay_v)

    def kv_second(j):
        for i in range(2):
            b1, b4 = kvs.at[j, i, 1], kvs.at[j, i, 4]
            arrive(b1, ksr.at[j, 1, i], mid)
            send(rcopy(b1, kvs.at[j, i, 2], kss.at[j, 2, i], ksr.at[j, 2, i], z_up), mid)
            arrive(b4, ksr.at[j, 4, i], hi)
            send(rcopy(b4, kvs.at[j, i, 3], kss.at[j, 3, i], ksr.at[j, 3, i], z_dn), hi & (z >= 1))
            send(rcopy(b4, kvs.at[j, i, 1], kss.at[j, 1, i], ksr.at[j, 1, i], z_up), hi & (z == 3))

    def kv_third(j):
        for i in range(2):
            b3 = kvs.at[j, i, 3]
            arrive(b3, ksr.at[j, 3, i], hi & mid)
            send(rcopy(b3, kvs.at[j, i, 2], kss.at[j, 5, i], ksr.at[j, 2, i], z_dn), hi & mid)

    def kv_finish(j):
        for i in range(2):
            arrive(kvs.at[j, i, 1], ksr.at[j, 1, i], (z == 3) | (hi & (z == 0)))
            arrive(kvs.at[j, i, 2], ksr.at[j, 2, i], (z >= 2) | hi)
            arrive(kvs.at[j, i, 3], ksr.at[j, 3, i], (z == 3) | (hi & (z == 0)))

    def project(j):
        cosine, sine = cos_ref[...], sin_ref[...]
        for load in loads[2 + 4 * j : 5 + 4 * j]:
            load.wait()
        xn = ag[j].reshape(TOK, D)
        q_gain, k_gain = gain(qg, j), gain(kg, j)
        kr = dot(xn, wk[j])
        kvs[j, 0, 0] = rope(kr * rms_of(kr) * k_gain, cosine, sine).astype(bf16)
        kvs[j, 1, 0] = dot(xn, wv[j]).astype(bf16)
        kv_start(j)
        if j == BACK:
            kraw[...] = kr
        for h in range(2):
            qr = dot(xn, wq[j, :, h * HD : (h + 1) * HD])
            qs[j, h * TOK : (h + 1) * TOK] = rope(
                qr * rms_of(qr) * q_gain, cosine, sine
            ).astype(bf16)
            if j == BACK:
                qraw[h * TOK : (h + 1) * TOK] = qr

    def attention(j, keep):
        @pl.loop(0, 4)
        def _(ci):
            rows = pl.ds(pl.multiple_of(ci * 128, 128), 128)
            sc = dot_nt(qs[j, rows, :], kvs[j, 0].reshape(5 * TOK, HD)) * (HD ** -0.5)
            col = lax.broadcasted_iota(jnp.int32, (1, 5 * TOK), 1)
            back = (col // TOK) * TOK - col % TOK
            back = jnp.where(col // TOK <= p, back, -4 * WINDOW)
            ii = (ci % 2) * 128 + lax.broadcasted_iota(jnp.int32, (128, 1), 0)
            rel = ii + back
            sc = jnp.where((rel >= 0) & (rel < WINDOW), sc, masked_score)
            e = jnp.exp(sc - jnp.max(sc, axis=-1, keepdims=True))
            w = e / jnp.sum(e, axis=-1, keepdims=True)
            low = w.astype(bf16)
            if keep:
                pw[rows, :] = w
                pl_s[rows, :] = low
            out = dot(low, kvs[j, 1].reshape(5 * TOK, HD)).astype(bf16)
            for h in range(2):
                @pl.when(ci // 2 == h)
                def _():
                    cx[j, pl.ds(4 * (ci % 2), 4), :, h * HD : (h + 1) * HD] = out.reshape(
                        4, ROWS, HD
                    )

    def out_product(j):
        return lambda lhs, n: dot(lhs, wo[j, :, n * CW : (n + 1) * CW])

    def hidden_product(lhs, n):
        w_rows = slice(n * CW, (n + 1) * CW)
        total = hq[:, cols(n)] + dot_nt(lhs[:, 2 * HD : 3 * HD], wk[BACK, w_rows, :])
        return total + dot_nt(lhs[:, 3 * HD :], wv[BACK, w_rows, :])

    loads[0].wait()
    x_back = sti[plan[0, 1]].astype(f32)
    ag[BACK, t] = (x_back * rms_of(x_back) * gain(ig, BACK)).astype(bf16)
    pl.semaphore_wait(barrier, 7)
    gather_start(BACK)
    x_fwd = sti[plan[0, 0]].astype(f32)
    ag[FWD, t] = (x_fwd * rms_of(x_fwd) * gain(ig, FWD)).astype(bf16)
    for j in range(2):
        for d in range(1, 5):
            @pl.when(d > p)
            def _():
                for i in range(2):
                    kvs[j, i, d] = jnp.zeros((TOK, HD), bf16)
    angles = (p * TOK + lax.broadcasted_iota(jnp.int32, (TOK, HD // 2), 0)).astype(f32) * freq[...]
    cos_ref[...] = jnp.cos(angles)
    sin_ref[...] = jnp.sin(angles)
    gather_relay(BACK)
    gather_start(FWD)
    gather_finish(BACK)
    project(BACK)
    gather_relay(FWD)
    kv_relay(BACK)
    gather_finish(FWD)
    kv_second(BACK)
    project(FWD)
    kv_third(BACK)
    kv_relay(FWD)
    kv_finish(BACK)
    attention(BACK, True)
    loads[5].wait()
    before = len(drains)
    scatter_first(BACK, out_product(BACK), rows_all(cx.at[BACK]))
    kv_second(FWD)
    scatter_second(BACK)
    scatter_relay(BACK)
    kv_third(FWD)
    projected = scatter_finish(BACK)
    loads[1].wait()
    incoming = stg[plan[0, 1]].astype(f32)
    ag[GRAD, t] = rms_back(projected, incoming, gain(og, BACK)).astype(bf16)
    gather_start(GRAD)
    go[...] = sti[plan[0, 1]]
    fo[...] = stg[plan[0, 1]]
    ahead = (
        rcopy(go, bo.at[0], swap_s.at[2], swap_r.at[2], other),
        rcopy(fo, bo.at[1], swap_s.at[0], swap_r.at[0], other),
    )
    for copy in ahead:
        copy.start()
    kv_finish(FWD)
    attention(FWD, False)
    gather_relay(GRAD)
    loads[9].wait()
    scatter_first(FWD, out_product(FWD), rows_all(cx.at[FWD]))
    gather_finish(GRAD)

    og_rows = ag[GRAD].reshape(TOK, D)
    for h in range(2):
        cgs[h * TOK : (h + 1) * TOK] = dot_nt(
            og_rows, wo[BACK, h * HD : (h + 1) * HD, :]
        ).astype(bf16)
    q_gain, k_gain = gain(qg, BACK), gain(kg, BACK)

    R1, R2, R3, R4, R5, RR = 0, 1, 2, 3, 4, 5

    def grad_block(i, d):
        if i == 0:
            gacc[0, d] = dot_tn(dss[:, d * TOK : (d + 1) * TOK], qs[BACK])
        else:
            gacc[1, d] = dot_tn(pl_s[:, d * TOK : (d + 1) * TOK], cgs[...])

    def g_send(d, e, se, device, cond, i):
        send(rcopy(gs.at[i, d - 1], gr.at[e, i], gss.at[se, i], gsr.at[e, i], device), cond)

    def g_add(e, d, cond, i):
        arrive(gr.at[e, i], gsr.at[e, i], cond)

        @pl.when(cond)
        def _():
            gacc[i, d] = gacc[i, d] + gr[e, i].astype(f32)

    def give(i, d):
        gs[i, d - 1] = gacc[i, d].astype(bf16)

    def g_second(i, cond):
        g_send(3, R3, 2, z_up, cond & ((z == 3) | hi), i)
        g_send(1, R1, 3, z_dn, cond & ((z >= 1) | hi), i)

    def g_first(i):
        grad_block(i, 2)
        give(i, 2)
        g_send(2, R2, 0, z_dn, z >= 2, i)
        g_send(2, R5, 1, z_up, hi & (z <= 1), i)
        grad_block(i, 3)
        give(i, 3)
        grad_block(i, 1)
        give(i, 1)
        g_second(i, ~mid)
        grad_block(i, 4)
        grad_block(i, 0)

    def g_middle(i):
        g_add(R5, 3, hi & mid, i)
        g_add(R2, 1, mid, i)

        @pl.when(mid)
        def _():
            give(i, 3)
            give(i, 1)
        g_second(i, mid)

    def g_third(i):
        g_add(R3, 4, hi & (z >= 1), i)
        g_add(R1, 4, hi & (z == 3), i)
        give(i, 4)
        send(rcopy(gs.at[i, 3], gr.at[RR, 0], gss.at[4, i], gsr.at[RR, 0],
                   y_up if i else y_dn), hi)

    g_first(1)

    @pl.loop(0, 4)
    def _(ci):
        rows = pl.ds(pl.multiple_of(ci * 128, 128), 128)
        w = pw[rows, :]
        wg = dot_nt(cgs[rows, :], kvs[BACK, 1].reshape(5 * TOK, HD))
        delta = jnp.sum(w * wg, axis=-1, keepdims=True)
        dss[rows, :] = (w * (wg - delta) * (HD ** -0.5)).astype(bf16)

    g_first(0)
    g_middle(1)
    scatter_second(FWD)
    g_middle(0)
    g_third(1)
    g_third(0)

    for h in range(2):
        rows = slice(h * TOK, (h + 1) * TOK)
        dq = dot(dss[rows, :], kvs[BACK, 0].reshape(5 * TOK, HD))
        low = rms_back(
            qraw[rows], rope_back(dq, cos_ref[...], sin_ref[...]), q_gain
        ).astype(bf16)
        lq[:, :, h * HD : (h + 1) * HD] = low.reshape(8, ROWS, HD)
    query_low = rows_all(lq)[:, : 2 * HD]
    for n in range(NCH):
        hq[:, cols(n)] = dot_nt(query_low, wq[BACK, n * CW : (n + 1) * CW, :])

    arrive(gr.at[RR, 0], gsr.at[RR, 0])
    send(rcopy(gr.at[RR, 0], gr.at[R4, 0], gss.at[5, 0], gsr.at[R4, 0], y_dn), relay_k)
    send(rcopy(gr.at[RR, 0], gr.at[R4, 1], gss.at[5, 1], gsr.at[R4, 1], y_up), relay_v)
    for copy in ahead:
        copy.wait_send()
    scatter_relay(FWD)
    for i in (1, 0):
        g_add(R1, 0, z < 3, i)
        g_add(R3, 0, z == 0, i)
        g_add(R4, 0, lo, i)
    key_low = rms_back(
        kraw[...], rope_back(gacc[0, 0], cos_ref[...], sin_ref[...]), k_gain
    ).astype(bf16)
    lq[:, :, 2 * HD : 3 * HD] = key_low.reshape(8, ROWS, HD)
    lq[:, :, 3 * HD :] = gacc[1, 0].astype(bf16).reshape(8, ROWS, HD)

    for copy, _ in drains[before : before + NCH]:
        copy.wait_send()
    del drains[before : before + NCH]
    scatter_first(2, hidden_product, rows_all(lq))
    scatter_second(2)
    fwd_proj = scatter_finish(FWD)
    x_fwd = sti[plan[0, 0]].astype(f32)
    fo[...] = (x_fwd + fwd_proj * rms_of(fwd_proj) * gain(og, FWD)).astype(bf16)
    send(rcopy(fo, act_out, swap_s.at[1], swap_r.at[1], other))
    scatter_relay(2)
    for n in range(NCH):
        hidden = scatter_part(2, n)
        gb[0, :, cols(n)] = (hidden * ig[pl.ds(legs[BACK], 1), cols(n)]).astype(bf16)
        send(rcopy(gb.at[0, :, cols(n)], gb.at[1, :, cols(n)],
                   swap_s.at[3 + n], swap_r.at[3 + n], other))
    arrive(bo.at[0], swap_r.at[2])
    arrive(bo.at[1], swap_r.at[0])
    x_other = bo[0].astype(f32)
    scale = rms_of(x_other)
    for n in range(NCH):
        arrive(gb.at[1, :, cols(n)], swap_r.at[3 + n])
    g = gb[1].astype(f32)
    centred = g - x_other * (scale * scale * jnp.mean(g * x_other, axis=-1, keepdims=True))
    go[...] = (bo[1].astype(f32) + scale * centred).astype(bf16)
    final = pltpu.make_async_copy(go, grad_out, lsem.at[10])
    final.start()
    arrive(act_out, swap_r.at[1])
    for copy, cond in drains:
        when(cond, copy.wait_send)
    final.wait()


def per_device(
    stash_inputs, stash_grads, plan, query_weight, key_weight, value_weight, out_weight,
    input_gain, output_gain, query_gain, key_gain,
):
    frequency = rope_base ** (-(jnp.arange(HD // 2).astype(f32) * 2.0 / HD))
    vmem = pl.BlockSpec(memory_space=pltpu.VMEM)
    hbm = pl.BlockSpec(memory_space=pl.ANY)
    smem = pl.BlockSpec(memory_space=pltpu.SMEM)
    V = pltpu.VMEM
    sem = pltpu.SemaphoreType.DMA
    act, grad = pl.pallas_call(
        kernel,
        out_shape=(jax.ShapeDtypeStruct((ROWS, D), bf16),) * 2,
        in_specs=[smem] + [vmem] * 5 + [hbm] * 6,
        out_specs=(hbm, hbm),
        scratch_shapes=[
            V((2, D, 2 * HD), bf16), V((2, D, HD), bf16), V((2, D, HD), bf16), V((2, 2 * HD, D), bf16),
            V((4, ROWS, D), bf16), V((4, ROWS, D), bf16),
            V((3, 8, ROWS, D), bf16),
            V((2, 2 * TOK, HD), bf16), V((2 * TOK, HD), f32), V((TOK, HD), f32),
            V((2, 2, 5, TOK, HD), bf16), V((2, TOK, HD), bf16),
            V((2, 8, ROWS, 2 * HD), bf16),
            V((2 * TOK, 5 * TOK), f32), V((2 * TOK, 5 * TOK), bf16), V((2 * TOK, 5 * TOK), bf16),
            V((2 * TOK, HD), bf16),
            V((2, 4, ROWS, D), bf16), V((3, 4, ROWS, D), bf16), V((3, 3, ROWS, D), bf16),
            V((3, 2, ROWS // 2, D), bf16), V((3, 2, ROWS, D), bf16), V((2, ROWS, D), f32),
            V((2, 4, TOK, HD), bf16), V((6, 2, TOK, HD), bf16), V((2, 5, TOK, HD), f32),
            V((8, ROWS, 4 * HD), bf16),
            V((ROWS, D), bf16), V((ROWS, D), bf16), V((TOK, HD // 2), f32), V((TOK, HD // 2), f32),
            V((2 * 4 * ROWS, D), f32), V((2, ROWS, D), bf16), V((2, ROWS, D), bf16),
            sem((11,)), sem((3, 13)), sem((3, 13)), sem((3, NCH, 7)), sem((3, NCH, 7)),
            sem((2, 7, 2)), sem((2, 5, 2)), sem((6, 2)), sem((6, 2)), sem((3 + NCH,)), sem((3 + NCH,)),
        ],
        compiler_params=pltpu.CompilerParams(
            collective_id=0, has_side_effects=True, vmem_limit_bytes=67043328
        ),
    )(
        plan, frequency[None, :], input_gain[0], output_gain[0], query_gain[0],
        key_gain[0], stash_inputs[0], stash_grads[0], query_weight[0], key_weight[0],
        value_weight[0], out_weight[0],
    )
    return act[None], grad[None]


def solution(mesh):
    return jax.shard_map(
        per_device,
        mesh=mesh,
        in_specs=(
            P("segment", None, ("ctx", "tp"), None),
            P("segment", None, ("ctx", "tp"), None),
            P("segment", None),
            P("segment", None, None, "tp"),
            P("segment", None, None, "tp"),
            P("segment", None, None, "tp"),
            P("segment", None, "tp", None),
            P("segment", None, None),
            P("segment", None, None),
            P("segment", None, None),
            P("segment", None, None),
        ),
        out_specs=(P("segment", ("ctx", "tp"), None), P("segment", ("ctx", "tp"), None)),
        check_vma=False,
    )
```

```python
import jax
import jax.numpy as jnp
from jax import lax
from jax.experimental import pallas as pl
from jax.experimental.pallas import tpu as pltpu
from jax.sharding import PartitionSpec as P

WINDOW = 1024
epsilon = 1e-06
rope_base = 10000.0
masked_score = -1e30

D = 3840
ROWS = 32
TOK = 256
HD = 256
NCH = 3
CW = D // NCH
BACK, FWD, GRAD = 0, 1, 2
f32 = jnp.float32
bf16 = jnp.bfloat16
MESH = pl.DeviceIdType.MESH


def dot(a, b):
    return lax.dot_general(a, b, (((1,), (0,)), ((), ())), preferred_element_type=f32)


def dot_nt(a, b):
    return lax.dot_general(a, b, (((1,), (1,)), ((), ())), preferred_element_type=f32)


def dot_tn(a, b):
    return lax.dot_general(a, b, (((0,), (0,)), ((), ())), preferred_element_type=f32)


def rms_of(x):
    return lax.rsqrt(jnp.mean(x * x, axis=-1, keepdims=True) + epsilon)


def rms_back(x, grad, gain):
    g = grad * gain
    r = rms_of(x)
    return r * (g - x * (r * r * jnp.mean(g * x, axis=-1, keepdims=True)))


def rope(y, cosine, sine):
    a, b = y[:, : HD // 2], y[:, HD // 2 :]
    return jnp.concatenate([a * cosine - b * sine, b * cosine + a * sine], axis=-1)


def rope_back(g, cosine, sine):
    a, b = g[:, : HD // 2], g[:, HD // 2 :]
    return jnp.concatenate([a * cosine + b * sine, b * cosine - a * sine], axis=-1)


def kernel(
    plan, freq, ig, og, qg, kg, si, sg, wq_h, wk_h, wv_h, wo_h,
    act_out, grad_out,
    wq, wk, wv, wo, sti, stg, ag, qs, qraw, kraw, kvs, kvrl, grr, cx, pw, pl_s, dss, cgs,
    ps, pr, sb, rl, fr, own, gs, gr, gacc, lq, fo, go, cos_ref, sin_ref, hq, bo, gb,
    lsem, ags, agr, rss, rsr, kss, ksr, gss, gsr, swap_s, swap_r,
):
    s = lax.axis_index("segment")
    p = lax.axis_index("ctx")
    t = lax.axis_index("tp")
    yh, z = p // 4, p % 4
    y = 2 * yh + s
    x, c = t // 2, t % 2
    legs = (1 - s, s)

    def dev(s_=None, p_=None, t_=None):
        return {
            "segment": s if s_ is None else s_,
            "ctx": p if p_ is None else p_,
            "tp": t if t_ is None else t_,
        }

    t_r, t_l = ((x + 1) % 4) * 2 + c, ((x + 3) % 4) * 2 + c
    t_o = ((x + 2) % 4) * 2 + c
    t_p = 2 * x + 1 - c
    right, left, partner = dev(t_=t_r), dev(t_=t_l), dev(t_=t_p)
    z_up, z_dn = dev(p_=4 * yh + (z + 1) % 4), dev(p_=4 * yh + (z + 3) % 4)
    z_op = dev(p_=4 * yh + (z + 2) % 4)
    y_u, y_d = (y + 1) % 4, (y + 3) % 4
    y_up = dev(s_=y_u % 2, p_=(y_u // 2) * 4 + z)
    y_dn = dev(s_=y_d % 2, p_=(y_d // 2) * 4 + z)
    other = dev(s_=1 - s)

    barrier = pltpu.get_barrier_semaphore()
    for device in (right, left, partner, z_up, z_dn, z_op, y_up, y_dn):
        pl.semaphore_signal(barrier, inc=1, device_id=device, device_id_type=MESH)

    loads = [
        pltpu.make_async_copy(si, sti, lsem.at[0]),
        pltpu.make_async_copy(sg, stg, lsem.at[1]),
    ]
    for j in range(2):
        loads += [
            pltpu.make_async_copy(wq_h.at[legs[j]], wq.at[j], lsem.at[2 + 4 * j]),
            pltpu.make_async_copy(wk_h.at[legs[j]], wk.at[j], lsem.at[3 + 4 * j]),
            pltpu.make_async_copy(wv_h.at[legs[j]], wv.at[j], lsem.at[4 + 4 * j]),
            pltpu.make_async_copy(wo_h.at[legs[j]], wo.at[j], lsem.at[5 + 4 * j]),
        ]
    for load in loads:
        load.start()

    def gain(ref, j):
        return ref[pl.ds(legs[j], 1), :]

    def rcopy(src, dst, ssem, rsem, device):
        return pltpu.make_async_remote_copy(
            src_ref=src, dst_ref=dst, send_sem=ssem, recv_sem=rsem,
            device_id=device, device_id_type=MESH,
        )

    drains = []

    def when(cond, run):
        if cond is None:
            run()
        else:
            pl.when(cond)(run)

    def send(copy, cond=None):
        when(cond, copy.start)
        drains.append((copy, cond))

    def arrive(dst, rsem, cond=None):
        copy = rcopy(dst, dst, swap_s.at[0], rsem, partner)
        when(cond, copy.wait_recv)

    H0, H1 = pl.ds(0, ROWS // 2), pl.ds(ROWS // 2, ROWS // 2)
    halves = (H0, H1)

    def gather_start(j):
        blk = ag.at[j, t]
        send(rcopy(blk.at[H0], blk.at[H0], ags.at[j, 0], agr.at[j, 0], right))
        send(rcopy(blk.at[H1], blk.at[H1], ags.at[j, 1], agr.at[j, 1], left))
        send(rcopy(blk.at[H1], blk.at[H1], ags.at[j, 2], agr.at[j, 2], right))
        send(rcopy(blk.at[H0], blk.at[H0], ags.at[j, 3], agr.at[j, 3], left))
        send(rcopy(blk, blk, ags.at[j, 6], agr.at[j, 6], partner))

    def across(j, place, half, i):
        part = ag.at[j, place, halves[half]]
        send(rcopy(part, part, ags.at[j, i], agr.at[j, i], partner))

    def gather_relay(j):
        a = ag.at[j, t_l, H0]
        arrive(a, agr.at[j, 0])
        send(rcopy(a, a, ags.at[j, 4], agr.at[j, 4], right))
        b = ag.at[j, t_r, H1]
        arrive(b, agr.at[j, 1])
        send(rcopy(b, b, ags.at[j, 5], agr.at[j, 5], left))
        across(j, t_l, 0, 7)
        across(j, t_r, 1, 8)

    def gather_finish(j):
        arrive(ag.at[j, t_l, H1], agr.at[j, 2])
        across(j, t_l, 1, 9)
        arrive(ag.at[j, t_r, H0], agr.at[j, 3])
        across(j, t_r, 0, 10)
        arrive(ag.at[j, t_o, H0], agr.at[j, 4])
        across(j, t_o, 0, 11)
        arrive(ag.at[j, t_o, H1], agr.at[j, 5])
        across(j, t_o, 1, 12)
        u_r, u_l, u_o = t_r + 1 - 2 * c, t_l + 1 - 2 * c, t_o + 1 - 2 * c
        arrive(ag.at[j, t_p], agr.at[j, 6])
        arrive(ag.at[j, u_l, H0], agr.at[j, 7])
        arrive(ag.at[j, u_r, H1], agr.at[j, 8])
        arrive(ag.at[j, u_l, H1], agr.at[j, 9])
        arrive(ag.at[j, u_r, H0], agr.at[j, 10])
        arrive(ag.at[j, u_o, H0], agr.at[j, 11])
        arrive(ag.at[j, u_o, H1], agr.at[j, 12])

    def cols(n):
        return pl.ds(n * CW, CW)

    def rows_of(ref, parity):
        parts = [ref[2 * ((x + k) % 4) + parity] for k in range(4)]
        return jnp.concatenate(parts, axis=0)

    def rows_all(ref):
        return jnp.concatenate([rows_of(ref, 1 - c), rows_of(ref, c)], axis=0)

    def scatter_first(r, product, lhs):
        for n in range(NCH):
            total = product(lhs, n)
            ps[r % 2, :, :, cols(n)] = total[: 4 * ROWS].astype(bf16).reshape(4, ROWS, CW)
            send(rcopy(ps.at[r % 2, :, :, cols(n)], pr.at[r, :, :, cols(n)],
                       rss.at[r, n, 0], rsr.at[r, n, 0], partner))
            hq[4 * ROWS :, cols(n)] = total[4 * ROWS :]

    def scatter_second(r):
        for n in range(NCH):
            arrive(pr.at[r, :, :, cols(n)], rsr.at[r, n, 0])
            total = hq[4 * ROWS :, cols(n)].reshape(4, ROWS, CW) + pr[r, :, :, cols(n)].astype(f32)
            own[r % 2, :, cols(n)] = total[0]
            sb[r, :, :, cols(n)] = total[1:].astype(bf16)
            send(rcopy(sb.at[r, 1, H0, cols(n)], rl.at[r, 0, :, cols(n)],
                       rss.at[r, n, 1], rsr.at[r, n, 1], right))
            send(rcopy(sb.at[r, 1, H1, cols(n)], rl.at[r, 1, :, cols(n)],
                       rss.at[r, n, 2], rsr.at[r, n, 2], left))
            send(rcopy(sb.at[r, 0, H1, cols(n)], fr.at[r, 0, H1, cols(n)],
                       rss.at[r, n, 3], rsr.at[r, n, 3], right))
            send(rcopy(sb.at[r, 2, H0, cols(n)], fr.at[r, 1, H0, cols(n)],
                       rss.at[r, n, 4], rsr.at[r, n, 4], left))

    def scatter_relay(r):
        for n in range(NCH):
            arrive(rl.at[r, 0, :, cols(n)], rsr.at[r, n, 1])
            sb[r, 0, H0, cols(n)] = (
                sb[r, 0, H0, cols(n)].astype(f32) + rl[r, 0, :, cols(n)].astype(f32)
            ).astype(bf16)
            send(rcopy(sb.at[r, 0, H0, cols(n)], fr.at[r, 0, H0, cols(n)],
                       rss.at[r, n, 5], rsr.at[r, n, 5], right))
            arrive(rl.at[r, 1, :, cols(n)], rsr.at[r, n, 2])
            sb[r, 2, H1, cols(n)] = (
                sb[r, 2, H1, cols(n)].astype(f32) + rl[r, 1, :, cols(n)].astype(f32)
            ).astype(bf16)
            send(rcopy(sb.at[r, 2, H1, cols(n)], fr.at[r, 1, H1, cols(n)],
                       rss.at[r, n, 6], rsr.at[r, n, 6], left))

    def scatter_part(r, n):
        arrive(fr.at[r, 0, H1, cols(n)], rsr.at[r, n, 3])
        arrive(fr.at[r, 1, H0, cols(n)], rsr.at[r, n, 4])
        arrive(fr.at[r, 0, H0, cols(n)], rsr.at[r, n, 5])
        arrive(fr.at[r, 1, H1, cols(n)], rsr.at[r, n, 6])
        return own[r % 2, :, cols(n)] + (
            fr[r, 0, :, cols(n)].astype(f32) + fr[r, 1, :, cols(n)].astype(f32)
        )

    def scatter_finish(r):
        return jnp.concatenate([scatter_part(r, n) for n in range(NCH)], axis=-1)

    hi, lo = yh == 1, yh == 0
    mid = (z == 1) | (z == 2)

    relay_k = (y == 1) | (y == 2)
    relay_v = (y == 0) | (y == 3)

    def kv_near(j):
        for i in range(2):
            o = kvs.at[j, i, 0]
            send(rcopy(o, kvs.at[j, i, 1], kss.at[j, 1, i], ksr.at[j, 1, i], z_up), z < 3)
            send(rcopy(o, kvs.at[j, i, 3], kss.at[j, 3, i], ksr.at[j, 3, i], z_dn), z == 0)
            send(rcopy(o, kvs.at[j, i, 2], kss.at[j, 5, i], ksr.at[j, 2, i], z_op), lo & (z >= 2))

    def kv_cross(j):
        k, v = kvs.at[j, 0, 0], kvs.at[j, 1, 0]
        send(rcopy(k, kvrl.at[j, 0], kss.at[j, 6, 0], ksr.at[j, 0, 0], y_up), lo)
        send(rcopy(v, kvrl.at[j, 0], kss.at[j, 6, 1], ksr.at[j, 0, 0], y_dn), lo)

    def kv_relay(j):
        b = kvrl.at[j, 0]
        arrive(b, ksr.at[j, 0, 0])
        send(rcopy(b, kvs.at[j, 0, 4], kss.at[j, 4, 0], ksr.at[j, 4, 0], y_up), relay_k)
        send(rcopy(b, kvs.at[j, 1, 4], kss.at[j, 4, 1], ksr.at[j, 4, 1], y_dn), relay_v)

    def kv_second(j):
        low = z <= 1
        for i in range(2):
            b1, b2, b4 = (kvs.at[j, i, d] for d in (1, 2, 4))
            arrive(b2, ksr.at[j, 2, i], lo & low)
            send(rcopy(b2, kvrl.at[j, 1], kss.at[j, 0, i], ksr.at[j, 5, 0],
                       y_dn if i else y_up), lo & low)
            arrive(b1, ksr.at[j, 1, i], mid)
            send(rcopy(b1, kvs.at[j, i, 2], kss.at[j, 2, i], ksr.at[j, 2, i], z_up), mid)
            arrive(b4, ksr.at[j, 4, i], hi)
            send(rcopy(b4, kvs.at[j, i, 3], kss.at[j, 3, i], ksr.at[j, 3, i], z_dn), hi & (z >= 1))
            send(rcopy(b4, kvs.at[j, i, 1], kss.at[j, 1, i], ksr.at[j, 1, i], z_up), hi & (z == 3))

    def kv_third(j):
        low = z <= 1
        b = kvrl.at[j, 1]
        arrive(b, ksr.at[j, 5, 0], low)
        send(rcopy(b, kvs.at[j, 0, 2], kss.at[j, 7, 0], ksr.at[j, 2, 0], y_up), low & relay_k)
        send(rcopy(b, kvs.at[j, 1, 2], kss.at[j, 7, 1], ksr.at[j, 2, 1], y_dn), low & relay_v)

    def kv_finish(j):
        for i in range(2):
            arrive(kvs.at[j, i, 1], ksr.at[j, 1, i], (z == 3) | (hi & (z == 0)))
            arrive(kvs.at[j, i, 2], ksr.at[j, 2, i], (z >= 2) | hi)
            arrive(kvs.at[j, i, 3], ksr.at[j, 3, i], (z == 3) | hi)

    def project(j):
        cosine, sine = cos_ref[...], sin_ref[...]
        for load in loads[2 + 4 * j : 5 + 4 * j]:
            load.wait()
        xn = ag[j].reshape(TOK, D)
        q_gain, k_gain = gain(qg, j), gain(kg, j)
        kr = dot(xn, wk[j])
        kvs[j, 0, 0] = rope(kr * rms_of(kr) * k_gain, cosine, sine).astype(bf16)
        kvs[j, 1, 0] = dot(xn, wv[j]).astype(bf16)
        if j == BACK:
            kv_cross(j)
        kv_near(j)
        if j == BACK:
            kraw[...] = kr
        for h in range(2):
            qr = dot(xn, wq[j, :, h * HD : (h + 1) * HD])
            qs[j, h * TOK : (h + 1) * TOK] = rope(
                qr * rms_of(qr) * q_gain, cosine, sine
            ).astype(bf16)
            if j == BACK:
                qraw[h * TOK : (h + 1) * TOK] = qr

    def attention(j, keep):
        @pl.loop(0, 4)
        def _(ci):
            rows = pl.ds(pl.multiple_of(ci * 128, 128), 128)
            sc = dot_nt(qs[j, rows, :], kvs[j, 0].reshape(5 * TOK, HD)) * (HD ** -0.5)
            col = lax.broadcasted_iota(jnp.int32, (1, 5 * TOK), 1)
            back = (col // TOK) * TOK - col % TOK
            back = jnp.where(col // TOK <= p, back, -4 * WINDOW)
            ii = (ci % 2) * 128 + lax.broadcasted_iota(jnp.int32, (128, 1), 0)
            rel = ii + back
            sc = jnp.where((rel >= 0) & (rel < WINDOW), sc, masked_score)
            e = jnp.exp(sc - jnp.max(sc, axis=-1, keepdims=True))
            w = e / jnp.sum(e, axis=-1, keepdims=True)
            low = w.astype(bf16)
            if keep:
                pw[rows, :] = w
                pl_s[rows, :] = low
            out = dot(low, kvs[j, 1].reshape(5 * TOK, HD)).astype(bf16)
            for h in range(2):
                @pl.when(ci // 2 == h)
                def _():
                    cx[j, pl.ds(4 * (ci % 2), 4), :, h * HD : (h + 1) * HD] = out.reshape(
                        4, ROWS, HD
                    )

    def out_product(j):
        return lambda lhs, n: dot(lhs, wo[j, :, n * CW : (n + 1) * CW])

    def hidden_product(lhs, n):
        w_rows = slice(n * CW, (n + 1) * CW)
        total = hq[:, cols(n)] + dot_nt(lhs[:, 2 * HD : 3 * HD], wk[BACK, w_rows, :])
        return total + dot_nt(lhs[:, 3 * HD :], wv[BACK, w_rows, :])

    loads[0].wait()
    x_back = sti[plan[0, 1]].astype(f32)
    ag[BACK, t] = (x_back * rms_of(x_back) * gain(ig, BACK)).astype(bf16)
    pl.semaphore_wait(barrier, 8)
    gather_start(BACK)
    x_fwd = sti[plan[0, 0]].astype(f32)
    ag[FWD, t] = (x_fwd * rms_of(x_fwd) * gain(ig, FWD)).astype(bf16)
    for j in range(2):
        for d in (1, 3, 4):
            @pl.when(d > p)
            def _():
                for i in range(2):
                    kvs[j, i, d] = jnp.zeros((TOK, HD), bf16)
    angles = (p * TOK + lax.broadcasted_iota(jnp.int32, (TOK, HD // 2), 0)).astype(f32) * freq[...]
    cos_ref[...] = jnp.cos(angles)
    sin_ref[...] = jnp.sin(angles)
    gather_relay(BACK)
    gather_start(FWD)
    gather_finish(BACK)
    project(BACK)
    gather_relay(FWD)
    kv_relay(BACK)
    gather_finish(FWD)
    kv_second(BACK)
    project(FWD)
    kv_third(BACK)
    kv_cross(FWD)
    kv_relay(FWD)
    kv_finish(BACK)
    attention(BACK, True)
    loads[5].wait()
    before = len(drains)
    scatter_first(BACK, out_product(BACK), rows_all(cx.at[BACK]))
    kv_second(FWD)
    scatter_second(BACK)
    scatter_relay(BACK)
    kv_third(FWD)
    projected = scatter_finish(BACK)
    loads[1].wait()
    incoming = stg[plan[0, 1]].astype(f32)
    ag[GRAD, t] = rms_back(projected, incoming, gain(og, BACK)).astype(bf16)
    gather_start(GRAD)
    go[...] = sti[plan[0, 1]]
    fo[...] = stg[plan[0, 1]]
    ahead = (
        rcopy(go, bo.at[0], swap_s.at[2], swap_r.at[2], other),
        rcopy(fo, bo.at[1], swap_s.at[0], swap_r.at[0], other),
    )
    for copy in ahead:
        copy.start()
    kv_finish(FWD)
    attention(FWD, False)
    gather_relay(GRAD)
    loads[9].wait()
    scatter_first(FWD, out_product(FWD), rows_all(cx.at[FWD]))
    gather_finish(GRAD)

    og_rows = ag[GRAD].reshape(TOK, D)
    for h in range(2):
        cgs[h * TOK : (h + 1) * TOK] = dot_nt(
            og_rows, wo[BACK, h * HD : (h + 1) * HD, :]
        ).astype(bf16)
    q_gain, k_gain = gain(qg, BACK), gain(kg, BACK)

    R1, R2, R3, R4, R5, RR, RS = 0, 1, 2, 3, 4, 5, 6
    OWN, ONE, FOUR = 0, 1, 2

    def grad_block(i, d):
        if i == 0:
            return dot_tn(dss[:, d * TOK : (d + 1) * TOK], qs[BACK])
        return dot_tn(pl_s[:, d * TOK : (d + 1) * TOK], cgs[...])

    def g_send(d, e, se, device, cond, i):
        send(rcopy(gs.at[i, d - 1], gr.at[e, i], gss.at[se, i], gsr.at[e, i], device), cond)

    def g_add(e, k, cond, i):
        arrive(gr.at[e, i], gsr.at[e, i], cond)

        @pl.when(cond)
        def _():
            gacc[i, k] = gacc[i, k] + gr[e, i].astype(f32)

    def g_first(i):
        gs[i, 1] = grad_block(i, 2).astype(bf16)
        send(rcopy(gs.at[i, 1], grr.at[1], gss.at[1, i], gsr.at[RS, 0],
                   y_up if i else y_dn), hi & (z <= 1))
        g_send(2, R2, 0, z_dn, z >= 2, i)
        gs[i, 2] = grad_block(i, 3).astype(bf16)
        g_send(3, R3, 2, z_up, (z == 3) | hi, i)
        gacc[i, ONE] = grad_block(i, 1)
        gs[i, 0] = gacc[i, ONE].astype(bf16)
        g_send(1, R1, 3, z_dn, (z == 3) | (hi & (z == 0)), i)
        gacc[i, FOUR] = grad_block(i, 4)
        gacc[i, OWN] = grad_block(i, 0)

    def g_middle(i):
        g_add(R2, ONE, mid, i)

        @pl.when(mid)
        def _():
            gs[i, 0] = gacc[i, ONE].astype(bf16)
        g_send(1, R1, 3, z_dn, mid, i)

    def g_third(i):
        g_add(R3, FOUR, hi & (z >= 1), i)
        g_add(R1, FOUR, hi & (z == 3), i)
        gs[i, 3] = gacc[i, FOUR].astype(bf16)
        send(rcopy(gs.at[i, 3], grr.at[0], gss.at[4, i], gsr.at[RR, 0],
                   y_up if i else y_dn), hi)

    def g_relay(i, far):
        cond, device = (relay_v, y_up) if i else (relay_k, y_dn)
        if far:
            cond = cond & (z <= 1)
        buf, rsem = grr.at[far], gsr.at[RS if far else RR, 0]
        e = R5 if far else R4
        arrive(buf, rsem, cond)
        send(rcopy(buf, gr.at[e, i], gss.at[6 if far else 5, i], gsr.at[e, i], device), cond)

    def g_forward(i):
        cond = lo & (z <= 1)
        arrive(gr.at[R5, i], gsr.at[R5, i], cond)
        send(rcopy(gr.at[R5, i], gr.at[R5, i], gss.at[7, i], gsr.at[R5, i], z_op), cond)

    g_first(1)

    @pl.loop(0, 4)
    def _(ci):
        rows = pl.ds(pl.multiple_of(ci * 128, 128), 128)
        w = pw[rows, :]
        wg = dot_nt(cgs[rows, :], kvs[BACK, 1].reshape(5 * TOK, HD))
        delta = jnp.sum(w * wg, axis=-1, keepdims=True)
        dss[rows, :] = (w * (wg - delta) * (HD ** -0.5)).astype(bf16)

    g_first(0)
    g_middle(1)
    g_third(1)
    g_relay(1, 1)
    scatter_second(FWD)
    g_middle(0)
    g_third(0)
    g_relay(0, 1)

    for h in range(2):
        rows = slice(h * TOK, (h + 1) * TOK)
        dq = dot(dss[rows, :], kvs[BACK, 0].reshape(5 * TOK, HD))
        low = rms_back(
            qraw[rows], rope_back(dq, cos_ref[...], sin_ref[...]), q_gain
        ).astype(bf16)
        lq[:, :, h * HD : (h + 1) * HD] = low.reshape(8, ROWS, HD)
    query_low = rows_all(lq)[:, : 2 * HD]
    for n in range(NCH):
        hq[:, cols(n)] = dot_nt(query_low, wq[BACK, n * CW : (n + 1) * CW, :])

    g_forward(1)
    g_relay(1, 0)
    g_forward(0)
    g_relay(0, 0)
    for copy in ahead:
        copy.wait_send()
    scatter_relay(FWD)
    for i in (1, 0):
        g_add(R1, OWN, z < 3, i)
        g_add(R3, OWN, z == 0, i)
        g_add(R4, OWN, lo, i)
        g_add(R5, OWN, lo & (z >= 2), i)
    key_low = rms_back(
        kraw[...], rope_back(gacc[0, 0], cos_ref[...], sin_ref[...]), k_gain
    ).astype(bf16)
    lq[:, :, 2 * HD : 3 * HD] = key_low.reshape(8, ROWS, HD)
    lq[:, :, 3 * HD :] = gacc[1, 0].astype(bf16).reshape(8, ROWS, HD)

    for copy, _ in drains[before : before + NCH]:
        copy.wait_send()
    del drains[before : before + NCH]
    scatter_first(2, hidden_product, rows_all(lq))
    scatter_second(2)
    fwd_proj = scatter_finish(FWD)
    x_fwd = sti[plan[0, 0]].astype(f32)
    fo[...] = (x_fwd + fwd_proj * rms_of(fwd_proj) * gain(og, FWD)).astype(bf16)
    send(rcopy(fo, act_out, swap_s.at[1], swap_r.at[1], other))
    scatter_relay(2)
    for n in range(NCH):
        hidden = scatter_part(2, n)
        gb[0, :, cols(n)] = (hidden * ig[pl.ds(legs[BACK], 1), cols(n)]).astype(bf16)
        send(rcopy(gb.at[0, :, cols(n)], gb.at[1, :, cols(n)],
                   swap_s.at[3 + n], swap_r.at[3 + n], other))
    arrive(bo.at[0], swap_r.at[2])
    arrive(bo.at[1], swap_r.at[0])
    x_other = bo[0].astype(f32)
    scale = rms_of(x_other)
    for n in range(NCH):
        arrive(gb.at[1, :, cols(n)], swap_r.at[3 + n])
    g = gb[1].astype(f32)
    centred = g - x_other * (scale * scale * jnp.mean(g * x_other, axis=-1, keepdims=True))
    go[...] = (bo[1].astype(f32) + scale * centred).astype(bf16)
    final = pltpu.make_async_copy(go, grad_out, lsem.at[10])
    final.start()
    arrive(act_out, swap_r.at[1])
    for copy, cond in drains:
        when(cond, copy.wait_send)
    final.wait()


def per_device(
    stash_inputs, stash_grads, plan, query_weight, key_weight, value_weight, out_weight,
    input_gain, output_gain, query_gain, key_gain,
):
    frequency = rope_base ** (-(jnp.arange(HD // 2).astype(f32) * 2.0 / HD))
    vmem = pl.BlockSpec(memory_space=pltpu.VMEM)
    hbm = pl.BlockSpec(memory_space=pl.ANY)
    smem = pl.BlockSpec(memory_space=pltpu.SMEM)
    V = pltpu.VMEM
    sem = pltpu.SemaphoreType.DMA
    act, grad = pl.pallas_call(
        kernel,
        out_shape=(jax.ShapeDtypeStruct((ROWS, D), bf16),) * 2,
        in_specs=[smem] + [vmem] * 5 + [hbm] * 6,
        out_specs=(hbm, hbm),
        scratch_shapes=[
            V((2, D, 2 * HD), bf16), V((2, D, HD), bf16), V((2, D, HD), bf16), V((2, 2 * HD, D), bf16),
            V((4, ROWS, D), bf16), V((4, ROWS, D), bf16),
            V((3, 8, ROWS, D), bf16),
            V((2, 2 * TOK, HD), bf16), V((2 * TOK, HD), f32), V((TOK, HD), f32),
            V((2, 2, 5, TOK, HD), bf16), V((2, 2, TOK, HD), bf16), V((2, TOK, HD), bf16),
            V((2, 8, ROWS, 2 * HD), bf16),
            V((2 * TOK, 5 * TOK), f32), V((2 * TOK, 5 * TOK), bf16), V((2 * TOK, 5 * TOK), bf16),
            V((2 * TOK, HD), bf16),
            V((2, 4, ROWS, D), bf16), V((3, 4, ROWS, D), bf16), V((3, 3, ROWS, D), bf16),
            V((3, 2, ROWS // 2, D), bf16), V((3, 2, ROWS, D), bf16), V((2, ROWS, D), f32),
            V((2, 4, TOK, HD), bf16), V((5, 2, TOK, HD), bf16), V((2, 3, TOK, HD), f32),
            V((8, ROWS, 4 * HD), bf16),
            V((ROWS, D), bf16), V((ROWS, D), bf16), V((TOK, HD // 2), f32), V((TOK, HD // 2), f32),
            V((2 * 4 * ROWS, D), f32), V((2, ROWS, D), bf16), V((2, ROWS, D), bf16),
            sem((11,)), sem((3, 13)), sem((3, 13)), sem((3, NCH, 7)), sem((3, NCH, 7)),
            sem((2, 8, 2)), sem((2, 6, 2)), sem((8, 2)), sem((7, 2)), sem((3 + NCH,)), sem((3 + NCH,)),
        ],
        compiler_params=pltpu.CompilerParams(
            collective_id=0, has_side_effects=True, vmem_limit_bytes=67043328
        ),
    )(
        plan, frequency[None, :], input_gain[0], output_gain[0], query_gain[0],
        key_gain[0], stash_inputs[0], stash_grads[0], query_weight[0], key_weight[0],
        value_weight[0], out_weight[0],
    )
    return act[None], grad[None]


def solution(mesh):
    return jax.shard_map(
        per_device,
        mesh=mesh,
        in_specs=(
            P("segment", None, ("ctx", "tp"), None),
            P("segment", None, ("ctx", "tp"), None),
            P("segment", None),
            P("segment", None, None, "tp"),
            P("segment", None, None, "tp"),
            P("segment", None, None, "tp"),
            P("segment", None, "tp", None),
            P("segment", None, None),
            P("segment", None, None),
            P("segment", None, None),
            P("segment", None, None),
        ),
        out_specs=(P("segment", ("ctx", "tp"), None), P("segment", ("ctx", "tp"), None)),
        check_vma=False,
    )
```

```python
import math

import jax
import jax.numpy as jnp
from jax import lax
from jax.experimental import pallas as pl
from jax.experimental.pallas import tpu as pltpu
from jax.sharding import PartitionSpec as P

WINDOW = 1024
epsilon = 1e-06
rope_base = 10000.0
masked_score = -1e30

D = 3840
ROWS = 32
TOK = 256
HD = 256
NCH = 5
CW = D // NCH
BACK, FWD, GRAD = 0, 1, 2
f32 = jnp.float32
bf16 = jnp.bfloat16
MESH = pl.DeviceIdType.MESH


def dot(a, b):
    return lax.dot_general(a, b, (((1,), (0,)), ((), ())), preferred_element_type=f32)


def dot_nt(a, b):
    return lax.dot_general(a, b, (((1,), (1,)), ((), ())), preferred_element_type=f32)


def dot_tn(a, b):
    return lax.dot_general(a, b, (((0,), (0,)), ((), ())), preferred_element_type=f32)


def rms_of(x):
    return lax.rsqrt(jnp.mean(x * x, axis=-1, keepdims=True) + epsilon)


def rms_back(x, grad, gain):
    g = grad * gain
    r = rms_of(x)
    return r * (g - x * (r * r * jnp.mean(g * x, axis=-1, keepdims=True)))


def rope(y, cosine, sine):
    a, b = y[:, : HD // 2], y[:, HD // 2 :]
    return jnp.concatenate([a * cosine - b * sine, b * cosine + a * sine], axis=-1)


def rope_back(g, cosine, sine):
    a, b = g[:, : HD // 2], g[:, HD // 2 :]
    return jnp.concatenate([a * cosine + b * sine, b * cosine - a * sine], axis=-1)


def kernel(
    plan, ig_h, og_h, qg_h, kg_h, si, sg, wq_h, wk_h, wv_h, wo_h,
    act_out, grad_out,
    wq, wk, wv, wo, sti, stg, ag, qs, qraw, kraw, kvs, kvrl, grr, cx, pw, pl_s, dss, cgs,
    ps, pr, sb, rl, fr, own, gs, gr, gacc, lq, fo, go, cos_ref, sin_ref, hq, bo, gb, ig, og, qg, kg, tops, sums,
    lsem, ags, agr, rss, rsr, kss, ksr, gss, gsr, swap_s, swap_r,
):
    s = lax.axis_index("segment")
    p = lax.axis_index("ctx")
    t = lax.axis_index("tp")
    yh, z = p // 4, p % 4
    y = 2 * yh + s
    x, c = t // 2, t % 2
    legs = (1 - s, s)

    def dev(s_=None, p_=None, t_=None):
        return {
            "segment": s if s_ is None else s_,
            "ctx": p if p_ is None else p_,
            "tp": t if t_ is None else t_,
        }

    t_r, t_l = ((x + 1) % 4) * 2 + c, ((x + 3) % 4) * 2 + c
    t_o = ((x + 2) % 4) * 2 + c
    t_p = 2 * x + 1 - c
    right, left, partner = dev(t_=t_r), dev(t_=t_l), dev(t_=t_p)
    z_up, z_dn = dev(p_=4 * yh + (z + 1) % 4), dev(p_=4 * yh + (z + 3) % 4)
    z_op = dev(p_=4 * yh + (z + 2) % 4)
    y_u, y_d = (y + 1) % 4, (y + 3) % 4
    y_up = dev(s_=y_u % 2, p_=(y_u // 2) * 4 + z)
    y_dn = dev(s_=y_d % 2, p_=(y_d // 2) * 4 + z)
    other = dev(s_=1 - s)

    barrier = pltpu.get_barrier_semaphore()
    for device in (right, left, partner, z_up, z_dn, z_op, y_up, y_dn):
        pl.semaphore_signal(barrier, inc=1, device_id=device, device_id_type=MESH)

    loads = [
        pltpu.make_async_copy(si, sti, lsem.at[0]),
        pltpu.make_async_copy(sg, stg, lsem.at[1]),
    ]
    for j in range(2):
        loads += [
            pltpu.make_async_copy(wq_h.at[legs[j]], wq.at[j], lsem.at[2 + 4 * j]),
            pltpu.make_async_copy(wk_h.at[legs[j]], wk.at[j], lsem.at[3 + 4 * j]),
            pltpu.make_async_copy(wv_h.at[legs[j]], wv.at[j], lsem.at[4 + 4 * j]),
            pltpu.make_async_copy(wo_h.at[legs[j]], wo.at[j], lsem.at[5 + 4 * j]),
        ]
    small = [
        pltpu.make_async_copy(src, dst, lsem.at[11 + k])
        for k, (src, dst) in enumerate(((ig_h, ig), (og_h, og), (qg_h, qg), (kg_h, kg)))
    ]
    for load in loads[:1] + small + loads[1:]:
        load.start()

    def gain(ref, j):
        return ref[pl.ds(legs[j], 1), :]

    def rcopy(src, dst, ssem, rsem, device):
        return pltpu.make_async_remote_copy(
            src_ref=src, dst_ref=dst, send_sem=ssem, recv_sem=rsem,
            device_id=device, device_id_type=MESH,
        )

    drains = []

    def when(cond, run):
        if cond is None:
            run()
        else:
            pl.when(cond)(run)

    def send(copy, cond=None):
        when(cond, copy.start)
        drains.append((copy, cond))

    def arrive(dst, rsem, cond=None):
        copy = rcopy(dst, dst, swap_s.at[0], rsem, partner)
        when(cond, copy.wait_recv)

    H0, H1 = pl.ds(0, ROWS // 2), pl.ds(ROWS // 2, ROWS // 2)
    halves = (H0, H1)

    def gather_start(j):
        blk = ag.at[j, t]
        send(rcopy(blk.at[H0], blk.at[H0], ags.at[j, 0], agr.at[j, 0], right))
        send(rcopy(blk.at[H1], blk.at[H1], ags.at[j, 1], agr.at[j, 1], left))
        send(rcopy(blk.at[H1], blk.at[H1], ags.at[j, 2], agr.at[j, 2], right))
        send(rcopy(blk.at[H0], blk.at[H0], ags.at[j, 3], agr.at[j, 3], left))
        send(rcopy(blk, blk, ags.at[j, 6], agr.at[j, 6], partner))

    def across(j, place, half, i):
        part = ag.at[j, place, halves[half]]
        send(rcopy(part, part, ags.at[j, i], agr.at[j, i], partner))

    def gather_relay(j):
        a = ag.at[j, t_l, H0]
        arrive(a, agr.at[j, 0])
        send(rcopy(a, a, ags.at[j, 4], agr.at[j, 4], right))
        b = ag.at[j, t_r, H1]
        arrive(b, agr.at[j, 1])
        send(rcopy(b, b, ags.at[j, 5], agr.at[j, 5], left))
        across(j, t_l, 0, 7)
        across(j, t_r, 1, 8)

    def gather_finish(j):
        arrive(ag.at[j, t_l, H1], agr.at[j, 2])
        across(j, t_l, 1, 9)
        arrive(ag.at[j, t_r, H0], agr.at[j, 3])
        across(j, t_r, 0, 10)
        arrive(ag.at[j, t_o, H0], agr.at[j, 4])
        across(j, t_o, 0, 11)
        arrive(ag.at[j, t_o, H1], agr.at[j, 5])
        across(j, t_o, 1, 12)
        u_r, u_l, u_o = t_r + 1 - 2 * c, t_l + 1 - 2 * c, t_o + 1 - 2 * c
        arrive(ag.at[j, t_p], agr.at[j, 6])
        arrive(ag.at[j, u_l, H0], agr.at[j, 7])
        arrive(ag.at[j, u_r, H1], agr.at[j, 8])
        arrive(ag.at[j, u_l, H1], agr.at[j, 9])
        arrive(ag.at[j, u_r, H0], agr.at[j, 10])
        arrive(ag.at[j, u_o, H0], agr.at[j, 11])
        arrive(ag.at[j, u_o, H1], agr.at[j, 12])

    def cols(n):
        return pl.ds(n * CW, CW)

    def rows_of(ref, parity):
        parts = [ref[2 * ((x + k) % 4) + parity] for k in range(4)]
        return jnp.concatenate(parts, axis=0)

    def rows_all(ref):
        return jnp.concatenate([rows_of(ref, 1 - c), rows_of(ref, c)], axis=0)

    def scatter_first(r, product, lhs):
        for n in range(NCH):
            total = product(lhs, n)
            ps[r % 2, :, :, cols(n)] = total[: 4 * ROWS].astype(bf16).reshape(4, ROWS, CW)
            send(rcopy(ps.at[r % 2, :, :, cols(n)], pr.at[r, :, :, cols(n)],
                       rss.at[r, n, 0], rsr.at[r, n, 0], partner))
            hq[4 * ROWS :, cols(n)] = total[4 * ROWS :]

    def scatter_second(r):
        for n in range(NCH):
            arrive(pr.at[r, :, :, cols(n)], rsr.at[r, n, 0])
            total = hq[4 * ROWS :, cols(n)].reshape(4, ROWS, CW) + pr[r, :, :, cols(n)].astype(f32)
            own[r % 2, :, cols(n)] = total[0]
            sb[r, :, :, cols(n)] = total[1:].astype(bf16)
            send(rcopy(sb.at[r, 1, H0, cols(n)], rl.at[r, 0, :, cols(n)],
                       rss.at[r, n, 1], rsr.at[r, n, 1], right))
            send(rcopy(sb.at[r, 1, H1, cols(n)], rl.at[r, 1, :, cols(n)],
                       rss.at[r, n, 2], rsr.at[r, n, 2], left))
            send(rcopy(sb.at[r, 0, H1, cols(n)], fr.at[r, 0, H1, cols(n)],
                       rss.at[r, n, 3], rsr.at[r, n, 3], right))
            send(rcopy(sb.at[r, 2, H0, cols(n)], fr.at[r, 1, H0, cols(n)],
                       rss.at[r, n, 4], rsr.at[r, n, 4], left))

    def scatter_relay(r):
        for n in range(NCH):
            arrive(rl.at[r, 0, :, cols(n)], rsr.at[r, n, 1])
            sb[r, 0, H0, cols(n)] = (
                sb[r, 0, H0, cols(n)].astype(f32) + rl[r, 0, :, cols(n)].astype(f32)
            ).astype(bf16)
            send(rcopy(sb.at[r, 0, H0, cols(n)], fr.at[r, 0, H0, cols(n)],
                       rss.at[r, n, 5], rsr.at[r, n, 5], right))
            arrive(rl.at[r, 1, :, cols(n)], rsr.at[r, n, 2])
            sb[r, 2, H1, cols(n)] = (
                sb[r, 2, H1, cols(n)].astype(f32) + rl[r, 1, :, cols(n)].astype(f32)
            ).astype(bf16)
            send(rcopy(sb.at[r, 2, H1, cols(n)], fr.at[r, 1, H1, cols(n)],
                       rss.at[r, n, 6], rsr.at[r, n, 6], left))

    def scatter_part(r, n):
        arrive(fr.at[r, 0, H1, cols(n)], rsr.at[r, n, 3])
        arrive(fr.at[r, 1, H0, cols(n)], rsr.at[r, n, 4])
        arrive(fr.at[r, 0, H0, cols(n)], rsr.at[r, n, 5])
        arrive(fr.at[r, 1, H1, cols(n)], rsr.at[r, n, 6])
        return own[r % 2, :, cols(n)] + (
            fr[r, 0, :, cols(n)].astype(f32) + fr[r, 1, :, cols(n)].astype(f32)
        )

    def scatter_finish(r):
        return jnp.concatenate([scatter_part(r, n) for n in range(NCH)], axis=-1)

    hi, lo = yh == 1, yh == 0
    mid = (z == 1) | (z == 2)

    relay_k = (y == 1) | (y == 2)
    relay_v = (y == 0) | (y == 3)

    TH = (pl.ds(0, TOK // 2), pl.ds(TOK // 2, TOK // 2))

    def kv_near(j):
        for i in range(2):
            o = kvs.at[j, i, 0]
            send(rcopy(o, kvs.at[j, i, 1], kss.at[j, 1, i], ksr.at[j, 1, i], z_up), z < 3)
            send(rcopy(o, kvs.at[j, i, 3], kss.at[j, 3, i], ksr.at[j, 3, i], z_dn), z == 0)
            send(rcopy(o, kvs.at[j, i, 2], kss.at[j, 5, i], ksr.at[j, 2, i], z_op), lo & (z == 3))
            send(rcopy(o, kvs.at[j, i, 3], kss.at[j, 3, i], ksr.at[j, 3, i], z_dn), lo & (z == 1))

    def kv_cross(j):
        k, v = kvs.at[j, 0, 0], kvs.at[j, 1, 0]
        send(rcopy(k, kvrl.at[j, 0], kss.at[j, 6, 0], ksr.at[j, 0, 0], y_up), lo)
        send(rcopy(v, kvrl.at[j, 0], kss.at[j, 6, 1], ksr.at[j, 0, 0], y_dn), lo)

    def kv_relay(j):
        b = kvrl.at[j, 0]
        arrive(b, ksr.at[j, 0, 0])
        send(rcopy(b, kvs.at[j, 0, 4], kss.at[j, 4, 0], ksr.at[j, 4, 0], y_up), relay_k)
        send(rcopy(b, kvs.at[j, 1, 4], kss.at[j, 4, 1], ksr.at[j, 4, 1], y_dn), relay_v)

    def kv_second(j):
        low = z <= 1
        far = jnp.maximum(3 - z, 2)
        for i in range(2):
            b1, b2, b4 = (kvs.at[j, i, d] for d in (1, far, 4))
            arrive(b2, ksr.at[j, far, i], lo & low)
            send(rcopy(b2, kvrl.at[j, 1], kss.at[j, 0, i], ksr.at[j, 5, 0],
                       y_dn if i else y_up), lo & low)
            arrive(b1, ksr.at[j, 1, i], mid)
            send(rcopy(b1, kvs.at[j, i, 2], kss.at[j, 2, i], ksr.at[j, 2, i], z_up), mid)
            arrive(b4, ksr.at[j, 4, i], hi)
            if i == 0:
                send(rcopy(b4, kvs.at[j, 0, 3], kss.at[j, 3, 0], ksr.at[j, 3, 0], z_dn), hi & (z >= 2))
            else:
                send(rcopy(b4, kvs.at[j, 1, 3], kss.at[j, 3, 1], ksr.at[j, 3, 1], z_dn), hi & (z == 3))
                for q in range(2):
                    send(rcopy(b4.at[TH[q]], kvs.at[j, 1, 3, TH[q]], kss.at[j, 8, q],
                               ksr.at[j, 6, q], z_dn), hi & (z == 2))
            send(rcopy(b4, kvs.at[j, i, 1], kss.at[j, 1, i], ksr.at[j, 1, i], z_up), hi & (z == 3))

    def kv_third(j):
        low = z <= 1
        b = kvrl.at[j, 1]
        arrive(b, ksr.at[j, 5, 0], low)
        far = jnp.maximum(3 - z, 2)
        send(rcopy(b, kvs.at[j, 0, far], kss.at[j, 7, 0], ksr.at[j, far, 0], y_up), low & relay_k)
        send(rcopy(b, kvs.at[j, 1, far], kss.at[j, 7, 1], ksr.at[j, far, 1], y_dn), low & relay_v)

    def kv_fourth(j):
        cond = hi & (z == 1)
        b3 = kvs.at[j, 0, 3]
        arrive(b3, ksr.at[j, 3, 0], cond)
        send(rcopy(b3, kvs.at[j, 0, 2], kss.at[j, 5, 0], ksr.at[j, 2, 0], z_dn), cond)
        for q in range(2):
            b3 = kvs.at[j, 1, 3, TH[q]]
            arrive(b3, ksr.at[j, 6, q], cond)
            send(rcopy(b3, kvs.at[j, 1, 2, TH[q]], kss.at[j, 9, q], ksr.at[j, 7, q], z_dn), cond)

    def kv_near_in(j):
        for i in range(2):
            arrive(kvs.at[j, i, 1], ksr.at[j, 1, i], (z == 3) | (hi & (z == 0)))
            arrive(kvs.at[j, i, 3], ksr.at[j, 3, i], (z == 3) | (hi & (z != 1)))

    def kv_far_in(j):
        four = hi & (z == 0)
        arrive(kvs.at[j, 0, 2], ksr.at[j, 2, 0], (z >= 2) | hi)
        arrive(kvs.at[j, 1, 2], ksr.at[j, 2, 1], (z >= 2) | (hi & (z == 1)))
        for q in range(2):
            arrive(kvs.at[j, 1, 2, TH[q]], ksr.at[j, 7, q], four)

    def kv_finish(j):
        kv_near_in(j)
        kv_far_in(j)

    def project(j):
        cosine, sine = cos_ref[...], sin_ref[...]
        for load in loads[2 + 4 * j : 5 + 4 * j]:
            load.wait()
        xn = ag[j].reshape(TOK, D)
        q_gain, k_gain = gain(qg, j), gain(kg, j)
        kr = dot(xn, wk[j])
        kvs[j, 0, 0] = rope(kr * rms_of(kr) * k_gain, cosine, sine).astype(bf16)
        kvs[j, 1, 0] = dot(xn, wv[j]).astype(bf16)
        if j == BACK:
            kv_cross(j)
        kv_near(j)
        if j == BACK:
            kraw[...] = kr
        for h in range(2):
            qr = dot(xn, wq[j, :, h * HD : (h + 1) * HD])
            qs[j, h * TOK : (h + 1) * TOK] = rope(
                qr * rms_of(qr) * q_gain, cosine, sine
            ).astype(bf16)
            if j == BACK:
                qraw[h * TOK : (h + 1) * TOK] = qr

    def visible(ci, first, count):
        col = first * TOK + lax.broadcasted_iota(jnp.int32, (1, count * TOK), 1)
        back = (col // TOK) * TOK - col % TOK
        back = jnp.where(col // TOK <= p, back, -4 * WINDOW)
        rel = (ci % 2) * 128 + lax.broadcasted_iota(jnp.int32, (128, 1), 0) + back
        return (rel >= 0) & (rel < WINDOW)

    def scores(j, ci, rows, first, count):
        keys = kvs[j, 0, first : first + count].reshape(count * TOK, HD)
        sc = dot_nt(qs[j, rows, :], keys) * (HD ** -0.5)
        return jnp.where(visible(ci, first, count), sc, masked_score)

    def chunk_rows(ci):
        return pl.ds(pl.multiple_of(ci * 128, 128), 128)

    def weigh(j, ci, low):
        out = dot(low, kvs[j, 1].reshape(5 * TOK, HD)).astype(bf16)
        for h in range(2):
            @pl.when(ci // 2 == h)
            def _():
                cx[j, pl.ds(4 * (ci % 2), 4), :, h * HD : (h + 1) * HD] = out.reshape(4, ROWS, HD)

    def attend_near():
        @pl.loop(0, 4)
        def _(ci):
            rows = chunk_rows(ci)
            sa, sb_ = scores(BACK, ci, rows, 0, 2), scores(BACK, ci, rows, 3, 2)
            top = jnp.maximum(
                jnp.max(sa, axis=-1, keepdims=True), jnp.max(sb_, axis=-1, keepdims=True)
            )
            ea, eb = jnp.exp(sa - top), jnp.exp(sb_ - top)
            pw[rows, : 2 * TOK] = ea
            pw[rows, 3 * TOK :] = eb
            tops[rows, :] = top
            sums[rows, :] = jnp.sum(ea, axis=-1, keepdims=True) + jnp.sum(eb, axis=-1, keepdims=True)

    def attend_far():
        @pl.loop(0, 4)
        def _(ci):
            rows = chunk_rows(ci)
            sc = scores(BACK, ci, rows, 2, 1)
            top = jnp.maximum(tops[rows, :], jnp.max(sc, axis=-1, keepdims=True))
            e = jnp.exp(sc - top)
            near = jnp.exp(tops[rows, :] - top)
            inverse = 1.0 / (sums[rows, :] * near + jnp.sum(e, axis=-1, keepdims=True))
            near = near * inverse
            w = jnp.concatenate(
                [pw[rows, : 2 * TOK] * near, e * inverse, pw[rows, 3 * TOK :] * near], axis=-1
            )
            low = w.astype(bf16)
            pw[rows, :] = w
            pl_s[rows, :] = low
            weigh(BACK, ci, low)

    def attention(j):
        @pl.loop(0, 4)
        def _(ci):
            sc = scores(j, ci, chunk_rows(ci), 0, 5)
            e = jnp.exp(sc - jnp.max(sc, axis=-1, keepdims=True))
            w = e * (1.0 / jnp.sum(e, axis=-1, keepdims=True))
            weigh(j, ci, w.astype(bf16))

    def out_product(j):
        return lambda lhs, n: dot(lhs, wo[j, :, n * CW : (n + 1) * CW])

    def hidden_product(lhs, n):
        w_rows = slice(n * CW, (n + 1) * CW)
        total = hq[:, cols(n)] + dot_nt(lhs[:, 2 * HD : 3 * HD], wk[BACK, w_rows, :])
        return total + dot_nt(lhs[:, 3 * HD :], wv[BACK, w_rows, :])

    loads[0].wait()
    for load in small:
        load.wait()
    x_back = sti[plan[0, 1]].astype(f32)
    ag[BACK, t] = (x_back * rms_of(x_back) * gain(ig, BACK)).astype(bf16)
    pl.semaphore_wait(barrier, 8)
    gather_start(BACK)
    x_fwd = sti[plan[0, 0]].astype(f32)
    ag[FWD, t] = (x_fwd * rms_of(x_fwd) * gain(ig, FWD)).astype(bf16)
    for j in range(2):
        for d in range(1, 5):
            @pl.when((d > p) & (d + p != 3))
            def _():
                for i in range(2):
                    kvs[j, i, d] = jnp.zeros((TOK, HD), bf16)
    angles = (p * TOK + lax.broadcasted_iota(jnp.int32, (TOK, HD // 2), 0)).astype(f32)
    pair = lax.broadcasted_iota(jnp.int32, (1, HD // 2), 1).astype(f32)
    angles = angles * jnp.exp(pair * (-2.0 * math.log(rope_base) / HD))
    cos_ref[...] = jnp.cos(angles)
    sin_ref[...] = jnp.sin(angles)
    gather_relay(BACK)
    gather_start(FWD)
    gather_finish(BACK)
    project(BACK)
    gather_relay(FWD)
    kv_relay(BACK)
    gather_finish(FWD)
    kv_second(BACK)
    project(FWD)
    kv_third(BACK)
    kv_cross(FWD)
    kv_fourth(BACK)
    kv_near_in(BACK)
    attend_near()
    kv_relay(FWD)
    kv_far_in(BACK)
    attend_far()
    loads[5].wait()
    before = len(drains)
    scatter_first(BACK, out_product(BACK), rows_all(cx.at[BACK]))
    kv_second(FWD)
    scatter_second(BACK)
    scatter_relay(BACK)
    kv_third(FWD)
    kv_fourth(FWD)
    projected = scatter_finish(BACK)
    loads[1].wait()
    incoming = stg[plan[0, 1]].astype(f32)
    ag[GRAD, t] = rms_back(projected, incoming, gain(og, BACK)).astype(bf16)
    gather_start(GRAD)
    go[...] = sti[plan[0, 1]]
    fo[...] = stg[plan[0, 1]]
    ahead = (
        rcopy(go, bo.at[0], swap_s.at[2], swap_r.at[2], other),
        rcopy(fo, bo.at[1], swap_s.at[0], swap_r.at[0], other),
    )
    for copy in ahead:
        copy.start()
    kv_finish(FWD)
    attention(FWD)
    gather_relay(GRAD)
    loads[9].wait()
    scatter_first(FWD, out_product(FWD), rows_all(cx.at[FWD]))
    gather_finish(GRAD)

    og_rows = ag[GRAD].reshape(TOK, D)
    for h in range(2):
        cgs[h * TOK : (h + 1) * TOK] = dot_nt(
            og_rows, wo[BACK, h * HD : (h + 1) * HD, :]
        ).astype(bf16)
    q_gain, k_gain = gain(qg, BACK), gain(kg, BACK)

    R1, R2, R3, R4, R5, RR, RS = 0, 1, 2, 3, 4, 5, 6
    OWN, ONE, FOUR = 0, 1, 2

    def grad_block(i, d):
        if i == 0:
            return dot_tn(dss[:, d * TOK : (d + 1) * TOK], qs[BACK])
        return dot_tn(pl_s[:, d * TOK : (d + 1) * TOK], cgs[...])

    def g_send(d, e, se, device, cond, i):
        send(rcopy(gs.at[i, d - 1], gr.at[e, i], gss.at[se, i], gsr.at[e, i], device), cond)

    def g_add(e, k, cond, i):
        arrive(gr.at[e, i], gsr.at[e, i], cond)

        @pl.when(cond)
        def _():
            gacc[i, k] = gacc[i, k] + gr[e, i].astype(f32)

    def g_first(i):
        gs[i, 1] = grad_block(i, 2).astype(bf16)
        send(rcopy(gs.at[i, 1], grr.at[1], gss.at[1, i], gsr.at[RS, 0],
                   y_up if i else y_dn), hi & (z <= 1))
        g_send(2, R2, 0, z_dn, z >= 2, i)
        gs[i, 2] = grad_block(i, 3).astype(bf16)
        g_send(3, R3, 2, z_up, (z == 3) | hi, i)
        gacc[i, ONE] = grad_block(i, 1)
        gs[i, 0] = gacc[i, ONE].astype(bf16)
        g_send(1, R1, 3, z_dn, (z == 3) | (hi & (z == 0)), i)
        gacc[i, FOUR] = grad_block(i, 4)
        gacc[i, OWN] = grad_block(i, 0)

    def g_middle(i):
        g_add(R2, ONE, mid, i)

        @pl.when(mid)
        def _():
            gs[i, 0] = gacc[i, ONE].astype(bf16)
        g_send(1, R1, 3, z_dn, mid, i)

    def g_third(i):
        g_add(R3, FOUR, hi & (z >= 1), i)
        g_add(R1, FOUR, hi & (z == 3), i)
        gs[i, 3] = gacc[i, FOUR].astype(bf16)
        send(rcopy(gs.at[i, 3], grr.at[0], gss.at[4, i], gsr.at[RR, 0],
                   y_up if i else y_dn), hi)

    def g_relay(i, far):
        cond, device = (relay_v, y_up) if i else (relay_k, y_dn)
        if far:
            cond = cond & (z <= 1)
        buf, rsem = grr.at[far], gsr.at[RS if far else RR, 0]
        e = R5 if far else R4
        arrive(buf, rsem, cond)
        send(rcopy(buf, gr.at[e, i], gss.at[6 if far else 5, i], gsr.at[e, i], device), cond)

    def g_forward(i):
        cond = lo & (z <= 1)
        arrive(gr.at[R5, i], gsr.at[R5, i], cond)
        send(rcopy(gr.at[R5, i], gr.at[R5, i], gss.at[7, i], gsr.at[R5, i], z_op), cond)

    g_first(1)

    @pl.loop(0, 4)
    def _(ci):
        rows = pl.ds(pl.multiple_of(ci * 128, 128), 128)
        w = pw[rows, :]
        wg = dot_nt(cgs[rows, :], kvs[BACK, 1].reshape(5 * TOK, HD))
        delta = jnp.sum(w * wg, axis=-1, keepdims=True)
        dss[rows, :] = (w * (wg - delta) * (HD ** -0.5)).astype(bf16)

    g_first(0)
    g_middle(1)
    g_third(1)
    g_relay(1, 1)
    scatter_second(FWD)
    g_middle(0)
    g_third(0)
    g_relay(0, 1)

    for h in range(2):
        rows = slice(h * TOK, (h + 1) * TOK)
        dq = dot(dss[rows, :], kvs[BACK, 0].reshape(5 * TOK, HD))
        low = rms_back(
            qraw[rows], rope_back(dq, cos_ref[...], sin_ref[...]), q_gain
        ).astype(bf16)
        lq[:, :, h * HD : (h + 1) * HD] = low.reshape(8, ROWS, HD)
    query_low = rows_all(lq)[:, : 2 * HD]
    for n in range(NCH):
        hq[:, cols(n)] = dot_nt(query_low, wq[BACK, n * CW : (n + 1) * CW, :])

    g_forward(1)
    g_relay(1, 0)
    g_forward(0)
    g_relay(0, 0)
    for copy in ahead:
        copy.wait_send()
    scatter_relay(FWD)
    for i in (1, 0):
        g_add(R1, OWN, z < 3, i)
        g_add(R3, OWN, z == 0, i)
        g_add(R4, OWN, lo, i)
        g_add(R5, OWN, lo & (z >= 2), i)
    key_low = rms_back(
        kraw[...], rope_back(gacc[0, 0], cos_ref[...], sin_ref[...]), k_gain
    ).astype(bf16)
    lq[:, :, 2 * HD : 3 * HD] = key_low.reshape(8, ROWS, HD)
    lq[:, :, 3 * HD :] = gacc[1, 0].astype(bf16).reshape(8, ROWS, HD)

    for copy, _ in drains[before : before + NCH]:
        copy.wait_send()
    del drains[before : before + NCH]
    scatter_first(2, hidden_product, rows_all(lq))
    scatter_second(2)
    fwd_proj = scatter_finish(FWD)
    x_fwd = sti[plan[0, 0]].astype(f32)
    fo[...] = (x_fwd + fwd_proj * rms_of(fwd_proj) * gain(og, FWD)).astype(bf16)
    send(rcopy(fo, act_out, swap_s.at[1], swap_r.at[1], other))
    scatter_relay(2)
    for n in range(NCH):
        hidden = scatter_part(2, n)
        gb[0, :, cols(n)] = (hidden * ig[pl.ds(legs[BACK], 1), cols(n)]).astype(bf16)
        send(rcopy(gb.at[0, :, cols(n)], gb.at[1, :, cols(n)],
                   swap_s.at[3 + n], swap_r.at[3 + n], other))
    arrive(bo.at[0], swap_r.at[2])
    arrive(bo.at[1], swap_r.at[0])
    x_other = bo[0].astype(f32)
    scale = rms_of(x_other)
    for n in range(NCH):
        arrive(gb.at[1, :, cols(n)], swap_r.at[3 + n])
    g = gb[1].astype(f32)
    centred = g - x_other * (scale * scale * jnp.mean(g * x_other, axis=-1, keepdims=True))
    go[...] = (bo[1].astype(f32) + scale * centred).astype(bf16)
    final = pltpu.make_async_copy(go, grad_out, lsem.at[10])
    final.start()
    arrive(act_out, swap_r.at[1])
    for copy, cond in drains:
        when(cond, copy.wait_send)
    final.wait()


def per_device(
    stash_inputs, stash_grads, plan, query_weight, key_weight, value_weight, out_weight,
    input_gain, output_gain, query_gain, key_gain,
):
    hbm = pl.BlockSpec(memory_space=pl.ANY)
    smem = pl.BlockSpec(memory_space=pltpu.SMEM)
    V = pltpu.VMEM
    sem = pltpu.SemaphoreType.DMA
    act, grad = pl.pallas_call(
        kernel,
        out_shape=(jax.ShapeDtypeStruct((ROWS, D), bf16),) * 2,
        in_specs=[smem] + [hbm] * 10,
        out_specs=(hbm, hbm),
        scratch_shapes=[
            V((2, D, 2 * HD), bf16), V((2, D, HD), bf16), V((2, D, HD), bf16), V((2, 2 * HD, D), bf16),
            V((4, ROWS, D), bf16), V((4, ROWS, D), bf16),
            V((3, 8, ROWS, D), bf16),
            V((2, 2 * TOK, HD), bf16), V((2 * TOK, HD), f32), V((TOK, HD), f32),
            V((2, 2, 5, TOK, HD), bf16), V((2, 2, TOK, HD), bf16), V((2, TOK, HD), bf16),
            V((2, 8, ROWS, 2 * HD), bf16),
            V((2 * TOK, 5 * TOK), f32), V((2 * TOK, 5 * TOK), bf16), V((2 * TOK, 5 * TOK), bf16),
            V((2 * TOK, HD), bf16),
            V((2, 4, ROWS, D), bf16), V((3, 4, ROWS, D), bf16), V((3, 3, ROWS, D), bf16),
            V((3, 2, ROWS // 2, D), bf16), V((3, 2, ROWS, D), bf16), V((2, ROWS, D), f32),
            V((2, 4, TOK, HD), bf16), V((5, 2, TOK, HD), bf16), V((2, 3, TOK, HD), f32),
            V((8, ROWS, 4 * HD), bf16),
            V((ROWS, D), bf16), V((ROWS, D), bf16), V((TOK, HD // 2), f32), V((TOK, HD // 2), f32),
            V((2 * 4 * ROWS, D), f32), V((2, ROWS, D), bf16), V((2, ROWS, D), bf16),
            V((2, D), f32), V((2, D), f32), V((2, HD), f32), V((2, HD), f32),
            V((2 * TOK, 1), f32), V((2 * TOK, 1), f32),
            sem((15,)), sem((3, 13)), sem((3, 13)), sem((3, NCH, 7)), sem((3, NCH, 7)),
            sem((2, 10, 2)), sem((2, 8, 2)), sem((8, 2)), sem((7, 2)), sem((3 + NCH,)), sem((3 + NCH,)),
        ],
        compiler_params=pltpu.CompilerParams(
            collective_id=0, has_side_effects=True, vmem_limit_bytes=67043328
        ),
    )(
        plan, input_gain[0], output_gain[0], query_gain[0],
        key_gain[0], stash_inputs[0], stash_grads[0], query_weight[0], key_weight[0],
        value_weight[0], out_weight[0],
    )
    return act[None], grad[None]


def solution(mesh):
    return jax.shard_map(
        per_device,
        mesh=mesh,
        in_specs=(
            P("segment", None, ("ctx", "tp"), None),
            P("segment", None, ("ctx", "tp"), None),
            P("segment", None),
            P("segment", None, None, "tp"),
            P("segment", None, None, "tp"),
            P("segment", None, None, "tp"),
            P("segment", None, "tp", None),
            P("segment", None, None),
            P("segment", None, None),
            P("segment", None, None),
            P("segment", None, None),
        ),
        out_specs=(P("segment", ("ctx", "tp"), None), P("segment", ("ctx", "tp"), None)),
        check_vma=False,
    )
```

```python
import math

import jax
import jax.numpy as jnp
from jax import lax
from jax.experimental import pallas as pl
from jax.experimental.pallas import tpu as pltpu
from jax.sharding import PartitionSpec as P

WINDOW = 1024
epsilon = 1e-06
rope_base = 10000.0
masked_score = -1e30

D = 3840
ROWS = 32
TOK = 256
HD = 256
NCH = 5
CW = D // NCH
BACK, FWD, GRAD = 0, 1, 2
f32 = jnp.float32
bf16 = jnp.bfloat16
MESH = pl.DeviceIdType.MESH


def dot(a, b):
    return lax.dot_general(a, b, (((1,), (0,)), ((), ())), preferred_element_type=f32)


def dot_nt(a, b):
    return lax.dot_general(a, b, (((1,), (1,)), ((), ())), preferred_element_type=f32)


def dot_tn(a, b):
    return lax.dot_general(a, b, (((0,), (0,)), ((), ())), preferred_element_type=f32)


def rms_of(x):
    return lax.rsqrt(jnp.mean(x * x, axis=-1, keepdims=True) + epsilon)


def rms_back(x, grad, gain):
    g = grad * gain
    r = rms_of(x)
    return r * (g - x * (r * r * jnp.mean(g * x, axis=-1, keepdims=True)))


def rope(y, cosine, sine):
    a, b = y[:, : HD // 2], y[:, HD // 2 :]
    return jnp.concatenate([a * cosine - b * sine, b * cosine + a * sine], axis=-1)


def rope_back(g, cosine, sine):
    a, b = g[:, : HD // 2], g[:, HD // 2 :]
    return jnp.concatenate([a * cosine + b * sine, b * cosine - a * sine], axis=-1)


def kernel(
    plan, ig_h, og_h, qg_h, kg_h, si, sg, wq_h, wk_h, wv_h, wo_h,
    act_out, grad_out,
    wq, wk, wv, wo, sti, stg, ag, qs, qraw, kraw, kvs, kvrl, grr, cx, pw, pl_s, dss, cgs,
    ps, pr, sb, rl, fr, own, gs, gr, gacc, lq, fo, go, cos_ref, sin_ref, hq, bo, gb, ig, og, qg, kg, tops, sums,
    lsem, ags, agr, rss, rsr, kss, ksr, gss, gsr, swap_s, swap_r,
):
    s = lax.axis_index("segment")
    p = lax.axis_index("ctx")
    t = lax.axis_index("tp")
    yh, z = p // 4, p % 4
    y = 2 * yh + s
    x, c = t // 2, t % 2
    legs = (1 - s, s)

    def dev(s_=None, p_=None, t_=None):
        return {
            "segment": s if s_ is None else s_,
            "ctx": p if p_ is None else p_,
            "tp": t if t_ is None else t_,
        }

    t_r, t_l = ((x + 1) % 4) * 2 + c, ((x + 3) % 4) * 2 + c
    t_o = ((x + 2) % 4) * 2 + c
    t_p = 2 * x + 1 - c
    right, left, partner = dev(t_=t_r), dev(t_=t_l), dev(t_=t_p)
    z_up, z_dn = dev(p_=4 * yh + (z + 1) % 4), dev(p_=4 * yh + (z + 3) % 4)
    z_op = dev(p_=4 * yh + (z + 2) % 4)
    y_u, y_d = (y + 1) % 4, (y + 3) % 4
    y_up = dev(s_=y_u % 2, p_=(y_u // 2) * 4 + z)
    y_dn = dev(s_=y_d % 2, p_=(y_d // 2) * 4 + z)
    other = dev(s_=1 - s)

    barrier = pltpu.get_barrier_semaphore()
    for device in (right, left, partner, z_up, z_dn, z_op, y_up, y_dn):
        pl.semaphore_signal(barrier, inc=1, device_id=device, device_id_type=MESH)

    loads = [
        pltpu.make_async_copy(si, sti, lsem.at[0]),
        pltpu.make_async_copy(sg, stg, lsem.at[1]),
    ]
    for j in range(2):
        loads += [
            pltpu.make_async_copy(wq_h.at[legs[j]], wq.at[j], lsem.at[2 + 4 * j]),
            pltpu.make_async_copy(wk_h.at[legs[j]], wk.at[j], lsem.at[3 + 4 * j]),
            pltpu.make_async_copy(wv_h.at[legs[j]], wv.at[j], lsem.at[4 + 4 * j]),
            pltpu.make_async_copy(wo_h.at[legs[j]], wo.at[j], lsem.at[5 + 4 * j]),
        ]
    small = [
        pltpu.make_async_copy(src, dst, lsem.at[11 + k])
        for k, (src, dst) in enumerate(((ig_h, ig), (og_h, og), (qg_h, qg), (kg_h, kg)))
    ]
    for load in loads[:1] + small + loads[1:]:
        load.start()

    def gain(ref, j):
        return ref[pl.ds(legs[j], 1), :]

    def rcopy(src, dst, ssem, rsem, device):
        return pltpu.make_async_remote_copy(
            src_ref=src, dst_ref=dst, send_sem=ssem, recv_sem=rsem,
            device_id=device, device_id_type=MESH,
        )

    drains = []

    def when(cond, run):
        if cond is None:
            run()
        else:
            pl.when(cond)(run)

    def send(copy, cond=None):
        when(cond, copy.start)
        drains.append((copy, cond))

    def arrive(dst, rsem, cond=None):
        copy = rcopy(dst, dst, swap_s.at[0], rsem, partner)
        when(cond, copy.wait_recv)

    H0, H1 = pl.ds(0, ROWS // 2), pl.ds(ROWS // 2, ROWS // 2)
    halves = (H0, H1)

    def gather_start(j):
        blk = ag.at[j, t]
        send(rcopy(blk.at[H0], blk.at[H0], ags.at[j, 0], agr.at[j, 0], right))
        send(rcopy(blk.at[H1], blk.at[H1], ags.at[j, 1], agr.at[j, 1], left))
        send(rcopy(blk.at[H1], blk.at[H1], ags.at[j, 2], agr.at[j, 2], right))
        send(rcopy(blk.at[H0], blk.at[H0], ags.at[j, 3], agr.at[j, 3], left))
        send(rcopy(blk, blk, ags.at[j, 6], agr.at[j, 6], partner))

    def across(j, place, half, i):
        part = ag.at[j, place, halves[half]]
        send(rcopy(part, part, ags.at[j, i], agr.at[j, i], partner))

    def gather_relay(j):
        a = ag.at[j, t_l, H0]
        arrive(a, agr.at[j, 0])
        send(rcopy(a, a, ags.at[j, 4], agr.at[j, 4], right))
        b = ag.at[j, t_r, H1]
        arrive(b, agr.at[j, 1])
        send(rcopy(b, b, ags.at[j, 5], agr.at[j, 5], left))
        across(j, t_l, 0, 7)
        across(j, t_r, 1, 8)

    def gather_finish(j):
        arrive(ag.at[j, t_l, H1], agr.at[j, 2])
        across(j, t_l, 1, 9)
        arrive(ag.at[j, t_r, H0], agr.at[j, 3])
        across(j, t_r, 0, 10)
        arrive(ag.at[j, t_o, H0], agr.at[j, 4])
        across(j, t_o, 0, 11)
        arrive(ag.at[j, t_o, H1], agr.at[j, 5])
        across(j, t_o, 1, 12)
        u_r, u_l, u_o = t_r + 1 - 2 * c, t_l + 1 - 2 * c, t_o + 1 - 2 * c
        arrive(ag.at[j, t_p], agr.at[j, 6])
        arrive(ag.at[j, u_l, H0], agr.at[j, 7])
        arrive(ag.at[j, u_r, H1], agr.at[j, 8])
        arrive(ag.at[j, u_l, H1], agr.at[j, 9])
        arrive(ag.at[j, u_r, H0], agr.at[j, 10])
        arrive(ag.at[j, u_o, H0], agr.at[j, 11])
        arrive(ag.at[j, u_o, H1], agr.at[j, 12])

    def cols(n):
        return pl.ds(n * CW, CW)

    def rows_of(ref, parity):
        parts = [ref[2 * ((x + k) % 4) + parity] for k in range(4)]
        return jnp.concatenate(parts, axis=0)

    def rows_all(ref):
        return jnp.concatenate([rows_of(ref, 1 - c), rows_of(ref, c)], axis=0)

    def sent(r, first, last):
        for key in [k for k in flying if k[0] == r and first <= k[1] <= last]:
            for copy in flying.pop(key):
                copy.wait_send()

    flying = {}

    def send_sum(r, i, copy):
        copy.start()
        flying.setdefault((r, i), []).append(copy)

    def scatter_first(r, product, lhs, then=None):
        if r:
            sent(r - 1, 0, 0)
        for n in range(NCH):
            if then and n >= 3:
                then(n - 3)
            total = product(lhs, n)
            ps[:, :, cols(n)] = total[: 4 * ROWS].astype(bf16).reshape(4, ROWS, CW)
            send_sum(r, 0, rcopy(ps.at[:, :, cols(n)], pr.at[r, :, :, cols(n)],
                       rss.at[r, n, 0], rsr.at[r, n, 0], partner))
            hq[4 * ROWS :, cols(n)] = total[4 * ROWS :]

    def scatter_second(r, numbers=range(NCH)):
        if r == 2 and 0 in numbers:
            sent(0, 1, 6)
        for n in numbers:
            arrive(pr.at[r, :, :, cols(n)], rsr.at[r, n, 0])
            total = hq[4 * ROWS :, cols(n)].reshape(4, ROWS, CW) + pr[r, :, :, cols(n)].astype(f32)
            own[r % 2, :, cols(n)] = total[0]
            sb[r % 2, :, :, cols(n)] = total[1:].astype(bf16)
            send_sum(r, 1, rcopy(sb.at[r % 2, 1, H0, cols(n)], rl.at[r, 0, :, cols(n)],
                       rss.at[r, n, 1], rsr.at[r, n, 1], right))
            send_sum(r, 2, rcopy(sb.at[r % 2, 1, H1, cols(n)], rl.at[r, 1, :, cols(n)],
                       rss.at[r, n, 2], rsr.at[r, n, 2], left))
            send_sum(r, 3, rcopy(sb.at[r % 2, 0, H1, cols(n)], fr.at[r, 0, H1, cols(n)],
                       rss.at[r, n, 3], rsr.at[r, n, 3], right))
            send_sum(r, 4, rcopy(sb.at[r % 2, 2, H0, cols(n)], fr.at[r, 1, H0, cols(n)],
                       rss.at[r, n, 4], rsr.at[r, n, 4], left))

    def scatter_relay(r):
        for n in range(NCH):
            arrive(rl.at[r, 0, :, cols(n)], rsr.at[r, n, 1])
            sb[r % 2, 0, H0, cols(n)] = (
                sb[r % 2, 0, H0, cols(n)].astype(f32) + rl[r, 0, :, cols(n)].astype(f32)
            ).astype(bf16)
            send_sum(r, 5, rcopy(sb.at[r % 2, 0, H0, cols(n)], fr.at[r, 0, H0, cols(n)],
                       rss.at[r, n, 5], rsr.at[r, n, 5], right))
            arrive(rl.at[r, 1, :, cols(n)], rsr.at[r, n, 2])
            sb[r % 2, 2, H1, cols(n)] = (
                sb[r % 2, 2, H1, cols(n)].astype(f32) + rl[r, 1, :, cols(n)].astype(f32)
            ).astype(bf16)
            send_sum(r, 6, rcopy(sb.at[r % 2, 2, H1, cols(n)], fr.at[r, 1, H1, cols(n)],
                       rss.at[r, n, 6], rsr.at[r, n, 6], left))

    def scatter_part(r, n):
        arrive(fr.at[r, 0, H1, cols(n)], rsr.at[r, n, 3])
        arrive(fr.at[r, 1, H0, cols(n)], rsr.at[r, n, 4])
        arrive(fr.at[r, 0, H0, cols(n)], rsr.at[r, n, 5])
        arrive(fr.at[r, 1, H1, cols(n)], rsr.at[r, n, 6])
        return own[r % 2, :, cols(n)] + (
            fr[r, 0, :, cols(n)].astype(f32) + fr[r, 1, :, cols(n)].astype(f32)
        )

    def scatter_finish(r):
        return jnp.concatenate([scatter_part(r, n) for n in range(NCH)], axis=-1)

    hi, lo = yh == 1, yh == 0
    mid = (z == 1) | (z == 2)

    relay_k = (y == 1) | (y == 2)
    relay_v = (y == 0) | (y == 3)

    TH = (pl.ds(0, TOK // 2), pl.ds(TOK // 2, TOK // 2))

    def kv_near(j):
        for i in range(2):
            o = kvs.at[j, i, 0]
            send(rcopy(o, kvs.at[j, i, 1], kss.at[j, 1, i], ksr.at[j, 1, i], z_up), z < 3)
            send(rcopy(o, kvs.at[j, i, 3], kss.at[j, 3, i], ksr.at[j, 3, i], z_dn), z == 0)
            send(rcopy(o, kvs.at[j, i, 2], kss.at[j, 5, i], ksr.at[j, 2, i], z_op), lo & (z == 3))
            send(rcopy(o, kvs.at[j, i, 3], kss.at[j, 3, i], ksr.at[j, 3, i], z_dn), lo & (z == 1))

    def kv_cross(j):
        k, v = kvs.at[j, 0, 0], kvs.at[j, 1, 0]
        send(rcopy(k, kvrl.at[j, 0], kss.at[j, 6, 0], ksr.at[j, 0, 0], y_up), lo)
        send(rcopy(v, kvrl.at[j, 0], kss.at[j, 6, 1], ksr.at[j, 0, 0], y_dn), lo)

    def kv_relay(j):
        b = kvrl.at[j, 0]
        arrive(b, ksr.at[j, 0, 0])
        send(rcopy(b, kvs.at[j, 0, 4], kss.at[j, 4, 0], ksr.at[j, 4, 0], y_up), relay_k)
        send(rcopy(b, kvs.at[j, 1, 4], kss.at[j, 4, 1], ksr.at[j, 4, 1], y_dn), relay_v)

    def kv_second(j):
        low = z <= 1
        far = jnp.maximum(3 - z, 2)
        for i in range(2):
            b1, b2, b4 = (kvs.at[j, i, d] for d in (1, far, 4))
            arrive(b2, ksr.at[j, far, i], lo & low)
            send(rcopy(b2, kvrl.at[j, 1], kss.at[j, 0, i], ksr.at[j, 5, 0],
                       y_dn if i else y_up), lo & low)
            arrive(b1, ksr.at[j, 1, i], mid)
            send(rcopy(b1, kvs.at[j, i, 2], kss.at[j, 2, i], ksr.at[j, 2, i], z_up), mid)
            arrive(b4, ksr.at[j, 4, i], hi)
            send(rcopy(b4, kvs.at[j, i, 3], kss.at[j, 3, i], ksr.at[j, 3, i], z_dn), hi & (z == 3))
            for q in range(2):
                send(rcopy(b4.at[TH[q]], kvs.at[j, i, 3, TH[q]], kss.at[j, 8 + i, q],
                           ksr.at[j, 6 + i, q], z_dn), hi & (z == 2))
            send(rcopy(b4, kvs.at[j, i, 1], kss.at[j, 1, i], ksr.at[j, 1, i], z_up), hi & (z == 3))

    def kv_third(j):
        low = z <= 1
        b = kvrl.at[j, 1]
        arrive(b, ksr.at[j, 5, 0], low)
        far = jnp.maximum(3 - z, 2)
        send(rcopy(b, kvs.at[j, 0, far], kss.at[j, 7, 0], ksr.at[j, far, 0], y_up), low & relay_k)
        send(rcopy(b, kvs.at[j, 1, far], kss.at[j, 7, 1], ksr.at[j, far, 1], y_dn), low & relay_v)

    def kv_fourth(j):
        cond = hi & (z == 1)
        for i in range(2):
            for q in range(2):
                b3 = kvs.at[j, i, 3, TH[q]]
                arrive(b3, ksr.at[j, 6 + i, q], cond)
                send(rcopy(b3, kvs.at[j, i, 2, TH[q]], kss.at[j, 10 + i, q],
                           ksr.at[j, 8 + i, q], z_dn), cond)

    def kv_near_in(j):
        for i in range(2):
            arrive(kvs.at[j, i, 1], ksr.at[j, 1, i], (z == 3) | (hi & (z == 0)))
            arrive(kvs.at[j, i, 3], ksr.at[j, 3, i], (z == 3) | (hi & (z != 1)))

    def kv_far_in(j):
        four = hi & (z == 0)
        for i in range(2):
            arrive(kvs.at[j, i, 2], ksr.at[j, 2, i], (z >= 2) | (hi & (z == 1)))
            for q in range(2):
                arrive(kvs.at[j, i, 2, TH[q]], ksr.at[j, 8 + i, q], four)

    def kv_finish(j):
        kv_near_in(j)
        kv_far_in(j)

    def project(j):
        cosine, sine = cos_ref[...], sin_ref[...]
        for load in loads[2 + 4 * j : 5 + 4 * j]:
            load.wait()
        xn = ag[j].reshape(TOK, D)
        q_gain, k_gain = gain(qg, j), gain(kg, j)
        kr = dot(xn, wk[j])
        kvs[j, 0, 0] = rope(kr * rms_of(kr) * k_gain, cosine, sine).astype(bf16)
        kvs[j, 1, 0] = dot(xn, wv[j]).astype(bf16)
        if j == BACK:
            kv_cross(j)
        kv_near(j)
        if j == BACK:
            kraw[...] = kr
        for h in range(2):
            qr = dot(xn, wq[j, :, h * HD : (h + 1) * HD])
            query = rope(qr * rms_of(qr) * q_gain, cosine, sine).astype(bf16)
            qs[j, h * TOK : (h + 1) * TOK] = query * jnp.asarray(HD ** -0.5, bf16)
            if j == BACK:
                qraw[h * TOK : (h + 1) * TOK] = qr

    def score(j, ci, d):
        sc = dot_nt(qs[j, chunk_rows(ci), :], kvs[j, 0, d])
        if d in (0, 4):
            ii = lax.broadcasted_iota(jnp.int32, (TOK, TOK), 0)
            ahead_by = ii - lax.broadcasted_iota(jnp.int32, (TOK, TOK), 1)
            if d == 0:
                return jnp.where(ahead_by >= 0, sc, masked_score)
            return jnp.where(ahead_by < jnp.where(p >= 4, 0, -TOK), sc, masked_score)
        return sc + jnp.where(p >= d, 0.0, masked_score)

    def top_of(scs):
        top = jnp.max(scs[0], axis=-1, keepdims=True)
        for sc in scs[1:]:
            top = jnp.maximum(top, jnp.max(sc, axis=-1, keepdims=True))
        return top

    def sum_of(es):
        total = es[0]
        for e in es[1:]:
            total = total + e
        return jnp.sum(total, axis=-1, keepdims=True)

    def chunk_rows(ci):
        return slice(ci * TOK, (ci + 1) * TOK)

    def weigh(j, ci, low):
        out = dot(low, kvs[j, 1].reshape(5 * TOK, HD)).astype(bf16)
        cx[j, :, :, ci * HD : (ci + 1) * HD] = out.reshape(8, ROWS, HD)

    near_blocks = (0, 1, 3, 4)

    def block_cols(d):
        return slice(d * TOK, (d + 1) * TOK)

    def attend_near():
        for ci in range(2):
            rows = chunk_rows(ci)
            scs = [score(BACK, ci, d) for d in near_blocks]
            top = top_of(scs)
            es = [jnp.exp(sc - top) for sc in scs]
            for d, e in zip(near_blocks, es):
                pw[rows, block_cols(d)] = e
            tops[rows, :] = top
            sums[rows, :] = sum_of(es)

    def attend_far():
        for ci in range(2):
            rows = chunk_rows(ci)
            sc = score(BACK, ci, 2)
            top = jnp.maximum(tops[rows, :], jnp.max(sc, axis=-1, keepdims=True))
            e = jnp.exp(sc - top)
            pw[rows, block_cols(2)] = e
            near = jnp.exp(tops[rows, :] - top)
            far = 1.0 / (sums[rows, :] * near + jnp.sum(e, axis=-1, keepdims=True))
            near = near * far
            tops[rows, :] = near
            sums[rows, :] = far
            lows = []
            for d in range(5):
                w = e * far if d == 2 else pw[rows, block_cols(d)] * near
                lows.append(w.astype(bf16))
                pl_s[rows, block_cols(d)] = lows[d]
            weigh(BACK, ci, jnp.concatenate(lows, axis=-1))

    def attention(j):
        for ci in range(2):
            scs = [score(j, ci, d) for d in range(5)]
            top = top_of(scs)
            es = [jnp.exp(sc - top) for sc in scs]
            inverse = 1.0 / sum_of(es)
            weigh(j, ci, jnp.concatenate([(e * inverse).astype(bf16) for e in es], axis=-1))

    def out_product(j):
        return lambda lhs, n: dot(lhs, wo[j, :, n * CW : (n + 1) * CW])

    def hidden_product(lhs, n):
        w_rows = slice(n * CW, (n + 1) * CW)
        total = hq[:, cols(n)] + dot_nt(lhs[:, 2 * HD : 3 * HD], wk[BACK, w_rows, :])
        return total + dot_nt(lhs[:, 3 * HD :], wv[BACK, w_rows, :])

    loads[0].wait()
    for load in small:
        load.wait()
    x_back = sti[plan[0, 1]].astype(f32)
    ag[BACK, t] = (x_back * rms_of(x_back) * gain(ig, BACK)).astype(bf16)
    pl.semaphore_wait(barrier, 8)
    gather_start(BACK)
    x_fwd = sti[plan[0, 0]].astype(f32)
    ag[FWD, t] = (x_fwd * rms_of(x_fwd) * gain(ig, FWD)).astype(bf16)
    for j in range(2):
        for d in range(1, 5):
            @pl.when((d > p) & (d + p != 3))
            def _():
                for i in range(2):
                    kvs[j, i, d] = jnp.zeros((TOK, HD), bf16)
    angles = (p * TOK + lax.broadcasted_iota(jnp.int32, (TOK, HD // 2), 0)).astype(f32)
    pair = lax.broadcasted_iota(jnp.int32, (1, HD // 2), 1).astype(f32)
    angles = angles * jnp.exp(pair * (-2.0 * math.log(rope_base) / HD))
    cos_ref[...] = jnp.cos(angles)
    sin_ref[...] = jnp.sin(angles)
    gather_relay(BACK)
    gather_start(FWD)
    gather_finish(BACK)
    project(BACK)
    gather_relay(FWD)
    kv_relay(BACK)
    gather_finish(FWD)
    kv_second(BACK)
    project(FWD)
    kv_third(BACK)
    kv_cross(FWD)
    kv_fourth(BACK)
    kv_near_in(BACK)
    attend_near()
    kv_relay(FWD)
    kv_far_in(BACK)
    attend_far()
    loads[5].wait()
    scatter_first(BACK, out_product(BACK), rows_all(cx.at[BACK]),
                  lambda n: scatter_second(BACK, (n,)))
    scatter_second(BACK, range(NCH - 3, NCH))
    kv_second(FWD)
    scatter_relay(BACK)
    kv_third(FWD)
    kv_fourth(FWD)
    projected = scatter_finish(BACK)
    loads[1].wait()
    incoming = stg[plan[0, 1]].astype(f32)
    ag[GRAD, t] = rms_back(projected, incoming, gain(og, BACK)).astype(bf16)
    gather_start(GRAD)
    go[...] = sti[plan[0, 1]]
    fo[...] = stg[plan[0, 1]]
    ahead = (
        rcopy(go, bo.at[0], swap_s.at[2], swap_r.at[2], other),
        rcopy(fo, bo.at[1], swap_s.at[0], swap_r.at[0], other),
    )
    for copy in ahead:
        copy.start()
    kv_finish(FWD)
    attention(FWD)
    gather_relay(GRAD)
    loads[9].wait()
    scatter_first(FWD, out_product(FWD), rows_all(cx.at[FWD]))
    gather_finish(GRAD)

    og_rows = ag[GRAD].reshape(TOK, D)
    for h in range(2):
        cgs[h * TOK : (h + 1) * TOK] = dot_nt(
            og_rows, wo[BACK, h * HD : (h + 1) * HD, :]
        ).astype(bf16)
    q_gain, k_gain = gain(qg, BACK), gain(kg, BACK)

    R1, R2, R3, R4, R5, RR, RS = 0, 1, 2, 3, 4, 5, 6
    OWN, ONE, FOUR = 0, 1, 2

    def grad_block(i, d):
        if i == 0:
            return dot_tn(dss[:, d * TOK : (d + 1) * TOK], qs[BACK])
        return dot_tn(pl_s[:, d * TOK : (d + 1) * TOK], cgs[...])

    def g_send(d, e, se, device, cond, i):
        send(rcopy(gs.at[i, d - 1], gr.at[e, i], gss.at[se, i], gsr.at[e, i], device), cond)

    def g_add(e, k, cond, i):
        arrive(gr.at[e, i], gsr.at[e, i], cond)

        @pl.when(cond)
        def _():
            gacc[i, k] = gacc[i, k] + gr[e, i].astype(f32)

    def g_first(i):
        gs[i, 1] = grad_block(i, 2).astype(bf16)
        send(rcopy(gs.at[i, 1], grr.at[1], gss.at[1, i], gsr.at[RS, 0],
                   y_up if i else y_dn), hi & (z <= 1))
        g_send(2, R2, 0, z_dn, z >= 2, i)
        gs[i, 2] = grad_block(i, 3).astype(bf16)
        g_send(3, R3, 2, z_up, (z == 3) | hi, i)
        gacc[i, ONE] = grad_block(i, 1)
        gs[i, 0] = gacc[i, ONE].astype(bf16)
        g_send(1, R1, 3, z_dn, (z == 3) | (hi & (z == 0)), i)
        gacc[i, FOUR] = grad_block(i, 4)
        gacc[i, OWN] = grad_block(i, 0)

    def g_middle(i):
        g_add(R2, ONE, mid, i)

        @pl.when(mid)
        def _():
            gs[i, 0] = gacc[i, ONE].astype(bf16)
        g_send(1, R1, 3, z_dn, mid, i)

    def g_third(i):
        g_add(R3, FOUR, hi & (z >= 1), i)
        g_add(R1, FOUR, hi & (z == 3), i)
        gs[i, 3] = gacc[i, FOUR].astype(bf16)
        send(rcopy(gs.at[i, 3], grr.at[0], gss.at[4, i], gsr.at[RR, 0],
                   y_up if i else y_dn), hi)

    def g_relay(i, far):
        cond, device = (relay_v, y_up) if i else (relay_k, y_dn)
        if far:
            cond = cond & (z <= 1)
        buf, rsem = grr.at[far], gsr.at[RS if far else RR, 0]
        e = R5 if far else R4
        arrive(buf, rsem, cond)
        send(rcopy(buf, gr.at[e, i], gss.at[6 if far else 5, i], gsr.at[e, i], device), cond)

    def g_forward(i):
        cond = lo & (z <= 1)
        arrive(gr.at[R5, i], gsr.at[R5, i], cond)
        send(rcopy(gr.at[R5, i], gr.at[R5, i], gss.at[7, i], gsr.at[R5, i], z_op), cond)

    g_first(1)

    for ci in range(2):
        rows = chunk_rows(ci)
        near, far = tops[rows, :], sums[rows, :]
        ws = [pw[rows, block_cols(d)] * (far if d == 2 else near) for d in range(5)]
        wgs = [dot_nt(cgs[rows, :], kvs[BACK, 1, d]) for d in range(5)]
        delta = sum_of([w * wg for w, wg in zip(ws, wgs)])
        for d in range(5):
            dss[rows, block_cols(d)] = (ws[d] * (wgs[d] - delta)).astype(bf16)

    g_first(0)
    g_middle(1)
    g_third(1)
    g_relay(1, 1)
    scatter_second(FWD)
    g_middle(0)
    g_third(0)
    g_relay(0, 1)

    for h in range(2):
        rows = slice(h * TOK, (h + 1) * TOK)
        dq = dot(dss[rows, :], kvs[BACK, 0].reshape(5 * TOK, HD)) * (HD ** -0.5)
        low = rms_back(
            qraw[rows], rope_back(dq, cos_ref[...], sin_ref[...]), q_gain
        ).astype(bf16)
        lq[:, :, h * HD : (h + 1) * HD] = low.reshape(8, ROWS, HD)
    query_low = rows_all(lq)[:, : 2 * HD]
    for n in range(NCH):
        hq[:, cols(n)] = dot_nt(query_low, wq[BACK, n * CW : (n + 1) * CW, :])

    g_forward(1)
    g_relay(1, 0)
    g_forward(0)
    g_relay(0, 0)
    for copy in ahead:
        copy.wait_send()
    scatter_relay(FWD)
    for i in (1, 0):
        g_add(R1, OWN, z < 3, i)
        g_add(R3, OWN, z == 0, i)
        g_add(R4, OWN, lo, i)
        g_add(R5, OWN, lo & (z >= 2), i)
    key_low = rms_back(
        kraw[...], rope_back(gacc[0, 0], cos_ref[...], sin_ref[...]), k_gain
    ).astype(bf16)
    lq[:, :, 2 * HD : 3 * HD] = key_low.reshape(8, ROWS, HD)
    lq[:, :, 3 * HD :] = gacc[1, 0].astype(bf16).reshape(8, ROWS, HD)

    scatter_first(2, hidden_product, rows_all(lq), lambda n: scatter_second(2, (n,)))
    scatter_second(2, range(NCH - 3, NCH))
    fwd_proj = scatter_finish(FWD)
    x_fwd = sti[plan[0, 0]].astype(f32)
    fo[...] = (x_fwd + fwd_proj * rms_of(fwd_proj) * gain(og, FWD)).astype(bf16)
    send(rcopy(fo, act_out, swap_s.at[1], swap_r.at[1], other))
    scatter_relay(2)
    for n in range(NCH):
        hidden = scatter_part(2, n)
        gb[0, :, cols(n)] = (hidden * ig[pl.ds(legs[BACK], 1), cols(n)]).astype(bf16)
        send(rcopy(gb.at[0, :, cols(n)], gb.at[1, :, cols(n)],
                   swap_s.at[3 + n], swap_r.at[3 + n], other))
    arrive(bo.at[0], swap_r.at[2])
    arrive(bo.at[1], swap_r.at[0])
    x_other = bo[0].astype(f32)
    scale = rms_of(x_other)
    for n in range(NCH):
        arrive(gb.at[1, :, cols(n)], swap_r.at[3 + n])
    g = gb[1].astype(f32)
    centred = g - x_other * (scale * scale * jnp.mean(g * x_other, axis=-1, keepdims=True))
    go[...] = (bo[1].astype(f32) + scale * centred).astype(bf16)
    final = pltpu.make_async_copy(go, grad_out, lsem.at[10])
    final.start()
    arrive(act_out, swap_r.at[1])
    for copy, cond in drains:
        when(cond, copy.wait_send)
    for r in range(3):
        sent(r, 0, 6)
    final.wait()


def hand_on(act_in, grad_in, act_out, grad_out, held, lsem):
    pairs = ((act_in, act_out), (grad_in, grad_out))
    ins = [pltpu.make_async_copy(src, held.at[k], lsem.at[k]) for k, (src, _) in enumerate(pairs)]
    outs = [
        pltpu.make_async_copy(held.at[k], dst, lsem.at[2 + k]) for k, (_, dst) in enumerate(pairs)
    ]
    for copy in ins:
        copy.start()
    for taken, given in zip(ins, outs):
        taken.wait()
        given.start()
    for copy in outs:
        copy.wait()


def per_device(
    stash_inputs, stash_grads, plan, query_weight, key_weight, value_weight, out_weight,
    input_gain, output_gain, query_gain, key_gain,
):
    hbm = pl.BlockSpec(memory_space=pl.ANY)
    smem = pl.BlockSpec(memory_space=pltpu.SMEM)
    V = pltpu.VMEM
    sem = pltpu.SemaphoreType.DMA
    act, grad = pl.pallas_call(
        kernel,
        out_shape=(jax.ShapeDtypeStruct((ROWS, D), bf16),) * 2,
        in_specs=[smem] + [hbm] * 10,
        out_specs=(hbm, hbm),
        scratch_shapes=[
            V((2, D, 2 * HD), bf16), V((2, D, HD), bf16), V((2, D, HD), bf16), V((2, 2 * HD, D), bf16),
            V((4, ROWS, D), bf16), V((4, ROWS, D), bf16),
            V((3, 8, ROWS, D), bf16),
            V((2, 2 * TOK, HD), bf16), V((2 * TOK, HD), f32), V((TOK, HD), f32),
            V((2, 2, 5, TOK, HD), bf16), V((2, 2, TOK, HD), bf16), V((2, TOK, HD), bf16),
            V((2, 8, ROWS, 2 * HD), bf16),
            V((2 * TOK, 5 * TOK), f32), V((2 * TOK, 5 * TOK), bf16), V((2 * TOK, 5 * TOK), bf16),
            V((2 * TOK, HD), bf16),
            V((4, ROWS, D), bf16), V((3, 4, ROWS, D), bf16), V((2, 3, ROWS, D), bf16),
            V((3, 2, ROWS // 2, D), bf16), V((3, 2, ROWS, D), bf16), V((2, ROWS, D), f32),
            V((2, 4, TOK, HD), bf16), V((5, 2, TOK, HD), bf16), V((2, 3, TOK, HD), f32),
            V((8, ROWS, 4 * HD), bf16),
            V((ROWS, D), bf16), V((ROWS, D), bf16), V((TOK, HD // 2), f32), V((TOK, HD // 2), f32),
            V((2 * 4 * ROWS, D), f32), V((2, ROWS, D), bf16), V((2, ROWS, D), bf16),
            V((2, D), f32), V((2, D), f32), V((2, HD), f32), V((2, HD), f32),
            V((2 * TOK, 1), f32), V((2 * TOK, 1), f32),
            sem((15,)), sem((3, 13)), sem((3, 13)), sem((3, NCH, 7)), sem((3, NCH, 7)),
            sem((2, 12, 2)), sem((2, 10, 2)), sem((8, 2)), sem((7, 2)), sem((3 + NCH,)), sem((3 + NCH,)),
        ],
        compiler_params=pltpu.CompilerParams(
            collective_id=0, has_side_effects=True, vmem_limit_bytes=67043328
        ),
    )(
        plan, input_gain[0], output_gain[0], query_gain[0],
        key_gain[0], stash_inputs[0], stash_grads[0], query_weight[0], key_weight[0],
        value_weight[0], out_weight[0],
    )
    act, grad = pl.pallas_call(
        hand_on,
        out_shape=(jax.ShapeDtypeStruct((ROWS, D), bf16),) * 2,
        in_specs=[hbm, hbm],
        out_specs=(hbm, hbm),
        scratch_shapes=[V((2, ROWS, D), bf16), sem((4,))],
    )(act, grad)
    return act[None], grad[None]


def solution(mesh):
    return jax.shard_map(
        per_device,
        mesh=mesh,
        in_specs=(
            P("segment", None, ("ctx", "tp"), None),
            P("segment", None, ("ctx", "tp"), None),
            P("segment", None),
            P("segment", None, None, "tp"),
            P("segment", None, None, "tp"),
            P("segment", None, None, "tp"),
            P("segment", None, "tp", None),
            P("segment", None, None),
            P("segment", None, None),
            P("segment", None, None),
            P("segment", None, None),
        ),
        out_specs=(P("segment", ("ctx", "tp"), None), P("segment", ("ctx", "tp"), None)),
        check_vma=False,
    )
```

```python
import math

import jax
import jax.numpy as jnp
from jax import lax
from jax.experimental import pallas as pl
from jax.experimental.pallas import tpu as pltpu
from jax.sharding import PartitionSpec as P

WINDOW = 1024
epsilon = 1e-06
rope_base = 10000.0
masked_score = -1e30

D = 3840
ROWS = 32
TOK = 256
HD = 256
NCH = 5
CW = D // NCH
BACK, FWD, GRAD = 0, 1, 2
f32 = jnp.float32
bf16 = jnp.bfloat16
MESH = pl.DeviceIdType.MESH


def dot(a, b):
    return lax.dot_general(a, b, (((1,), (0,)), ((), ())), preferred_element_type=f32)


def dot_nt(a, b):
    return lax.dot_general(a, b, (((1,), (1,)), ((), ())), preferred_element_type=f32)


def dot_tn(a, b):
    return lax.dot_general(a, b, (((0,), (0,)), ((), ())), preferred_element_type=f32)


def rms_of(x):
    return lax.rsqrt(jnp.mean(x * x, axis=-1, keepdims=True) + epsilon)


def rms_back(x, grad, gain):
    g = grad * gain
    r = rms_of(x)
    return r * (g - x * (r * r * jnp.mean(g * x, axis=-1, keepdims=True)))


def rope(y, cosine, sine):
    a, b = y[:, : HD // 2], y[:, HD // 2 :]
    return jnp.concatenate([a * cosine - b * sine, b * cosine + a * sine], axis=-1)


def rope_back(g, cosine, sine):
    a, b = g[:, : HD // 2], g[:, HD // 2 :]
    return jnp.concatenate([a * cosine + b * sine, b * cosine - a * sine], axis=-1)


def kernel(
    plan, ig_h, og_h, qg_h, kg_h, si, sg, wq_h, wk_h, wv_h, wo_h,
    act_out, grad_out,
    wq, wk, wv, wo, sti, stg, ag, qs, qraw, kraw, kvs, kvrl, grr, cx, pw, pl_s, dss, cgs,
    ps, pr, sb, rl, fr, own, gs, gr, gacc, lq, fo, go, cos_ref, sin_ref, hq, bo, gb, ig, og, qg, kg, tops, sums,
    lsem, ags, agr, rss, rsr, kss, ksr, gss, gsr, gsc, gcr, gsx, gsh, gsy, gsz, swap_s, swap_r,
):
    s = lax.axis_index("segment")
    p = lax.axis_index("ctx")
    t = lax.axis_index("tp")
    yh, z = p // 4, p % 4
    y = 2 * yh + s
    x, c = t // 2, t % 2
    legs = (1 - s, s)

    def dev(s_=None, p_=None, t_=None):
        return {
            "segment": s if s_ is None else s_,
            "ctx": p if p_ is None else p_,
            "tp": t if t_ is None else t_,
        }

    t_r, t_l = ((x + 1) % 4) * 2 + c, ((x + 3) % 4) * 2 + c
    t_o = ((x + 2) % 4) * 2 + c
    t_p = 2 * x + 1 - c
    right, left, partner = dev(t_=t_r), dev(t_=t_l), dev(t_=t_p)
    z_up, z_dn = dev(p_=4 * yh + (z + 1) % 4), dev(p_=4 * yh + (z + 3) % 4)
    z_op = dev(p_=4 * yh + (z + 2) % 4)
    y_u, y_d = (y + 1) % 4, (y + 3) % 4
    y_up = dev(s_=y_u % 2, p_=(y_u // 2) * 4 + z)
    y_dn = dev(s_=y_d % 2, p_=(y_d // 2) * 4 + z)
    other = dev(s_=1 - s)

    barrier = pltpu.get_barrier_semaphore()
    for device in (right, left, partner, z_up, z_dn, z_op, y_up, y_dn):
        pl.semaphore_signal(barrier, inc=1, device_id=device, device_id_type=MESH)

    loads = [
        pltpu.make_async_copy(si, sti, lsem.at[0]),
        pltpu.make_async_copy(sg, stg, lsem.at[1]),
    ]
    for j in range(2):
        loads += [
            pltpu.make_async_copy(wq_h.at[legs[j]], wq.at[j], lsem.at[2 + 4 * j]),
            pltpu.make_async_copy(wk_h.at[legs[j]], wk.at[j], lsem.at[3 + 4 * j]),
            pltpu.make_async_copy(wv_h.at[legs[j]], wv.at[j], lsem.at[4 + 4 * j]),
            pltpu.make_async_copy(wo_h.at[legs[j]], wo.at[j], lsem.at[5 + 4 * j]),
        ]
    small = [
        pltpu.make_async_copy(src, dst, lsem.at[11 + k])
        for k, (src, dst) in enumerate(((ig_h, ig), (og_h, og), (qg_h, qg), (kg_h, kg)))
    ]
    for load in loads[:1] + small + loads[1:]:
        load.start()

    def gain(ref, j):
        return ref[pl.ds(legs[j], 1), :]

    def rcopy(src, dst, ssem, rsem, device):
        return pltpu.make_async_remote_copy(
            src_ref=src, dst_ref=dst, send_sem=ssem, recv_sem=rsem,
            device_id=device, device_id_type=MESH,
        )

    drains = []

    def when(cond, run):
        if cond is None:
            run()
        else:
            pl.when(cond)(run)

    def send(copy, cond=None):
        when(cond, copy.start)
        drains.append((copy, cond))

    def launch(copy, cond=None):
        when(cond, copy.start)

    def owe(ref, ssem, cond=None):
        drains.append((rcopy(ref, ref, ssem, swap_r.at[0], partner), cond))

    def flush(first, last):
        groups = {}
        for copy, cond in drains[first:last]:
            groups.setdefault(id(cond), (cond, []))[1].append(copy)
        for cond, copies in groups.values():
            def run(copies=copies):
                for copy in copies:
                    copy.wait_send()
            when(cond, run)
        del drains[first:last]

    def arrive(dst, rsem, cond=None):
        copy = rcopy(dst, dst, swap_s.at[0], rsem, partner)
        when(cond, copy.wait_recv)

    H0, H1 = pl.ds(0, ROWS // 2), pl.ds(ROWS // 2, ROWS // 2)
    halves = (H0, H1)

    def gather_start(j):
        blk = ag.at[j, t]
        launch(rcopy(blk.at[H0], blk.at[H0], ags.at[j], agr.at[j, 0], right))
        launch(rcopy(blk.at[H1], blk.at[H1], ags.at[j], agr.at[j, 1], left))
        launch(rcopy(blk.at[H1], blk.at[H1], ags.at[j], agr.at[j, 2], right))
        launch(rcopy(blk.at[H0], blk.at[H0], ags.at[j], agr.at[j, 3], left))
        launch(rcopy(blk, blk, ags.at[j], agr.at[j, 6], partner))

    def across(j, place, half):
        part = ag.at[j, place, halves[half]]
        launch(rcopy(part, part, ags.at[j], agr.at[j, 6], partner))

    def gather_relay(j):
        a = ag.at[j, t_l, H0]
        arrive(a, agr.at[j, 0])
        launch(rcopy(a, a, ags.at[j], agr.at[j, 4], right))
        b = ag.at[j, t_r, H1]
        arrive(b, agr.at[j, 1])
        launch(rcopy(b, b, ags.at[j], agr.at[j, 5], left))
        across(j, t_l, 0)
        across(j, t_r, 1)

    def gather_finish(j):
        arrive(ag.at[j, t_l, H1], agr.at[j, 2])
        across(j, t_l, 1)
        arrive(ag.at[j, t_r, H0], agr.at[j, 3])
        across(j, t_r, 0)
        arrive(ag.at[j, t_o, H0], agr.at[j, 4])
        across(j, t_o, 0)
        arrive(ag.at[j, t_o, H1], agr.at[j, 5])
        across(j, t_o, 1)
        arrive(ag.at[j, pl.ds(0, 4)], agr.at[j, 6])
        owe(ag.at[j, pl.ds(0, 7)], ags.at[j])

    def cols(n):
        return pl.ds(n * CW, CW)

    def rows_of(ref, parity):
        parts = [ref[2 * ((x + k) % 4) + parity] for k in range(4)]
        return jnp.concatenate(parts, axis=0)

    def rows_all(ref):
        return jnp.concatenate([rows_of(ref, 1 - c), rows_of(ref, c)], axis=0)

    def sent(r, first, last):
        b = r % 2
        parts = (
            ps, sb.at[b, 1, H0], sb.at[b, 1, H1], sb.at[b, 0, H1],
            sb.at[b, 2, H0], sb.at[b, 0, H0], sb.at[b, 2, H1],
        )
        for i in range(first, last + 1):
            if (r, i) in flying:
                flying.remove((r, i))
                rcopy(parts[i], parts[i], rss.at[r, i], swap_r.at[0], partner).wait_send()

    flying = set()

    def send_sum(r, i, copy):
        copy.start()
        flying.add((r, i))

    def scatter_first(r, product, lhs, then=None):
        if r:
            sent(r - 1, 0, 0)
        for n in range(NCH):
            if then and n >= 3:
                then(n - 3)
            total = product(lhs, n)
            ps[:, :, cols(n)] = total[: 4 * ROWS].astype(bf16).reshape(4, ROWS, CW)
            send_sum(r, 0, rcopy(ps.at[:, :, cols(n)], pr.at[r, :, :, cols(n)],
                       rss.at[r, 0], rsr.at[r, n, 0], partner))
            hq[4 * ROWS :, cols(n)] = total[4 * ROWS :]

    def scatter_second(r, numbers=range(NCH)):
        if r == 2 and 0 in numbers:
            sent(0, 1, 6)
        for n in numbers:
            arrive(pr.at[r, :, :, cols(n)], rsr.at[r, n, 0])
            total = hq[4 * ROWS :, cols(n)].reshape(4, ROWS, CW) + pr[r, :, :, cols(n)].astype(f32)
            own[r % 2, :, cols(n)] = total[0]
            sb[r % 2, :, :, cols(n)] = total[1:].astype(bf16)
            send_sum(r, 1, rcopy(sb.at[r % 2, 1, H0, cols(n)], rl.at[r, 0, :, cols(n)],
                       rss.at[r, 1], rsr.at[r, n, 1], right))
            send_sum(r, 2, rcopy(sb.at[r % 2, 1, H1, cols(n)], rl.at[r, 1, :, cols(n)],
                       rss.at[r, 2], rsr.at[r, n, 2], left))
            send_sum(r, 3, rcopy(sb.at[r % 2, 0, H1, cols(n)], fr.at[r, 0, H1, cols(n)],
                       rss.at[r, 3], rsr.at[r, n, 3], right))
            send_sum(r, 4, rcopy(sb.at[r % 2, 2, H0, cols(n)], fr.at[r, 1, H0, cols(n)],
                       rss.at[r, 4], rsr.at[r, n, 3], left))

    def scatter_relay(r):
        for n in range(NCH):
            arrive(rl.at[r, 0, :, cols(n)], rsr.at[r, n, 1])
            sb[r % 2, 0, H0, cols(n)] = (
                sb[r % 2, 0, H0, cols(n)].astype(f32) + rl[r, 0, :, cols(n)].astype(f32)
            ).astype(bf16)
            send_sum(r, 5, rcopy(sb.at[r % 2, 0, H0, cols(n)], fr.at[r, 0, H0, cols(n)],
                       rss.at[r, 5], rsr.at[r, n, 3], right))
            arrive(rl.at[r, 1, :, cols(n)], rsr.at[r, n, 2])
            sb[r % 2, 2, H1, cols(n)] = (
                sb[r % 2, 2, H1, cols(n)].astype(f32) + rl[r, 1, :, cols(n)].astype(f32)
            ).astype(bf16)
            send_sum(r, 6, rcopy(sb.at[r % 2, 2, H1, cols(n)], fr.at[r, 1, H1, cols(n)],
                       rss.at[r, 6], rsr.at[r, n, 3], left))

    def scatter_part(r, n):
        arrive(fr.at[r, :, :, cols(n)], rsr.at[r, n, 3])
        return own[r % 2, :, cols(n)] + (
            fr[r, 0, :, cols(n)].astype(f32) + fr[r, 1, :, cols(n)].astype(f32)
        )

    def scatter_finish(r):
        return jnp.concatenate([scatter_part(r, n) for n in range(NCH)], axis=-1)

    hi, lo = yh == 1, yh == 0
    mid = (z == 1) | (z == 2)

    relay_k = (y == 1) | (y == 2)
    relay_v = (y == 0) | (y == 3)

    TH = (pl.ds(0, TOK // 2), pl.ds(TOK // 2, TOK // 2))

    def kv_near(j):
        for i in range(2):
            o = kvs.at[j, i, 0]
            launch(rcopy(o, kvs.at[j, i, 1], kss.at[j, 1], ksr.at[j, 1, i], z_up), z < 3)
            launch(rcopy(o, kvs.at[j, i, 3], kss.at[j, 3], ksr.at[j, 3, i], z_dn), z == 0)
            launch(rcopy(o, kvs.at[j, i, 2], kss.at[j, 5], ksr.at[j, 2, i], z_op), lo & (z == 3))
            launch(rcopy(o, kvs.at[j, i, 3], kss.at[j, 3], ksr.at[j, 3, i], z_dn), lo & (z == 1))
        both = kvs.at[j, :, 0]
        owe(both, kss.at[j, 1], z < 3)
        owe(both, kss.at[j, 3], (z == 0) | (lo & (z == 1)))
        owe(both, kss.at[j, 5], lo & (z == 3))

    def kv_cross(j):
        k, v = kvs.at[j, 0, 0], kvs.at[j, 1, 0]
        launch(rcopy(k, kvrl.at[j, 0], kss.at[j, 6], ksr.at[j, 0, 0], y_up), lo)
        launch(rcopy(v, kvrl.at[j, 0], kss.at[j, 6], ksr.at[j, 0, 0], y_dn), lo)
        owe(kvs.at[j, :, 0], kss.at[j, 6], lo)

    def kv_relay(j):
        b = kvrl.at[j, 0]
        arrive(b, ksr.at[j, 0, 0])
        launch(rcopy(b, kvs.at[j, 0, 4], kss.at[j, 4], ksr.at[j, 4, 0], y_up), relay_k)
        launch(rcopy(b, kvs.at[j, 1, 4], kss.at[j, 4], ksr.at[j, 4, 1], y_dn), relay_v)
        owe(b, kss.at[j, 4])

    def kv_second(j):
        low = z <= 1
        far = jnp.maximum(3 - z, 2)
        for i in range(2):
            b1, b2, b4 = (kvs.at[j, i, d] for d in (1, far, 4))
            arrive(b2, ksr.at[j, far, i], lo & low)
            launch(rcopy(b2, kvrl.at[j, 1], kss.at[j, 0], ksr.at[j, 5, 0],
                       y_dn if i else y_up), lo & low)
            arrive(b1, ksr.at[j, 1, i], mid)
            launch(rcopy(b1, kvs.at[j, i, 2], kss.at[j, 2], ksr.at[j, 2, i], z_up), mid)
            arrive(b4, ksr.at[j, 4, i], hi)
            launch(rcopy(b4, kvs.at[j, i, 3], kss.at[j, 10], ksr.at[j, 3, i], z_dn), hi & (z == 3))
            for q in range(2):
                launch(rcopy(b4.at[TH[q]], kvs.at[j, i, 3, TH[q]], kss.at[j, 8],
                           ksr.at[j, 6 + i, q], z_dn), hi & (z == 2))
            launch(rcopy(b4, kvs.at[j, i, 1], kss.at[j, 11], ksr.at[j, 1, i], z_up), hi & (z == 3))
        both = kvs.at[j, :, 0]
        owe(both, kss.at[j, 0], lo & low)
        owe(both, kss.at[j, 2], mid)
        owe(both, kss.at[j, 10], hi & (z == 3))
        owe(both, kss.at[j, 8], hi & (z == 2))
        owe(both, kss.at[j, 11], hi & (z == 3))

    def kv_third(j):
        low = z <= 1
        b = kvrl.at[j, 1]
        arrive(b, ksr.at[j, 5, 0], low)
        far = jnp.maximum(3 - z, 2)
        launch(rcopy(b, kvs.at[j, 0, far], kss.at[j, 7], ksr.at[j, far, 0], y_up), low & relay_k)
        launch(rcopy(b, kvs.at[j, 1, far], kss.at[j, 7], ksr.at[j, far, 1], y_dn), low & relay_v)
        owe(b, kss.at[j, 7], low)

    def kv_fourth(j):
        cond = hi & (z == 1)
        for i in range(2):
            for q in range(2):
                b3 = kvs.at[j, i, 3, TH[q]]
                arrive(b3, ksr.at[j, 6 + i, q], cond)
                launch(rcopy(b3, kvs.at[j, i, 2, TH[q]], kss.at[j, 9],
                           ksr.at[j, 8 + i, q], z_dn), cond)
        owe(kvs.at[j, :, 0], kss.at[j, 9], cond)


    def kv_near_in(j):
        for i in range(2):
            arrive(kvs.at[j, i, 1], ksr.at[j, 1, i], (z == 3) | (hi & (z == 0)))
            arrive(kvs.at[j, i, 3], ksr.at[j, 3, i], (z == 3) | (hi & (z != 1)))

    def kv_far_in(j):
        four = hi & (z == 0)
        for i in range(2):
            arrive(kvs.at[j, i, 2], ksr.at[j, 2, i], (z >= 2) | (hi & (z == 1)))
            for q in range(2):
                arrive(kvs.at[j, i, 2, TH[q]], ksr.at[j, 8 + i, q], four)

    def kv_finish(j):
        kv_near_in(j)
        kv_far_in(j)

    def project(j):
        cosine, sine = cos_ref[...], sin_ref[...]
        for load in loads[2 + 4 * j : 5 + 4 * j]:
            load.wait()
        xn = ag[j].reshape(TOK, D)
        q_gain, k_gain = gain(qg, j), gain(kg, j)
        kr = dot(xn, wk[j])
        kvs[j, 0, 0] = rope(kr * rms_of(kr) * k_gain, cosine, sine).astype(bf16)
        kvs[j, 1, 0] = dot(xn, wv[j]).astype(bf16)
        if j == BACK:
            kv_cross(j)
        kv_near(j)
        if j == BACK:
            kraw[...] = kr
        for h in range(2):
            qr = dot(xn, wq[j, :, h * HD : (h + 1) * HD])
            query = rope(qr * rms_of(qr) * q_gain, cosine, sine).astype(bf16)
            qs[j, h * TOK : (h + 1) * TOK] = query * jnp.asarray(HD ** -0.5, bf16)
            if j == BACK:
                qraw[h * TOK : (h + 1) * TOK] = qr

    def score(j, ci, d):
        sc = dot_nt(qs[j, chunk_rows(ci), :], kvs[j, 0, d])
        if d in (0, 4):
            ii = lax.broadcasted_iota(jnp.int32, (TOK, TOK), 0)
            ahead_by = ii - lax.broadcasted_iota(jnp.int32, (TOK, TOK), 1)
            if d == 0:
                return jnp.where(ahead_by >= 0, sc, masked_score)
            return jnp.where(ahead_by < jnp.where(p >= 4, 0, -TOK), sc, masked_score)
        return sc + jnp.where(p >= d, 0.0, masked_score)

    def top_of(scs):
        top = jnp.max(scs[0], axis=-1, keepdims=True)
        for sc in scs[1:]:
            top = jnp.maximum(top, jnp.max(sc, axis=-1, keepdims=True))
        return top

    def sum_of(es):
        total = es[0]
        for e in es[1:]:
            total = total + e
        return jnp.sum(total, axis=-1, keepdims=True)

    def chunk_rows(ci):
        return slice(ci * TOK, (ci + 1) * TOK)

    def weigh(j, ci, low):
        out = dot(low, kvs[j, 1].reshape(5 * TOK, HD)).astype(bf16)
        cx[j, :, :, ci * HD : (ci + 1) * HD] = out.reshape(8, ROWS, HD)

    near_blocks = (0, 1, 3, 4)

    def block_cols(d):
        return slice(d * TOK, (d + 1) * TOK)

    def attend_near():
        for ci in range(2):
            rows = chunk_rows(ci)
            scs = [score(BACK, ci, d) for d in near_blocks]
            top = top_of(scs)
            es = [jnp.exp(sc - top) for sc in scs]
            for d, e in zip(near_blocks, es):
                pw[rows, block_cols(d)] = e
            tops[rows, :] = top
            sums[rows, :] = sum_of(es)

    def attend_far():
        for ci in range(2):
            rows = chunk_rows(ci)
            sc = score(BACK, ci, 2)
            top = jnp.maximum(tops[rows, :], jnp.max(sc, axis=-1, keepdims=True))
            e = jnp.exp(sc - top)
            pw[rows, block_cols(2)] = e
            near = jnp.exp(tops[rows, :] - top)
            far = 1.0 / (sums[rows, :] * near + jnp.sum(e, axis=-1, keepdims=True))
            near = near * far
            tops[rows, :] = near
            sums[rows, :] = far
            lows = []
            for d in range(5):
                w = e * far if d == 2 else pw[rows, block_cols(d)] * near
                lows.append(w.astype(bf16))
                pl_s[rows, block_cols(d)] = lows[d]
            weigh(BACK, ci, jnp.concatenate(lows, axis=-1))

    def attention(j):
        for ci in range(2):
            scs = [score(j, ci, d) for d in range(5)]
            top = top_of(scs)
            es = [jnp.exp(sc - top) for sc in scs]
            inverse = 1.0 / sum_of(es)
            weigh(j, ci, jnp.concatenate([(e * inverse).astype(bf16) for e in es], axis=-1))

    def out_product(j):
        return lambda lhs, n: dot(lhs, wo[j, :, n * CW : (n + 1) * CW])

    def hidden_product(lhs, n):
        w_rows = slice(n * CW, (n + 1) * CW)
        total = hq[:, cols(n)] + dot_nt(lhs[:, 2 * HD : 3 * HD], wk[BACK, w_rows, :])
        return total + dot_nt(lhs[:, 3 * HD :], wv[BACK, w_rows, :])

    loads[0].wait()
    for load in small:
        load.wait()
    x_back = sti[plan[0, 1]].astype(f32)
    ag[BACK, t] = (x_back * rms_of(x_back) * gain(ig, BACK)).astype(bf16)
    pl.semaphore_wait(barrier, 8)
    gather_start(BACK)
    x_fwd = sti[plan[0, 0]].astype(f32)
    ag[FWD, t] = (x_fwd * rms_of(x_fwd) * gain(ig, FWD)).astype(bf16)
    for j in range(2):
        for d in range(1, 5):
            @pl.when((d > p) & (d + p != 3))
            def _():
                for i in range(2):
                    kvs[j, i, d] = jnp.zeros((TOK, HD), bf16)
    angles = (p * TOK + lax.broadcasted_iota(jnp.int32, (TOK, HD // 2), 0)).astype(f32)
    pair = lax.broadcasted_iota(jnp.int32, (1, HD // 2), 1).astype(f32)
    angles = angles * jnp.exp(pair * (-2.0 * math.log(rope_base) / HD))
    cos_ref[...] = jnp.cos(angles)
    sin_ref[...] = jnp.sin(angles)
    gather_relay(BACK)
    gather_start(FWD)
    gather_finish(BACK)
    project(BACK)
    gather_relay(FWD)
    kv_relay(BACK)
    gather_finish(FWD)
    kv_second(BACK)
    project(FWD)
    kv_third(BACK)
    kv_cross(FWD)
    kv_fourth(BACK)
    kv_near_in(BACK)
    attend_near()
    kv_relay(FWD)
    kv_far_in(BACK)
    attend_far()
    loads[5].wait()
    scatter_first(BACK, out_product(BACK), rows_all(cx.at[BACK]),
                  lambda n: scatter_second(BACK, (n,)))
    scatter_second(BACK, range(NCH - 3, NCH))
    kv_second(FWD)
    scatter_relay(BACK)
    kv_third(FWD)
    kv_fourth(FWD)
    projected = scatter_finish(BACK)
    loads[1].wait()
    incoming = stg[plan[0, 1]].astype(f32)
    ag[GRAD, t] = rms_back(projected, incoming, gain(og, BACK)).astype(bf16)
    gather_start(GRAD)
    go[...] = sti[plan[0, 1]]
    fo[...] = stg[plan[0, 1]]
    ahead = (
        rcopy(go, bo.at[0], swap_s.at[2], swap_r.at[2], other),
        rcopy(fo, bo.at[1], swap_s.at[0], swap_r.at[0], other),
    )
    for copy in ahead:
        copy.start()
    kv_finish(FWD)
    attention(FWD)
    gather_relay(GRAD)
    loads[9].wait()
    scatter_first(FWD, out_product(FWD), rows_all(cx.at[FWD]))
    gather_finish(GRAD)

    og_rows = ag[GRAD].reshape(TOK, D)
    for h in range(2):
        cgs[h * TOK : (h + 1) * TOK] = dot_nt(
            og_rows, wo[BACK, h * HD : (h + 1) * HD, :]
        ).astype(bf16)
    q_gain, k_gain = gain(qg, BACK), gain(kg, BACK)

    R1, R2, R3, R4, R5 = 0, 1, 2, 3, 4
    OWN, ONE, FOUR = 0, 1, 2

    def grad_block(i, d):
        if i == 0:
            return dot_tn(dss[:, d * TOK : (d + 1) * TOK], qs[BACK])
        return dot_tn(pl_s[:, d * TOK : (d + 1) * TOK], cgs[...])

    def g_send(d, e, se, device, cond, i):
        send(rcopy(gs.at[i, d - 1], gr.at[e, i], gss.at[se, i], gsr.at[e, i], device), cond)

    def g_add(e, k, cond, i):
        arrive(gr.at[e, i], gsr.at[e, i], cond)

        @pl.when(cond)
        def _():
            gacc[i, k] = gacc[i, k] + gr[e, i].astype(f32)

    def g_cross(i, d, far, cond):
        for h, device in enumerate((y_dn, y_up)):
            send(rcopy(gs.at[i, d - 1, TH[h]], grr.at[far, i], gsc.at[far, i, h],
                       gcr.at[far, i], device), cond)

    def g_relay(i, far):
        cond = z <= 1 if far else None
        e = R5 if far else R4
        buf = grr.at[far, i]
        arrive(buf, gcr.at[far, i], cond)
        for h, (role, device) in enumerate(((relay_k, y_dn), (relay_v, y_up))):
            send(rcopy(buf, gr.at[e, i, TH[h]], gsx.at[far, i], gsh.at[far, i, h], device),
                 role & cond if far else role)

    def g_halves(i, far, cond):
        for h in range(2):
            arrive(gr.at[R5 if far else R4, i, TH[h]], gsh.at[far, i, h], cond)

    def g_forward(i):
        cond = lo & (z <= 1)
        g_halves(i, 1, cond)
        ahead_cond = cond if i else lo & (z == 1)
        send(rcopy(gr.at[R5, i], gr.at[R5, i], gss.at[7, i], gsr.at[R5, i], z_op), ahead_cond)
        if i == 0:
            for h in range(2):
                send(rcopy(gr.at[R5, 0, TH[h]], gr.at[R3, 0, TH[h]], gsz.at[h], gsy.at[0, h], z_up),
                     lo & (z == 0))

    def g_forward_again():
        cond = lo & (z == 1)
        for h in range(2):
            part = gr.at[R3, 0, TH[h]]
            arrive(part, gsy.at[0, h], cond)
            send(rcopy(part, gr.at[R5, 0, TH[h]], gsz.at[h], gsy.at[1, h], z_up), cond)

    def g_first(i):
        gs[i, 1] = grad_block(i, 2).astype(bf16)
        g_cross(i, 2, 1, hi & (z <= 1))
        g_send(2, R2, 0, z_dn, z >= 2, i)
        gs[i, 2] = grad_block(i, 3).astype(bf16)
        g_send(3, R3, 2, z_up, (z == 3) | hi, i)
        gacc[i, ONE] = grad_block(i, 1)
        gs[i, 0] = gacc[i, ONE].astype(bf16)
        g_send(1, R1, 3, z_dn, (z == 3) | (hi & (z == 0)), i)
        gacc[i, FOUR] = grad_block(i, 4)
        gacc[i, OWN] = grad_block(i, 0)

    def g_middle(i):
        g_add(R2, ONE, mid, i)

        @pl.when(mid)
        def _():
            gs[i, 0] = gacc[i, ONE].astype(bf16)
        g_send(1, R1, 3, z_dn, mid, i)

    def g_third(i):
        g_add(R3, FOUR, hi & (z >= 1), i)
        g_add(R1, FOUR, hi & (z == 3), i)
        gs[i, 3] = gacc[i, FOUR].astype(bf16)
        g_cross(i, 4, 0, hi)

    early = len(drains)
    g_first(1)

    for ci in range(2):
        rows = chunk_rows(ci)
        near, far = tops[rows, :], sums[rows, :]
        ws = [pw[rows, block_cols(d)] * (far if d == 2 else near) for d in range(5)]
        wgs = [dot_nt(cgs[rows, :], kvs[BACK, 1, d]) for d in range(5)]
        delta = sum_of([w * wg for w, wg in zip(ws, wgs)])
        for d in range(5):
            dss[rows, block_cols(d)] = (ws[d] * (wgs[d] - delta)).astype(bf16)

    g_first(0)
    g_middle(1)
    g_relay(1, 1)
    g_third(1)
    scatter_second(FWD)
    g_middle(0)
    g_relay(0, 1)
    g_third(0)

    for h in range(2):
        rows = slice(h * TOK, (h + 1) * TOK)
        dq = dot(dss[rows, :], kvs[BACK, 0].reshape(5 * TOK, HD)) * (HD ** -0.5)
        low = rms_back(
            qraw[rows], rope_back(dq, cos_ref[...], sin_ref[...]), q_gain
        ).astype(bf16)
        lq[:, :, h * HD : (h + 1) * HD] = low.reshape(8, ROWS, HD)
    query_low = rows_all(lq)[:, : 2 * HD]
    for n in range(NCH):
        hq[:, cols(n)] = dot_nt(query_low, wq[BACK, n * CW : (n + 1) * CW, :])

    g_forward(1)
    g_relay(1, 0)
    g_forward(0)
    g_relay(0, 0)
    g_forward_again()
    for copy in ahead:
        copy.wait_send()
    scatter_relay(FWD)
    flush(0, early)
    sent(0, 0, 6)
    sent(1, 0, 4)
    for i in (1, 0):
        g_add(R1, OWN, z < 3, i)
        g_add(R3, OWN, z == 0, i)
        g_halves(i, 0, lo)

        @pl.when(lo)
        def _():
            gacc[i, OWN] = gacc[i, OWN] + gr[R4, i].astype(f32)
        if i:
            g_add(R5, OWN, lo & (z >= 2), i)
        else:
            for h in range(2):
                arrive(gr.at[R5, 0, TH[h]], gsy.at[1, h], lo & (z == 2))
            arrive(gr.at[R5, 0], gsr.at[R5, 0], lo & (z == 3))

            @pl.when(lo & (z >= 2))
            def _():
                gacc[0, OWN] = gacc[0, OWN] + gr[R5, 0].astype(f32)
    key_low = rms_back(
        kraw[...], rope_back(gacc[0, 0], cos_ref[...], sin_ref[...]), k_gain
    ).astype(bf16)
    lq[:, :, 2 * HD : 3 * HD] = key_low.reshape(8, ROWS, HD)
    lq[:, :, 3 * HD :] = gacc[1, 0].astype(bf16).reshape(8, ROWS, HD)

    scatter_first(2, hidden_product, rows_all(lq), lambda n: scatter_second(2, (n,)))
    scatter_second(2, range(NCH - 3, NCH))
    fwd_proj = scatter_finish(FWD)
    x_fwd = sti[plan[0, 0]].astype(f32)
    fo[...] = (x_fwd + fwd_proj * rms_of(fwd_proj) * gain(og, FWD)).astype(bf16)
    send(rcopy(fo, act_out, swap_s.at[1], swap_r.at[1], other))
    scatter_relay(2)
    flush(0, len(drains))
    sent(1, 0, 6)
    sent(2, 0, 4)
    for n in range(NCH):
        hidden = scatter_part(2, n)
        gb[0, :, cols(n)] = (hidden * ig[pl.ds(legs[BACK], 1), cols(n)]).astype(bf16)
        send(rcopy(gb.at[0, :, cols(n)], gb.at[1, :, cols(n)],
                   swap_s.at[3 + n], swap_r.at[3 + n], other))
    arrive(bo.at[0], swap_r.at[2])
    arrive(bo.at[1], swap_r.at[0])
    x_other = bo[0].astype(f32)
    scale = rms_of(x_other)
    for n in range(NCH):
        arrive(gb.at[1, :, cols(n)], swap_r.at[3 + n])
    g = gb[1].astype(f32)
    centred = g - x_other * (scale * scale * jnp.mean(g * x_other, axis=-1, keepdims=True))
    go[...] = (bo[1].astype(f32) + scale * centred).astype(bf16)
    final = pltpu.make_async_copy(go, grad_out, lsem.at[10])
    final.start()
    arrive(act_out, swap_r.at[1])
    flush(0, len(drains))
    sent(2, 0, 6)
    final.wait()


def hand_on(act_in, grad_in, act_out, grad_out, held, lsem):
    pairs = ((act_in, act_out), (grad_in, grad_out))
    ins = [pltpu.make_async_copy(src, held.at[k], lsem.at[k]) for k, (src, _) in enumerate(pairs)]
    outs = [
        pltpu.make_async_copy(held.at[k], dst, lsem.at[2 + k]) for k, (_, dst) in enumerate(pairs)
    ]
    for copy in ins:
        copy.start()
    for taken, given in zip(ins, outs):
        taken.wait()
        given.start()
    for copy in outs:
        copy.wait()


def per_device(
    stash_inputs, stash_grads, plan, query_weight, key_weight, value_weight, out_weight,
    input_gain, output_gain, query_gain, key_gain,
):
    hbm = pl.BlockSpec(memory_space=pl.ANY)
    smem = pl.BlockSpec(memory_space=pltpu.SMEM)
    V = pltpu.VMEM
    sem = pltpu.SemaphoreType.DMA
    act, grad = pl.pallas_call(
        kernel,
        out_shape=(jax.ShapeDtypeStruct((ROWS, D), bf16),) * 2,
        in_specs=[smem] + [hbm] * 10,
        out_specs=(hbm, hbm),
        scratch_shapes=[
            V((2, D, 2 * HD), bf16), V((2, D, HD), bf16), V((2, D, HD), bf16), V((2, 2 * HD, D), bf16),
            V((4, ROWS, D), bf16), V((4, ROWS, D), bf16),
            V((3, 8, ROWS, D), bf16),
            V((2, 2 * TOK, HD), bf16), V((2 * TOK, HD), f32), V((TOK, HD), f32),
            V((2, 2, 5, TOK, HD), bf16), V((2, 2, TOK, HD), bf16), V((2, 2, TOK // 2, HD), bf16),
            V((2, 8, ROWS, 2 * HD), bf16),
            V((2 * TOK, 5 * TOK), f32), V((2 * TOK, 5 * TOK), bf16), V((2 * TOK, 5 * TOK), bf16),
            V((2 * TOK, HD), bf16),
            V((4, ROWS, D), bf16), V((3, 4, ROWS, D), bf16), V((2, 3, ROWS, D), bf16),
            V((3, 2, ROWS // 2, D), bf16), V((3, 2, ROWS, D), bf16), V((2, ROWS, D), f32),
            V((2, 4, TOK, HD), bf16), V((5, 2, TOK, HD), bf16), V((2, 3, TOK, HD), f32),
            V((8, ROWS, 4 * HD), bf16),
            V((ROWS, D), bf16), V((ROWS, D), bf16), V((TOK, HD // 2), f32), V((TOK, HD // 2), f32),
            V((2 * 4 * ROWS, D), f32), V((2, ROWS, D), bf16), V((2, ROWS, D), bf16),
            V((2, D), f32), V((2, D), f32), V((2, HD), f32), V((2, HD), f32),
            V((2 * TOK, 1), f32), V((2 * TOK, 1), f32),
            sem((15,)), sem((3,)), sem((3, 7)), sem((3, 7)), sem((3, NCH, 4)),
            sem((2, 12)), sem((2, 10, 2)), sem((8, 2)), sem((5, 2)),
            sem((2, 2, 2)), sem((2, 2)), sem((2, 2)), sem((2, 2, 2)), sem((2, 2)), sem((2,)), sem((3 + NCH,)), sem((3 + NCH,)),
        ],
        compiler_params=pltpu.CompilerParams(
            collective_id=0, has_side_effects=True, vmem_limit_bytes=67043328
        ),
    )(
        plan, input_gain[0], output_gain[0], query_gain[0],
        key_gain[0], stash_inputs[0], stash_grads[0], query_weight[0], key_weight[0],
        value_weight[0], out_weight[0],
    )
    act, grad = pl.pallas_call(
        hand_on,
        out_shape=(jax.ShapeDtypeStruct((ROWS, D), bf16),) * 2,
        in_specs=[hbm, hbm],
        out_specs=(hbm, hbm),
        scratch_shapes=[V((2, ROWS, D), bf16), sem((4,))],
    )(act, grad)
    return act[None], grad[None]


def solution(mesh):
    return jax.shard_map(
        per_device,
        mesh=mesh,
        in_specs=(
            P("segment", None, ("ctx", "tp"), None),
            P("segment", None, ("ctx", "tp"), None),
            P("segment", None),
            P("segment", None, None, "tp"),
            P("segment", None, None, "tp"),
            P("segment", None, None, "tp"),
            P("segment", None, "tp", None),
            P("segment", None, None),
            P("segment", None, None),
            P("segment", None, None),
            P("segment", None, None),
        ),
        out_specs=(P("segment", ("ctx", "tp"), None), P("segment", ("ctx", "tp"), None)),
        check_vma=False,
    )
```

```python
import math

import jax
import jax.numpy as jnp
from jax import lax
from jax.experimental import pallas as pl
from jax.experimental.pallas import tpu as pltpu
from jax.sharding import PartitionSpec as P

WINDOW = 1024
epsilon = 1e-06
rope_base = 10000.0
masked_score = -1e30

D = 3840
ROWS = 32
TOK = 256
HD = 256
NCH = 5
CW = D // NCH
BACK, FWD, GRAD = 0, 1, 2
f32 = jnp.float32
bf16 = jnp.bfloat16
MESH = pl.DeviceIdType.MESH


def dot(a, b):
    return lax.dot_general(a, b, (((1,), (0,)), ((), ())), preferred_element_type=f32)


def dot_nt(a, b):
    return lax.dot_general(a, b, (((1,), (1,)), ((), ())), preferred_element_type=f32)


def dot_tn(a, b):
    return lax.dot_general(a, b, (((0,), (0,)), ((), ())), preferred_element_type=f32)


def rms_of(x):
    return lax.rsqrt(jnp.mean(x * x, axis=-1, keepdims=True) + epsilon)


def rms_back(x, grad, gain):
    g = grad * gain
    r = rms_of(x)
    return r * (g - x * (r * r * jnp.mean(g * x, axis=-1, keepdims=True)))


def rope(y, cosine, sine):
    a, b = y[:, : HD // 2], y[:, HD // 2 :]
    return jnp.concatenate([a * cosine - b * sine, b * cosine + a * sine], axis=-1)


def rope_back(g, cosine, sine):
    a, b = g[:, : HD // 2], g[:, HD // 2 :]
    return jnp.concatenate([a * cosine + b * sine, b * cosine - a * sine], axis=-1)


def kernel(
    plan, ig_h, og_h, qg_h, kg_h, si, sg, wq_h, wk_h, wv_h, wo_h,
    act_out, g_out, xi_out,
    wq, wk, wv, wo, sti, stg, ag, qs, qraw, kraw, kvs, kvrl, grr, cx, pw, pl_s, dss, cgs,
    ps, pr, sb, rl, fr, own, gs, gr, gacc, lq, fo, go, cos_ref, sin_ref, hq, gb, ig, og, qg, kg, tops, sums,
    lsem, ags, agr, rss, rsr, kss, ksr, gss, gsr, gsc, gcr, gsx, gsh, gsy, gsz, swap_s, swap_r,
):
    s = lax.axis_index("segment")
    p = lax.axis_index("ctx")
    t = lax.axis_index("tp")
    yh, z = p // 4, p % 4
    y = 2 * yh + s
    x, c = t // 2, t % 2
    legs = (1 - s, s)

    def dev(s_=None, p_=None, t_=None):
        return {
            "segment": s if s_ is None else s_,
            "ctx": p if p_ is None else p_,
            "tp": t if t_ is None else t_,
        }

    t_r, t_l = ((x + 1) % 4) * 2 + c, ((x + 3) % 4) * 2 + c
    t_o = ((x + 2) % 4) * 2 + c
    t_p = 2 * x + 1 - c
    right, left, partner = dev(t_=t_r), dev(t_=t_l), dev(t_=t_p)
    z_up, z_dn = dev(p_=4 * yh + (z + 1) % 4), dev(p_=4 * yh + (z + 3) % 4)
    z_op = dev(p_=4 * yh + (z + 2) % 4)
    y_u, y_d = (y + 1) % 4, (y + 3) % 4
    y_up = dev(s_=y_u % 2, p_=(y_u // 2) * 4 + z)
    y_dn = dev(s_=y_d % 2, p_=(y_d // 2) * 4 + z)
    other = dev(s_=1 - s)

    barrier = pltpu.get_barrier_semaphore()
    for device in (right, left, partner, z_up, z_dn, z_op, y_up, y_dn):
        pl.semaphore_signal(barrier, inc=1, device_id=device, device_id_type=MESH)

    loads = [
        pltpu.make_async_copy(si, sti, lsem.at[0]),
        pltpu.make_async_copy(sg, stg, lsem.at[1]),
    ]
    for j in range(2):
        loads += [
            pltpu.make_async_copy(wq_h.at[legs[j]], wq.at[j], lsem.at[2 + 4 * j]),
            pltpu.make_async_copy(wk_h.at[legs[j]], wk.at[j], lsem.at[3 + 4 * j]),
            pltpu.make_async_copy(wv_h.at[legs[j]], wv.at[j], lsem.at[4 + 4 * j]),
            pltpu.make_async_copy(wo_h.at[legs[j]], wo.at[j], lsem.at[5 + 4 * j]),
        ]
    small = [
        pltpu.make_async_copy(src, dst, lsem.at[11 + k])
        for k, (src, dst) in enumerate(((ig_h, ig), (og_h, og), (qg_h, qg), (kg_h, kg)))
    ]
    for load in loads[:1] + small + loads[1:]:
        load.start()

    def gain(ref, j):
        return ref[pl.ds(legs[j], 1), :]

    def rcopy(src, dst, ssem, rsem, device):
        return pltpu.make_async_remote_copy(
            src_ref=src, dst_ref=dst, send_sem=ssem, recv_sem=rsem,
            device_id=device, device_id_type=MESH,
        )

    drains = []

    def when(cond, run):
        if cond is None:
            run()
        else:
            pl.when(cond)(run)

    def send(copy, cond=None):
        when(cond, copy.start)
        drains.append((copy, cond))

    def launch(copy, cond=None):
        when(cond, copy.start)

    def owe(ref, ssem, cond=None):
        drains.append((rcopy(ref, ref, ssem, swap_r.at[0], partner), cond))

    def flush(first, last):
        groups = {}
        for copy, cond in drains[first:last]:
            groups.setdefault(id(cond), (cond, []))[1].append(copy)
        for cond, copies in groups.values():
            def run(copies=copies):
                for copy in copies:
                    copy.wait_send()
            when(cond, run)
        del drains[first:last]

    def arrive(dst, rsem, cond=None):
        copy = rcopy(dst, dst, swap_s.at[0], rsem, partner)
        when(cond, copy.wait_recv)

    H0, H1 = pl.ds(0, ROWS // 2), pl.ds(ROWS // 2, ROWS // 2)
    halves = (H0, H1)

    def gather_start(j):
        blk = ag.at[j, t]
        launch(rcopy(blk.at[H0], blk.at[H0], ags.at[j], agr.at[j, 0], right))
        launch(rcopy(blk.at[H1], blk.at[H1], ags.at[j], agr.at[j, 1], left))
        launch(rcopy(blk.at[H1], blk.at[H1], ags.at[j], agr.at[j, 2], right))
        launch(rcopy(blk.at[H0], blk.at[H0], ags.at[j], agr.at[j, 3], left))
        launch(rcopy(blk, blk, ags.at[j], agr.at[j, 6], partner))

    def across(j, place, half):
        part = ag.at[j, place, halves[half]]
        launch(rcopy(part, part, ags.at[j], agr.at[j, 6], partner))

    def gather_relay(j):
        a = ag.at[j, t_l, H0]
        arrive(a, agr.at[j, 0])
        launch(rcopy(a, a, ags.at[j], agr.at[j, 4], right))
        b = ag.at[j, t_r, H1]
        arrive(b, agr.at[j, 1])
        launch(rcopy(b, b, ags.at[j], agr.at[j, 5], left))
        across(j, t_l, 0)
        across(j, t_r, 1)

    def gather_finish(j):
        arrive(ag.at[j, t_l, H1], agr.at[j, 2])
        across(j, t_l, 1)
        arrive(ag.at[j, t_r, H0], agr.at[j, 3])
        across(j, t_r, 0)
        arrive(ag.at[j, t_o, H0], agr.at[j, 4])
        across(j, t_o, 0)
        arrive(ag.at[j, t_o, H1], agr.at[j, 5])
        across(j, t_o, 1)
        arrive(ag.at[j, pl.ds(0, 4)], agr.at[j, 6])
        owe(ag.at[j, pl.ds(0, 7)], ags.at[j])

    def cols(n):
        return pl.ds(n * CW, CW)

    def rows_of(ref, parity):
        parts = [ref[2 * ((x + k) % 4) + parity] for k in range(4)]
        return jnp.concatenate(parts, axis=0)

    def rows_all(ref):
        return jnp.concatenate([rows_of(ref, 1 - c), rows_of(ref, c)], axis=0)

    def sent(r, first, last):
        b = r % 2
        parts = (
            ps, sb.at[b, 1, H0], sb.at[b, 1, H1], sb.at[b, 0, H1],
            sb.at[b, 2, H0], sb.at[b, 0, H0], sb.at[b, 2, H1],
        )
        for i in range(first, last + 1):
            if (r, i) in flying:
                flying.remove((r, i))
                rcopy(parts[i], parts[i], rss.at[r, i], swap_r.at[0], partner).wait_send()

    flying = set()

    def send_sum(r, i, copy):
        copy.start()
        flying.add((r, i))

    def scatter_first(r, product, lhs, then=None):
        if r:
            sent(r - 1, 0, 0)
        for n in range(NCH):
            if then and n >= 3:
                then(n - 3)
            total = product(lhs, n)
            ps[:, :, cols(n)] = total[: 4 * ROWS].astype(bf16).reshape(4, ROWS, CW)
            send_sum(r, 0, rcopy(ps.at[:, :, cols(n)], pr.at[r, :, :, cols(n)],
                       rss.at[r, 0], rsr.at[r, n, 0], partner))
            hq[4 * ROWS :, cols(n)] = total[4 * ROWS :]

    def send_direct(r, n):
        send_sum(r, 3, rcopy(sb.at[r % 2, 0, H1, cols(n)], fr.at[r, 0, H1, cols(n)],
                             rss.at[r, 3], rsr.at[r, n, 3], right))
        send_sum(r, 4, rcopy(sb.at[r % 2, 2, H0, cols(n)], fr.at[r, 1, H0, cols(n)],
                             rss.at[r, 4], rsr.at[r, n, 3], left))

    def scatter_second(r, numbers=range(NCH)):
        if r == 2 and 0 in numbers:
            sent(0, 1, 6)
        for n in numbers:
            arrive(pr.at[r, :, :, cols(n)], rsr.at[r, n, 0])
            total = hq[4 * ROWS :, cols(n)].reshape(4, ROWS, CW) + pr[r, :, :, cols(n)].astype(f32)
            own[r % 2, :, cols(n)] = total[0]
            sb[r % 2, :, :, cols(n)] = total[1:].astype(bf16)
            send_sum(r, 1, rcopy(sb.at[r % 2, 1, H0, cols(n)], rl.at[r, 0, :, cols(n)],
                       rss.at[r, 1], rsr.at[r, n, 1], right))
            send_sum(r, 2, rcopy(sb.at[r % 2, 1, H1, cols(n)], rl.at[r, 1, :, cols(n)],
                       rss.at[r, 2], rsr.at[r, n, 2], left))
            if r == 1:
                send_direct(r, n)

    def scatter_relay(r):
        for n in range(NCH):
            arrive(rl.at[r, 0, :, cols(n)], rsr.at[r, n, 1])
            sb[r % 2, 0, H0, cols(n)] = (
                sb[r % 2, 0, H0, cols(n)].astype(f32) + rl[r, 0, :, cols(n)].astype(f32)
            ).astype(bf16)
            send_sum(r, 5, rcopy(sb.at[r % 2, 0, H0, cols(n)], fr.at[r, 0, H0, cols(n)],
                       rss.at[r, 5], rsr.at[r, n, 3], right))
            arrive(rl.at[r, 1, :, cols(n)], rsr.at[r, n, 2])
            sb[r % 2, 2, H1, cols(n)] = (
                sb[r % 2, 2, H1, cols(n)].astype(f32) + rl[r, 1, :, cols(n)].astype(f32)
            ).astype(bf16)
            send_sum(r, 6, rcopy(sb.at[r % 2, 2, H1, cols(n)], fr.at[r, 1, H1, cols(n)],
                       rss.at[r, 6], rsr.at[r, n, 3], left))
            if r != 1:
                send_direct(r, n)

    def scatter_part(r, n):
        arrive(fr.at[r, :, :, cols(n)], rsr.at[r, n, 3])
        return own[r % 2, :, cols(n)] + (
            fr[r, 0, :, cols(n)].astype(f32) + fr[r, 1, :, cols(n)].astype(f32)
        )

    def scatter_finish(r):
        return jnp.concatenate([scatter_part(r, n) for n in range(NCH)], axis=-1)

    hi, lo = yh == 1, yh == 0
    mid = (z == 1) | (z == 2)

    relay_k = (y == 1) | (y == 2)
    relay_v = (y == 0) | (y == 3)

    TH = (pl.ds(0, TOK // 2), pl.ds(TOK // 2, TOK // 2))

    def kv_near(j):
        for i in range(2):
            o = kvs.at[j, i, 0]
            launch(rcopy(o, kvs.at[j, i, 1], kss.at[j, 1], ksr.at[j, 1, i], z_up), z < 3)
            launch(rcopy(o, kvs.at[j, i, 3], kss.at[j, 3], ksr.at[j, 3, i], z_dn), z == 0)
            launch(rcopy(o, kvs.at[j, i, 2], kss.at[j, 5], ksr.at[j, 2, i], z_op), lo & (z == 3))
            launch(rcopy(o, kvs.at[j, i, 3], kss.at[j, 3], ksr.at[j, 3, i], z_dn), lo & (z == 1))
        both = kvs.at[j, :, 0]
        owe(both, kss.at[j, 1], z < 3)
        owe(both, kss.at[j, 3], (z == 0) | (lo & (z == 1)))
        owe(both, kss.at[j, 5], lo & (z == 3))

    def kv_cross(j):
        k, v = kvs.at[j, 0, 0], kvs.at[j, 1, 0]
        launch(rcopy(k, kvrl.at[j, 0], kss.at[j, 6], ksr.at[j, 0, 0], y_up), lo)
        launch(rcopy(v, kvrl.at[j, 0], kss.at[j, 6], ksr.at[j, 0, 0], y_dn), lo)
        owe(kvs.at[j, :, 0], kss.at[j, 6], lo)

    def kv_relay(j):
        b = kvrl.at[j, 0]
        arrive(b, ksr.at[j, 0, 0])
        launch(rcopy(b, kvs.at[j, 0, 4], kss.at[j, 4], ksr.at[j, 4, 0], y_up), relay_k)
        launch(rcopy(b, kvs.at[j, 1, 4], kss.at[j, 4], ksr.at[j, 4, 1], y_dn), relay_v)
        owe(b, kss.at[j, 4])

    def kv_second(j):
        low = z <= 1
        far = jnp.maximum(3 - z, 2)
        for i in range(2):
            b1, b2, b4 = (kvs.at[j, i, d] for d in (1, far, 4))
            arrive(b2, ksr.at[j, far, i], lo & low)
            launch(rcopy(b2, kvrl.at[j, 1], kss.at[j, 0], ksr.at[j, 5, 0],
                       y_dn if i else y_up), lo & low)
            arrive(b1, ksr.at[j, 1, i], mid)
            launch(rcopy(b1, kvs.at[j, i, 2], kss.at[j, 2], ksr.at[j, 2, i], z_up), mid)
            arrive(b4, ksr.at[j, 4, i], hi)
            launch(rcopy(b4, kvs.at[j, i, 3], kss.at[j, 10], ksr.at[j, 3, i], z_dn), hi & (z == 3))
            for q in range(2):
                launch(rcopy(b4.at[TH[q]], kvs.at[j, i, 3, TH[q]], kss.at[j, 8],
                           ksr.at[j, 6 + i, q], z_dn), hi & (z == 2))
            launch(rcopy(b4, kvs.at[j, i, 1], kss.at[j, 11], ksr.at[j, 1, i], z_up), hi & (z == 3))
        both = kvs.at[j, :, 0]
        owe(both, kss.at[j, 0], lo & low)
        owe(both, kss.at[j, 2], mid)
        owe(both, kss.at[j, 10], hi & (z == 3))
        owe(both, kss.at[j, 8], hi & (z == 2))
        owe(both, kss.at[j, 11], hi & (z == 3))

    def kv_third(j):
        low = z <= 1
        b = kvrl.at[j, 1]
        arrive(b, ksr.at[j, 5, 0], low)
        far = jnp.maximum(3 - z, 2)
        launch(rcopy(b, kvs.at[j, 0, far], kss.at[j, 7], ksr.at[j, far, 0], y_up), low & relay_k)
        launch(rcopy(b, kvs.at[j, 1, far], kss.at[j, 7], ksr.at[j, far, 1], y_dn), low & relay_v)
        owe(b, kss.at[j, 7], low)

    def kv_fourth(j, pieces=((0, 0), (0, 1), (1, 0), (1, 1))):
        cond = hi & (z == 1)
        for i, q in pieces:
            b3 = kvs.at[j, i, 3, TH[q]]
            arrive(b3, ksr.at[j, 6 + i, q], cond)
            launch(rcopy(b3, kvs.at[j, i, 2, TH[q]], kss.at[j, 9],
                         ksr.at[j, 8 + i, q], z_dn), cond)
        if (1, 1) in pieces:
            owe(kvs.at[j, :, 0], kss.at[j, 9], cond)


    def kv_near_in(j):
        for i in range(2):
            arrive(kvs.at[j, i, 1], ksr.at[j, 1, i], (z == 3) | (hi & (z == 0)))
            arrive(kvs.at[j, i, 3], ksr.at[j, 3, i], (z == 3) | (hi & (z != 1)))

    def kv_far_in(j):
        four = hi & (z == 0)
        for i in range(2):
            arrive(kvs.at[j, i, 2], ksr.at[j, 2, i], (z >= 2) | (hi & (z == 1)))
            for q in range(2):
                arrive(kvs.at[j, i, 2, TH[q]], ksr.at[j, 8 + i, q], four)

    def kv_finish(j):
        kv_near_in(j)
        kv_far_in(j)

    def project(j):
        cosine, sine = cos_ref[...], sin_ref[...]
        for load in loads[2 + 4 * j : 5 + 4 * j]:
            load.wait()
        xn = ag[j].reshape(TOK, D)
        q_gain, k_gain = gain(qg, j), gain(kg, j)
        kr = dot(xn, wk[j])
        kvs[j, 0, 0] = rope(kr * rms_of(kr) * k_gain, cosine, sine).astype(bf16)
        kvs[j, 1, 0] = dot(xn, wv[j]).astype(bf16)
        if j == BACK:
            kv_cross(j)
        kv_near(j)
        if j == BACK:
            kraw[...] = kr
        for h in range(2):
            qr = dot(xn, wq[j, :, h * HD : (h + 1) * HD])
            query = rope(qr * rms_of(qr) * q_gain, cosine, sine).astype(bf16)
            qs[j, h * TOK : (h + 1) * TOK] = query * jnp.asarray(HD ** -0.5, bf16)
            if j == BACK:
                qraw[h * TOK : (h + 1) * TOK] = qr

    def score(j, ci, d):
        sc = dot_nt(qs[j, chunk_rows(ci), :], kvs[j, 0, d])
        if d in (0, 4):
            ii = lax.broadcasted_iota(jnp.int32, (TOK, TOK), 0)
            ahead_by = ii - lax.broadcasted_iota(jnp.int32, (TOK, TOK), 1)
            if d == 0:
                return jnp.where(ahead_by >= 0, sc, masked_score)
            return jnp.where(ahead_by < jnp.where(p >= 4, 0, -TOK), sc, masked_score)
        return sc + jnp.where(p >= d, 0.0, masked_score)

    def top_of(scs):
        top = jnp.max(scs[0], axis=-1, keepdims=True)
        for sc in scs[1:]:
            top = jnp.maximum(top, jnp.max(sc, axis=-1, keepdims=True))
        return top

    def sum_of(es):
        total = es[0]
        for e in es[1:]:
            total = total + e
        return jnp.sum(total, axis=-1, keepdims=True)

    def chunk_rows(ci):
        return slice(ci * TOK, (ci + 1) * TOK)

    def weigh(j, ci, low):
        out = dot(low, kvs[j, 1].reshape(5 * TOK, HD)).astype(bf16)
        cx[j, :, :, ci * HD : (ci + 1) * HD] = out.reshape(8, ROWS, HD)

    near_blocks = (0, 1, 3, 4)

    def block_cols(d):
        return slice(d * TOK, (d + 1) * TOK)

    def attend_near():
        for ci in range(2):
            rows = chunk_rows(ci)
            scs = [score(BACK, ci, d) for d in near_blocks]
            top = top_of(scs)
            es = [jnp.exp(sc - top) for sc in scs]
            for d, e in zip(near_blocks, es):
                pw[rows, block_cols(d)] = e
            tops[rows, :] = top
            sums[rows, :] = sum_of(es)

    def attend_far():
        for ci in range(2):
            rows = chunk_rows(ci)
            sc = score(BACK, ci, 2)
            top = jnp.maximum(tops[rows, :], jnp.max(sc, axis=-1, keepdims=True))
            e = jnp.exp(sc - top)
            pw[rows, block_cols(2)] = e
            near = jnp.exp(tops[rows, :] - top)
            far = 1.0 / (sums[rows, :] * near + jnp.sum(e, axis=-1, keepdims=True))
            near = near * far
            tops[rows, :] = near
            sums[rows, :] = far
            lows = []
            for d in range(5):
                w = e * far if d == 2 else pw[rows, block_cols(d)] * near
                lows.append(w.astype(bf16))
                pl_s[rows, block_cols(d)] = lows[d]
            weigh(BACK, ci, jnp.concatenate(lows, axis=-1))

    def attention(j):
        for ci in range(2):
            scs = [score(j, ci, d) for d in range(5)]
            top = top_of(scs)
            es = [jnp.exp(sc - top) for sc in scs]
            inverse = 1.0 / sum_of(es)
            weigh(j, ci, jnp.concatenate([(e * inverse).astype(bf16) for e in es], axis=-1))

    def out_product(j):
        return lambda lhs, n: dot(lhs, wo[j, :, n * CW : (n + 1) * CW])

    def hidden_product(lhs, n):
        w_rows = slice(n * CW, (n + 1) * CW)
        total = hq[:, cols(n)] + dot_nt(lhs[:, 2 * HD : 3 * HD], wk[BACK, w_rows, :])
        return total + dot_nt(lhs[:, 3 * HD :], wv[BACK, w_rows, :])

    loads[0].wait()
    for load in small:
        load.wait()
    x_back = sti[plan[0, 1]].astype(f32)
    ag[BACK, t] = (x_back * rms_of(x_back) * gain(ig, BACK)).astype(bf16)
    pl.semaphore_wait(barrier, 8)
    gather_start(BACK)
    x_fwd = sti[plan[0, 0]].astype(f32)
    ag[FWD, t] = (x_fwd * rms_of(x_fwd) * gain(ig, FWD)).astype(bf16)
    for j in range(2):
        for d in range(1, 5):
            @pl.when((d > p) & (d + p != 3))
            def _():
                for i in range(2):
                    kvs[j, i, d] = jnp.zeros((TOK, HD), bf16)
    angles = (p * TOK + lax.broadcasted_iota(jnp.int32, (TOK, HD // 2), 0)).astype(f32)
    pair = lax.broadcasted_iota(jnp.int32, (1, HD // 2), 1).astype(f32)
    angles = angles * jnp.exp(pair * (-2.0 * math.log(rope_base) / HD))
    cos_ref[...] = jnp.cos(angles)
    sin_ref[...] = jnp.sin(angles)
    gather_relay(BACK)
    gather_start(FWD)
    gather_finish(BACK)
    project(BACK)
    gather_relay(FWD)
    kv_relay(BACK)
    gather_finish(FWD)
    kv_second(BACK)
    project(FWD)
    kv_fourth(BACK, ((0, 0),))
    kv_third(BACK)
    kv_cross(FWD)
    kv_fourth(BACK, ((0, 1), (1, 0), (1, 1)))
    kv_near_in(BACK)
    attend_near()
    kv_relay(FWD)
    kv_far_in(BACK)
    attend_far()
    loads[5].wait()
    scatter_first(BACK, out_product(BACK), rows_all(cx.at[BACK]),
                  lambda n: scatter_second(BACK, (n,)))
    scatter_second(BACK, range(NCH - 3, NCH))
    kv_second(FWD)
    scatter_relay(BACK)
    kv_third(FWD)
    kv_fourth(FWD)
    projected = scatter_finish(BACK)
    loads[1].wait()
    incoming = stg[plan[0, 1]].astype(f32)
    ag[GRAD, t] = rms_back(projected, incoming, gain(og, BACK)).astype(bf16)
    gather_start(GRAD)
    go[...] = sti[plan[0, 1]]
    fo[...] = stg[plan[0, 1]]
    ahead = (
        rcopy(go, xi_out.at[0], swap_s.at[2], swap_r.at[2], other),
        rcopy(fo, xi_out.at[1], swap_s.at[0], swap_r.at[0], other),
    )
    for copy in ahead:
        copy.start()
    kv_finish(FWD)
    attention(FWD)
    gather_relay(GRAD)
    loads[9].wait()
    scatter_first(FWD, out_product(FWD), rows_all(cx.at[FWD]))
    gather_finish(GRAD)

    og_rows = ag[GRAD].reshape(TOK, D)
    for h in range(2):
        cgs[h * TOK : (h + 1) * TOK] = dot_nt(
            og_rows, wo[BACK, h * HD : (h + 1) * HD, :]
        ).astype(bf16)
    q_gain, k_gain = gain(qg, BACK), gain(kg, BACK)

    R1, R2, R3, R4, R5 = 0, 1, 2, 3, 4
    OWN, ONE, FOUR = 0, 1, 2

    def grad_block(i, d):
        if i == 0:
            return dot_tn(dss[:, d * TOK : (d + 1) * TOK], qs[BACK])
        return dot_tn(pl_s[:, d * TOK : (d + 1) * TOK], cgs[...])

    def g_send(d, e, se, device, cond, i):
        send(rcopy(gs.at[i, d - 1], gr.at[e, i], gss.at[se, i], gsr.at[e, i], device), cond)

    def g_add(e, k, cond, i):
        arrive(gr.at[e, i], gsr.at[e, i], cond)

        @pl.when(cond)
        def _():
            gacc[i, k] = gacc[i, k] + gr[e, i].astype(f32)

    def g_cross(i, d, far, cond):
        for h, device in enumerate((y_dn, y_up)):
            send(rcopy(gs.at[i, d - 1, TH[h]], grr.at[far, i], gsc.at[far, i, h],
                       gcr.at[far, i], device), cond)

    def g_relay(i, far):
        cond = z <= 1 if far else None
        e = R5 if far else R4
        buf = grr.at[far, i]
        arrive(buf, gcr.at[far, i], cond)
        for h, (role, device) in enumerate(((relay_k, y_dn), (relay_v, y_up))):
            send(rcopy(buf, gr.at[e, i, TH[h]], gsx.at[far, i], gsh.at[far, i, h], device),
                 role & cond if far else role)

    def g_halves(i, far, cond):
        for h in range(2):
            arrive(gr.at[R5 if far else R4, i, TH[h]], gsh.at[far, i, h], cond)

    def g_forward(i):
        cond = lo & (z <= 1)
        g_halves(i, 1, cond)
        ahead_cond = cond if i else lo & (z == 1)
        send(rcopy(gr.at[R5, i], gr.at[R5, i], gss.at[7, i], gsr.at[R5, i], z_op), ahead_cond)
        if i == 0:
            for h in range(2):
                send(rcopy(gr.at[R5, 0, TH[h]], gr.at[R3, 0, TH[h]], gsz.at[h], gsy.at[0, h], z_up),
                     lo & (z == 0))

    def g_forward_again():
        cond = lo & (z == 1)
        for h in range(2):
            part = gr.at[R3, 0, TH[h]]
            arrive(part, gsy.at[0, h], cond)
            send(rcopy(part, gr.at[R5, 0, TH[h]], gsz.at[h], gsy.at[1, h], z_up), cond)

    def g_first(i):
        gs[i, 1] = grad_block(i, 2).astype(bf16)
        g_cross(i, 2, 1, hi & (z <= 1))
        g_send(2, R2, 0, z_dn, z >= 2, i)
        gs[i, 2] = grad_block(i, 3).astype(bf16)
        g_send(3, R3, 2, z_up, (z == 3) | hi, i)
        gacc[i, ONE] = grad_block(i, 1)
        gs[i, 0] = gacc[i, ONE].astype(bf16)
        g_send(1, R1, 3, z_dn, (z == 3) | (hi & (z == 0)), i)
        gacc[i, FOUR] = grad_block(i, 4)
        gacc[i, OWN] = grad_block(i, 0)

    def g_middle(i):
        g_add(R2, ONE, mid, i)

        @pl.when(mid)
        def _():
            gs[i, 0] = gacc[i, ONE].astype(bf16)
        g_send(1, R1, 3, z_dn, mid, i)

    def g_third(i):
        g_add(R3, FOUR, hi & (z >= 1), i)
        g_add(R1, FOUR, hi & (z == 3), i)
        gs[i, 3] = gacc[i, FOUR].astype(bf16)
        g_cross(i, 4, 0, hi)

    early = len(drains)
    g_first(1)

    for ci in range(2):
        rows = chunk_rows(ci)
        near, far = tops[rows, :], sums[rows, :]
        ws = [pw[rows, block_cols(d)] * (far if d == 2 else near) for d in range(5)]
        wgs = [dot_nt(cgs[rows, :], kvs[BACK, 1, d]) for d in range(5)]
        delta = sum_of([w * wg for w, wg in zip(ws, wgs)])
        for d in range(5):
            dss[rows, block_cols(d)] = (ws[d] * (wgs[d] - delta)).astype(bf16)

    g_first(0)
    g_middle(1)
    g_relay(1, 1)
    g_third(1)
    scatter_second(FWD)
    g_middle(0)
    g_relay(0, 1)
    g_third(0)

    for h in range(2):
        rows = slice(h * TOK, (h + 1) * TOK)
        dq = dot(dss[rows, :], kvs[BACK, 0].reshape(5 * TOK, HD)) * (HD ** -0.5)
        low = rms_back(
            qraw[rows], rope_back(dq, cos_ref[...], sin_ref[...]), q_gain
        ).astype(bf16)
        lq[:, :, h * HD : (h + 1) * HD] = low.reshape(8, ROWS, HD)
    query_low = rows_all(lq)[:, : 2 * HD]
    for n in range(NCH):
        hq[:, cols(n)] = dot_nt(query_low, wq[BACK, n * CW : (n + 1) * CW, :])

    g_forward(1)
    g_relay(1, 0)
    g_forward(0)
    scatter_relay(FWD)
    g_relay(0, 0)
    g_forward_again()
    for copy in ahead:
        copy.wait_send()
    flush(0, early)
    sent(0, 0, 6)
    sent(1, 0, 4)
    fwd_proj = scatter_finish(FWD)
    x_fwd = sti[plan[0, 0]].astype(f32)
    fo[...] = (x_fwd + fwd_proj * rms_of(fwd_proj) * gain(og, FWD)).astype(bf16)
    send(rcopy(fo, act_out, swap_s.at[1], swap_r.at[1], other))
    for i in (1, 0):
        g_add(R1, OWN, z < 3, i)
        g_add(R3, OWN, z == 0, i)
        g_halves(i, 0, lo)

        @pl.when(lo)
        def _():
            gacc[i, OWN] = gacc[i, OWN] + gr[R4, i].astype(f32)
        if i:
            g_add(R5, OWN, lo & (z >= 2), i)
        else:
            for h in range(2):
                arrive(gr.at[R5, 0, TH[h]], gsy.at[1, h], lo & (z == 2))
            arrive(gr.at[R5, 0], gsr.at[R5, 0], lo & (z == 3))

            @pl.when(lo & (z >= 2))
            def _():
                gacc[0, OWN] = gacc[0, OWN] + gr[R5, 0].astype(f32)
    key_low = rms_back(
        kraw[...], rope_back(gacc[0, 0], cos_ref[...], sin_ref[...]), k_gain
    ).astype(bf16)
    lq[:, :, 2 * HD : 3 * HD] = key_low.reshape(8, ROWS, HD)
    lq[:, :, 3 * HD :] = gacc[1, 0].astype(bf16).reshape(8, ROWS, HD)

    scatter_first(2, hidden_product, rows_all(lq), lambda n: scatter_second(2, (n,)))
    scatter_second(2, range(NCH - 3, NCH))
    scatter_relay(2)
    flush(0, len(drains))
    sent(1, 0, 6)
    sent(2, 0, 2)
    for n in range(NCH):
        hidden = scatter_part(2, n)
        gb[:, cols(n)] = (hidden * ig[pl.ds(legs[BACK], 1), cols(n)]).astype(bf16)
        send(rcopy(gb.at[:, cols(n)], g_out.at[:, cols(n)],
                   swap_s.at[3 + n], swap_r.at[3 + n], other))
    arrive(xi_out.at[0], swap_r.at[2])
    arrive(xi_out.at[1], swap_r.at[0])
    for n in range(NCH):
        arrive(g_out.at[:, cols(n)], swap_r.at[3 + n])
    arrive(act_out, swap_r.at[1])
    flush(0, len(drains))
    sent(2, 0, 6)


def hand_on(act_in, g_in, xi_in, act_out, grad_out, act, g, xi, lsem):
    ins = [
        pltpu.make_async_copy(src, dst, lsem.at[k])
        for k, (src, dst) in enumerate(((xi_in, xi), (g_in, g), (act_in, act)))
    ]
    outs = [
        pltpu.make_async_copy(src, dst, lsem.at[3 + k])
        for k, (src, dst) in enumerate(((act, act_out), (g, grad_out)))
    ]
    for copy in ins:
        copy.start()
    ins[0].wait()
    x = xi[0].astype(f32)
    scale = rms_of(x)
    ins[1].wait()
    grad = g[...].astype(f32)
    centred = grad - x * (scale * scale * jnp.mean(grad * x, axis=-1, keepdims=True))
    g[...] = (xi[1].astype(f32) + scale * centred).astype(bf16)
    outs[1].start()
    ins[2].wait()
    outs[0].start()
    for copy in outs:
        copy.wait()


def per_device(
    stash_inputs, stash_grads, plan, query_weight, key_weight, value_weight, out_weight,
    input_gain, output_gain, query_gain, key_gain,
):
    hbm = pl.BlockSpec(memory_space=pl.ANY)
    smem = pl.BlockSpec(memory_space=pltpu.SMEM)
    V = pltpu.VMEM
    sem = pltpu.SemaphoreType.DMA
    act, g, xi = pl.pallas_call(
        kernel,
        out_shape=(jax.ShapeDtypeStruct((ROWS, D), bf16),) * 2
        + (jax.ShapeDtypeStruct((2, ROWS, D), bf16),),
        in_specs=[smem] + [hbm] * 10,
        out_specs=(hbm,) * 3,
        scratch_shapes=[
            V((2, D, 2 * HD), bf16), V((2, D, HD), bf16), V((2, D, HD), bf16), V((2, 2 * HD, D), bf16),
            V((4, ROWS, D), bf16), V((4, ROWS, D), bf16),
            V((3, 8, ROWS, D), bf16),
            V((2, 2 * TOK, HD), bf16), V((2 * TOK, HD), f32), V((TOK, HD), f32),
            V((2, 2, 5, TOK, HD), bf16), V((2, 2, TOK, HD), bf16), V((2, 2, TOK // 2, HD), bf16),
            V((2, 8, ROWS, 2 * HD), bf16),
            V((2 * TOK, 5 * TOK), f32), V((2 * TOK, 5 * TOK), bf16), V((2 * TOK, 5 * TOK), bf16),
            V((2 * TOK, HD), bf16),
            V((4, ROWS, D), bf16), V((3, 4, ROWS, D), bf16), V((2, 3, ROWS, D), bf16),
            V((3, 2, ROWS // 2, D), bf16), V((3, 2, ROWS, D), bf16), V((2, ROWS, D), f32),
            V((2, 4, TOK, HD), bf16), V((5, 2, TOK, HD), bf16), V((2, 3, TOK, HD), f32),
            V((8, ROWS, 4 * HD), bf16),
            V((ROWS, D), bf16), V((ROWS, D), bf16), V((TOK, HD // 2), f32), V((TOK, HD // 2), f32),
            V((2 * 4 * ROWS, D), f32), V((ROWS, D), bf16),
            V((2, D), f32), V((2, D), f32), V((2, HD), f32), V((2, HD), f32),
            V((2 * TOK, 1), f32), V((2 * TOK, 1), f32),
            sem((15,)), sem((3,)), sem((3, 7)), sem((3, 7)), sem((3, NCH, 4)),
            sem((2, 12)), sem((2, 10, 2)), sem((8, 2)), sem((5, 2)),
            sem((2, 2, 2)), sem((2, 2)), sem((2, 2)), sem((2, 2, 2)), sem((2, 2)), sem((2,)), sem((3 + NCH,)), sem((3 + NCH,)),
        ],
        compiler_params=pltpu.CompilerParams(
            collective_id=0, has_side_effects=True, vmem_limit_bytes=67043328
        ),
    )(
        plan, input_gain[0], output_gain[0], query_gain[0],
        key_gain[0], stash_inputs[0], stash_grads[0], query_weight[0], key_weight[0],
        value_weight[0], out_weight[0],
    )
    act, grad = pl.pallas_call(
        hand_on,
        out_shape=(jax.ShapeDtypeStruct((ROWS, D), bf16),) * 2,
        in_specs=[hbm] * 3,
        out_specs=(hbm, hbm),
        scratch_shapes=[V((ROWS, D), bf16), V((ROWS, D), bf16), V((2, ROWS, D), bf16), sem((5,))],
    )(act, g, xi)
    return act[None], grad[None]


def solution(mesh):
    return jax.shard_map(
        per_device,
        mesh=mesh,
        in_specs=(
            P("segment", None, ("ctx", "tp"), None),
            P("segment", None, ("ctx", "tp"), None),
            P("segment", None),
            P("segment", None, None, "tp"),
            P("segment", None, None, "tp"),
            P("segment", None, None, "tp"),
            P("segment", None, "tp", None),
            P("segment", None, None),
            P("segment", None, None),
            P("segment", None, None),
            P("segment", None, None),
        ),
        out_specs=(P("segment", ("ctx", "tp"), None), P("segment", ("ctx", "tp"), None)),
        check_vma=False,
    )
```

```python
import math

import jax
import jax.numpy as jnp
from jax import lax
from jax.experimental import pallas as pl
from jax.experimental.pallas import tpu as pltpu
from jax.sharding import PartitionSpec as P

WINDOW = 1024
epsilon = 1e-06
rope_base = 10000.0
masked_score = -1e30

D = 3840
ROWS = 32
TOK = 256
HD = 256
NCH = 6
CW = D // NCH
BACK, FWD, GRAD = 0, 1, 2
f32 = jnp.float32
bf16 = jnp.bfloat16
MESH = pl.DeviceIdType.MESH


def dot(a, b):
    return lax.dot_general(a, b, (((1,), (0,)), ((), ())), preferred_element_type=f32)


def dot_nt(a, b):
    return lax.dot_general(a, b, (((1,), (1,)), ((), ())), preferred_element_type=f32)


def dot_tn(a, b):
    return lax.dot_general(a, b, (((0,), (0,)), ((), ())), preferred_element_type=f32)


def rms_of(x):
    return lax.rsqrt(jnp.mean(x * x, axis=-1, keepdims=True) + epsilon)


def rms_back(x, grad, gain):
    g = grad * gain
    r = rms_of(x)
    return r * (g - x * (r * r * jnp.mean(g * x, axis=-1, keepdims=True)))


def rope(y, cosine, sine):
    a, b = y[:, : HD // 2], y[:, HD // 2 :]
    return jnp.concatenate([a * cosine - b * sine, b * cosine + a * sine], axis=-1)


def rope_back(g, cosine, sine):
    a, b = g[:, : HD // 2], g[:, HD // 2 :]
    return jnp.concatenate([a * cosine + b * sine, b * cosine - a * sine], axis=-1)


def kernel(
    plan, ig_h, og_h, qg_h, kg_h, si, sg, wq_h, wk_h, wv_h, wo_h,
    act_out, g_out, xi_out,
    wq, wk, wv, wo, sti, stg, ag, qs, qraw, kraw, kvs, kvrl, grr, cx, pw, pl_s, dss, cgs,
    ps, pr, sb, rl, fr, own, gs, gr, gacc, lq, fo, go, cos_ref, sin_ref, hq, gb, ig, og, qg, kg, tops, sums,
    lsem, ags, agr, rss, rsr, kss, ksr, gss, gsr, gsc, gcr, gsx, gsh, gsy, gsz, swap_s, swap_r,
):
    s = lax.axis_index("segment")
    p = lax.axis_index("ctx")
    t = lax.axis_index("tp")
    yh, z = p // 4, p % 4
    y = 2 * yh + s
    x, c = t // 2, t % 2
    legs = (1 - s, s)

    def dev(s_=None, p_=None, t_=None):
        return {
            "segment": s if s_ is None else s_,
            "ctx": p if p_ is None else p_,
            "tp": t if t_ is None else t_,
        }

    t_r, t_l = ((x + 1) % 4) * 2 + c, ((x + 3) % 4) * 2 + c
    t_o = ((x + 2) % 4) * 2 + c
    t_p = 2 * x + 1 - c
    right, left, partner = dev(t_=t_r), dev(t_=t_l), dev(t_=t_p)
    z_up, z_dn = dev(p_=4 * yh + (z + 1) % 4), dev(p_=4 * yh + (z + 3) % 4)
    z_op = dev(p_=4 * yh + (z + 2) % 4)
    y_u, y_d = (y + 1) % 4, (y + 3) % 4
    y_up = dev(s_=y_u % 2, p_=(y_u // 2) * 4 + z)
    y_dn = dev(s_=y_d % 2, p_=(y_d // 2) * 4 + z)
    other = dev(s_=1 - s)

    barrier = pltpu.get_barrier_semaphore()
    for device in (right, left, partner, z_up, z_dn, z_op, y_up, y_dn):
        pl.semaphore_signal(barrier, inc=1, device_id=device, device_id_type=MESH)

    loads = [
        pltpu.make_async_copy(si, sti, lsem.at[0]),
        pltpu.make_async_copy(sg, stg, lsem.at[1]),
    ]
    for j in range(2):
        loads += [
            pltpu.make_async_copy(wq_h.at[legs[j]], wq.at[j], lsem.at[2 + 4 * j]),
            pltpu.make_async_copy(wk_h.at[legs[j]], wk.at[j], lsem.at[3 + 4 * j]),
            pltpu.make_async_copy(wv_h.at[legs[j]], wv.at[j], lsem.at[4 + 4 * j]),
            pltpu.make_async_copy(wo_h.at[legs[j]], wo.at[j], lsem.at[5 + 4 * j]),
        ]
    small = [
        pltpu.make_async_copy(src, dst, lsem.at[11 + k])
        for k, (src, dst) in enumerate(((ig_h, ig), (og_h, og), (qg_h, qg), (kg_h, kg)))
    ]
    for load in loads[:1] + small + loads[1:]:
        load.start()

    def gain(ref, j):
        return ref[pl.ds(legs[j], 1), :]

    def rcopy(src, dst, ssem, rsem, device):
        return pltpu.make_async_remote_copy(
            src_ref=src, dst_ref=dst, send_sem=ssem, recv_sem=rsem,
            device_id=device, device_id_type=MESH,
        )

    drains = []

    def when(cond, run):
        if cond is None:
            run()
        else:
            pl.when(cond)(run)

    def send(copy, cond=None):
        when(cond, copy.start)
        drains.append((copy, cond))

    def launch(copy, cond=None):
        when(cond, copy.start)

    def owe(ref, ssem, cond=None):
        drains.append((rcopy(ref, ref, ssem, swap_r.at[0], partner), cond))

    def flush(first, last):
        groups = {}
        for copy, cond in drains[first:last]:
            groups.setdefault(id(cond), (cond, []))[1].append(copy)
        for cond, copies in groups.values():
            def run(copies=copies):
                for copy in copies:
                    copy.wait_send()
            when(cond, run)
        del drains[first:last]

    def arrive(dst, rsem, cond=None):
        copy = rcopy(dst, dst, swap_s.at[0], rsem, partner)
        when(cond, copy.wait_recv)

    H0, H1 = pl.ds(0, ROWS // 2), pl.ds(ROWS // 2, ROWS // 2)
    halves = (H0, H1)

    def gather_start(j):
        blk = ag.at[j, t]
        launch(rcopy(blk.at[H0], blk.at[H0], ags.at[j], agr.at[j, 0], right))
        launch(rcopy(blk.at[H1], blk.at[H1], ags.at[j], agr.at[j, 1], left))
        launch(rcopy(blk.at[H1], blk.at[H1], ags.at[j], agr.at[j, 2], right))
        launch(rcopy(blk.at[H0], blk.at[H0], ags.at[j], agr.at[j, 3], left))
        launch(rcopy(blk, blk, ags.at[j], agr.at[j, 6], partner))

    def across(j, place, half):
        part = ag.at[j, place, halves[half]]
        launch(rcopy(part, part, ags.at[j], agr.at[j, 6], partner))

    def gather_relay(j):
        a = ag.at[j, t_l, H0]
        arrive(a, agr.at[j, 0])
        launch(rcopy(a, a, ags.at[j], agr.at[j, 4], right))
        b = ag.at[j, t_r, H1]
        arrive(b, agr.at[j, 1])
        launch(rcopy(b, b, ags.at[j], agr.at[j, 5], left))
        across(j, t_l, 0)
        across(j, t_r, 1)

    def gather_finish(j):
        arrive(ag.at[j, t_l, H1], agr.at[j, 2])
        across(j, t_l, 1)
        arrive(ag.at[j, t_r, H0], agr.at[j, 3])
        across(j, t_r, 0)
        arrive(ag.at[j, t_o, H0], agr.at[j, 4])
        across(j, t_o, 0)
        arrive(ag.at[j, t_o, H1], agr.at[j, 5])
        across(j, t_o, 1)
        arrive(ag.at[j, pl.ds(0, 4)], agr.at[j, 6])
        owe(ag.at[j, pl.ds(0, 7)], ags.at[j])

    def cols(n):
        return pl.ds(n * CW, CW)

    def rows_of(ref, parity):
        parts = [ref[2 * ((x + k) % 4) + parity] for k in range(4)]
        return jnp.concatenate(parts, axis=0)

    def rows_all(ref):
        return jnp.concatenate([rows_of(ref, 1 - c), rows_of(ref, c)], axis=0)

    def sent(r, first, last):
        b = r % 2
        parts = (
            ps, sb.at[b, 1, H0], sb.at[b, 1, H1], sb.at[b, 0, H1],
            sb.at[b, 2, H0], sb.at[b, 0, H0], sb.at[b, 2, H1],
        )
        for i in range(first, last + 1):
            if (r, i) in flying:
                flying.remove((r, i))
                rcopy(parts[i], parts[i], rss.at[r, i], swap_r.at[0], partner).wait_send()

    flying = set()

    def send_sum(r, i, copy):
        copy.start()
        flying.add((r, i))

    def scatter_first(r, product, lhs, then=None):
        if r:
            sent(r - 1, 0, 0)
        for n in range(NCH):
            if then and n >= 3:
                then(n - 3)
            total = product(lhs, n)
            ps[:, :, cols(n)] = total[: 4 * ROWS].astype(bf16).reshape(4, ROWS, CW)
            send_sum(r, 0, rcopy(ps.at[:, :, cols(n)], pr.at[r, :, :, cols(n)],
                       rss.at[r, 0], rsr.at[r, n, 0], partner))
            hq[4 * ROWS :, cols(n)] = total[4 * ROWS :]

    def send_direct(r, n):
        send_sum(r, 3, rcopy(sb.at[r % 2, 0, H1, cols(n)], fr.at[r, 0, H1, cols(n)],
                             rss.at[r, 3], rsr.at[r, n, 3], right))
        send_sum(r, 4, rcopy(sb.at[r % 2, 2, H0, cols(n)], fr.at[r, 1, H0, cols(n)],
                             rss.at[r, 4], rsr.at[r, n, 3], left))

    def scatter_second(r, numbers=range(NCH)):
        if r == 2 and 0 in numbers:
            sent(0, 1, 6)
        for n in numbers:
            arrive(pr.at[r, :, :, cols(n)], rsr.at[r, n, 0])
            total = hq[4 * ROWS :, cols(n)].reshape(4, ROWS, CW) + pr[r, :, :, cols(n)].astype(f32)
            own[r % 2, :, cols(n)] = total[0]
            sb[r % 2, :, :, cols(n)] = total[1:].astype(bf16)
            send_sum(r, 1, rcopy(sb.at[r % 2, 1, H0, cols(n)], rl.at[r, 0, :, cols(n)],
                       rss.at[r, 1], rsr.at[r, n, 1], right))
            send_sum(r, 2, rcopy(sb.at[r % 2, 1, H1, cols(n)], rl.at[r, 1, :, cols(n)],
                       rss.at[r, 2], rsr.at[r, n, 2], left))
            if r == 1:
                send_direct(r, n)

    def scatter_relay(r):
        for n in range(NCH):
            arrive(rl.at[r, 0, :, cols(n)], rsr.at[r, n, 1])
            sb[r % 2, 0, H0, cols(n)] = (
                sb[r % 2, 0, H0, cols(n)].astype(f32) + rl[r, 0, :, cols(n)].astype(f32)
            ).astype(bf16)
            send_sum(r, 5, rcopy(sb.at[r % 2, 0, H0, cols(n)], fr.at[r, 0, H0, cols(n)],
                       rss.at[r, 5], rsr.at[r, n, 3], right))
            arrive(rl.at[r, 1, :, cols(n)], rsr.at[r, n, 2])
            sb[r % 2, 2, H1, cols(n)] = (
                sb[r % 2, 2, H1, cols(n)].astype(f32) + rl[r, 1, :, cols(n)].astype(f32)
            ).astype(bf16)
            send_sum(r, 6, rcopy(sb.at[r % 2, 2, H1, cols(n)], fr.at[r, 1, H1, cols(n)],
                       rss.at[r, 6], rsr.at[r, n, 3], left))
            if r != 1:
                send_direct(r, n)

    def scatter_part(r, n):
        arrive(fr.at[r, :, :, cols(n)], rsr.at[r, n, 3])
        return own[r % 2, :, cols(n)] + (
            fr[r, 0, :, cols(n)].astype(f32) + fr[r, 1, :, cols(n)].astype(f32)
        )

    def scatter_finish(r):
        return jnp.concatenate([scatter_part(r, n) for n in range(NCH)], axis=-1)

    hi, lo = yh == 1, yh == 0
    mid = (z == 1) | (z == 2)

    relay_k = (y == 1) | (y == 2)
    relay_v = (y == 0) | (y == 3)

    TH = (pl.ds(0, TOK // 2), pl.ds(TOK // 2, TOK // 2))

    def kv_near(j):
        for i in range(2):
            o = kvs.at[j, i, 0]
            launch(rcopy(o, kvs.at[j, i, 1], kss.at[j, 1], ksr.at[j, 1, i], z_up), z < 3)
            launch(rcopy(o, kvs.at[j, i, 3], kss.at[j, 3], ksr.at[j, 3, i], z_dn), z == 0)
            launch(rcopy(o, kvs.at[j, i, 2], kss.at[j, 5], ksr.at[j, 2, i], z_op), lo & (z == 3))
            launch(rcopy(o, kvs.at[j, i, 3], kss.at[j, 3], ksr.at[j, 3, i], z_dn), lo & (z == 1))
        both = kvs.at[j, :, 0]
        owe(both, kss.at[j, 1], z < 3)
        owe(both, kss.at[j, 3], (z == 0) | (lo & (z == 1)))
        owe(both, kss.at[j, 5], lo & (z == 3))

    def kv_cross(j):
        k, v = kvs.at[j, 0, 0], kvs.at[j, 1, 0]
        launch(rcopy(k, kvrl.at[j, 0], kss.at[j, 6], ksr.at[j, 0, 0], y_up), lo)
        launch(rcopy(v, kvrl.at[j, 0], kss.at[j, 6], ksr.at[j, 0, 0], y_dn), lo)
        owe(kvs.at[j, :, 0], kss.at[j, 6], lo)

    def kv_relay(j):
        b = kvrl.at[j, 0]
        arrive(b, ksr.at[j, 0, 0])
        launch(rcopy(b, kvs.at[j, 0, 4], kss.at[j, 4], ksr.at[j, 4, 0], y_up), relay_k)
        launch(rcopy(b, kvs.at[j, 1, 4], kss.at[j, 4], ksr.at[j, 4, 1], y_dn), relay_v)
        owe(b, kss.at[j, 4])

    def kv_second(j):
        low = z <= 1
        far = jnp.maximum(3 - z, 2)
        for i in range(2):
            b1, b2, b4 = (kvs.at[j, i, d] for d in (1, far, 4))
            arrive(b2, ksr.at[j, far, i], lo & low)
            launch(rcopy(b2, kvrl.at[j, 1], kss.at[j, 0], ksr.at[j, 5, 0],
                       y_dn if i else y_up), lo & low)
            arrive(b1, ksr.at[j, 1, i], mid)
            launch(rcopy(b1, kvs.at[j, i, 2], kss.at[j, 2], ksr.at[j, 2, i], z_up), mid)
            arrive(b4, ksr.at[j, 4, i], hi)
            launch(rcopy(b4, kvs.at[j, i, 3], kss.at[j, 10], ksr.at[j, 3, i], z_dn), hi & (z == 3))
            for q in range(2):
                launch(rcopy(b4.at[TH[q]], kvs.at[j, i, 3, TH[q]], kss.at[j, 8],
                           ksr.at[j, 6 + i, q], z_dn), hi & (z == 2))
            launch(rcopy(b4, kvs.at[j, i, 1], kss.at[j, 11], ksr.at[j, 1, i], z_up), hi & (z == 3))
        both = kvs.at[j, :, 0]
        owe(both, kss.at[j, 0], lo & low)
        owe(both, kss.at[j, 2], mid)
        owe(both, kss.at[j, 10], hi & (z == 3))
        owe(both, kss.at[j, 8], hi & (z == 2))
        owe(both, kss.at[j, 11], hi & (z == 3))

    def kv_third(j):
        low = z <= 1
        b = kvrl.at[j, 1]
        arrive(b, ksr.at[j, 5, 0], low)
        far = jnp.maximum(3 - z, 2)
        launch(rcopy(b, kvs.at[j, 0, far], kss.at[j, 7], ksr.at[j, far, 0], y_up), low & relay_k)
        launch(rcopy(b, kvs.at[j, 1, far], kss.at[j, 7], ksr.at[j, far, 1], y_dn), low & relay_v)
        owe(b, kss.at[j, 7], low)

    def kv_fourth(j, pieces=((0, 0), (0, 1), (1, 0), (1, 1))):
        cond = hi & (z == 1)
        for i, q in pieces:
            b3 = kvs.at[j, i, 3, TH[q]]
            arrive(b3, ksr.at[j, 6 + i, q], cond)
            launch(rcopy(b3, kvs.at[j, i, 2, TH[q]], kss.at[j, 9],
                         ksr.at[j, 8 + i, q], z_dn), cond)
        if (1, 1) in pieces:
            owe(kvs.at[j, :, 0], kss.at[j, 9], cond)


    def kv_near_in(j):
        for i in range(2):
            arrive(kvs.at[j, i, 1], ksr.at[j, 1, i], (z == 3) | (hi & (z == 0)))
            arrive(kvs.at[j, i, 3], ksr.at[j, 3, i], (z == 3) | (hi & (z != 1)))

    def kv_far_in(j):
        four = hi & (z == 0)
        for i in range(2):
            arrive(kvs.at[j, i, 2], ksr.at[j, 2, i], (z >= 2) | (hi & (z == 1)))
            for q in range(2):
                arrive(kvs.at[j, i, 2, TH[q]], ksr.at[j, 8 + i, q], four)

    def kv_finish(j):
        kv_near_in(j)
        kv_far_in(j)

    def project(j):
        cosine, sine = cos_ref[...], sin_ref[...]
        for load in loads[2 + 4 * j : 5 + 4 * j]:
            load.wait()
        xn = ag[j].reshape(TOK, D)
        q_gain, k_gain = gain(qg, j), gain(kg, j)
        kr = dot(xn, wk[j])
        kvs[j, 0, 0] = rope(kr * rms_of(kr) * k_gain, cosine, sine).astype(bf16)
        kvs[j, 1, 0] = dot(xn, wv[j]).astype(bf16)
        if j == BACK:
            kv_cross(j)
        kv_near(j)
        if j == BACK:
            kraw[...] = kr
        for h in range(2):
            qr = dot(xn, wq[j, :, h * HD : (h + 1) * HD])
            query = rope(qr * rms_of(qr) * q_gain, cosine, sine).astype(bf16)
            qs[j, h * TOK : (h + 1) * TOK] = query * jnp.asarray(HD ** -0.5, bf16)
            if j == BACK:
                qraw[h * TOK : (h + 1) * TOK] = qr

    def score(j, ci, d):
        sc = dot_nt(qs[j, chunk_rows(ci), :], kvs[j, 0, d])
        if d in (0, 4):
            ii = lax.broadcasted_iota(jnp.int32, (TOK, TOK), 0)
            ahead_by = ii - lax.broadcasted_iota(jnp.int32, (TOK, TOK), 1)
            if d == 0:
                return jnp.where(ahead_by >= 0, sc, masked_score)
            return jnp.where(ahead_by < jnp.where(p >= 4, 0, -TOK), sc, masked_score)
        return sc + jnp.where(p >= d, 0.0, masked_score)

    def top_of(scs):
        top = jnp.max(scs[0], axis=-1, keepdims=True)
        for sc in scs[1:]:
            top = jnp.maximum(top, jnp.max(sc, axis=-1, keepdims=True))
        return top

    def sum_of(es):
        total = es[0]
        for e in es[1:]:
            total = total + e
        return jnp.sum(total, axis=-1, keepdims=True)

    def chunk_rows(ci):
        return slice(ci * TOK, (ci + 1) * TOK)

    def weigh(j, ci, low):
        out = dot(low, kvs[j, 1].reshape(5 * TOK, HD)).astype(bf16)
        cx[j, :, :, ci * HD : (ci + 1) * HD] = out.reshape(8, ROWS, HD)

    near_blocks = (0, 1, 3, 4)

    def block_cols(d):
        return slice(d * TOK, (d + 1) * TOK)

    def attend_near():
        for ci in range(2):
            rows = chunk_rows(ci)
            scs = [score(BACK, ci, d) for d in near_blocks]
            top = top_of(scs)
            es = [jnp.exp(sc - top) for sc in scs]
            for d, e in zip(near_blocks, es):
                pw[rows, block_cols(d)] = e
            tops[rows, :] = top
            sums[rows, :] = sum_of(es)

    def attend_far():
        for ci in range(2):
            rows = chunk_rows(ci)
            sc = score(BACK, ci, 2)
            top = jnp.maximum(tops[rows, :], jnp.max(sc, axis=-1, keepdims=True))
            e = jnp.exp(sc - top)
            pw[rows, block_cols(2)] = e
            near = jnp.exp(tops[rows, :] - top)
            far = 1.0 / (sums[rows, :] * near + jnp.sum(e, axis=-1, keepdims=True))
            near = near * far
            tops[rows, :] = near
            sums[rows, :] = far
            lows = []
            for d in range(5):
                w = e * far if d == 2 else pw[rows, block_cols(d)] * near
                lows.append(w.astype(bf16))
                pl_s[rows, block_cols(d)] = lows[d]
            weigh(BACK, ci, jnp.concatenate(lows, axis=-1))

    def attention(j):
        for ci in range(2):
            scs = [score(j, ci, d) for d in range(5)]
            top = top_of(scs)
            es = [jnp.exp(sc - top) for sc in scs]
            inverse = 1.0 / sum_of(es)
            weigh(j, ci, jnp.concatenate([(e * inverse).astype(bf16) for e in es], axis=-1))

    def out_product(j):
        return lambda lhs, n: dot(lhs, wo[j, :, n * CW : (n + 1) * CW])

    def hidden_product(lhs, n):
        w_rows = slice(n * CW, (n + 1) * CW)
        total = hq[:, cols(n)] + dot_nt(lhs[:, 2 * HD : 3 * HD], wk[BACK, w_rows, :])
        return total + dot_nt(lhs[:, 3 * HD :], wv[BACK, w_rows, :])

    loads[0].wait()
    for load in small:
        load.wait()
    x_back = sti[plan[0, 1]].astype(f32)
    ag[BACK, t] = (x_back * rms_of(x_back) * gain(ig, BACK)).astype(bf16)
    pl.semaphore_wait(barrier, 8)
    gather_start(BACK)
    x_fwd = sti[plan[0, 0]].astype(f32)
    ag[FWD, t] = (x_fwd * rms_of(x_fwd) * gain(ig, FWD)).astype(bf16)
    for j in range(2):
        for d in range(1, 5):
            @pl.when((d > p) & (d + p != 3))
            def _():
                for i in range(2):
                    kvs[j, i, d] = jnp.zeros((TOK, HD), bf16)
    angles = (p * TOK + lax.broadcasted_iota(jnp.int32, (TOK, HD // 2), 0)).astype(f32)
    pair = lax.broadcasted_iota(jnp.int32, (1, HD // 2), 1).astype(f32)
    angles = angles * jnp.exp(pair * (-2.0 * math.log(rope_base) / HD))
    cos_ref[...] = jnp.cos(angles)
    sin_ref[...] = jnp.sin(angles)
    gather_relay(BACK)
    gather_start(FWD)
    gather_finish(BACK)
    project(BACK)
    gather_relay(FWD)
    kv_relay(BACK)
    gather_finish(FWD)
    kv_second(BACK)
    project(FWD)
    kv_fourth(BACK, ((0, 0),))
    kv_third(BACK)
    kv_cross(FWD)
    kv_fourth(BACK, ((0, 1), (1, 0), (1, 1)))
    kv_near_in(BACK)
    attend_near()
    kv_relay(FWD)
    kv_far_in(BACK)
    attend_far()
    loads[5].wait()
    scatter_first(BACK, out_product(BACK), rows_all(cx.at[BACK]),
                  lambda n: scatter_second(BACK, (n,)))
    scatter_second(BACK, range(NCH - 3, NCH))
    kv_second(FWD)
    scatter_relay(BACK)
    kv_third(FWD)
    kv_fourth(FWD)
    projected = scatter_finish(BACK)
    loads[1].wait()
    incoming = stg[plan[0, 1]].astype(f32)
    ag[GRAD, t] = rms_back(projected, incoming, gain(og, BACK)).astype(bf16)
    gather_start(GRAD)
    go[...] = sti[plan[0, 1]]
    fo[...] = stg[plan[0, 1]]
    ahead = (
        rcopy(go, xi_out.at[0], swap_s.at[2], swap_r.at[2], other),
        rcopy(fo, xi_out.at[1], swap_s.at[0], swap_r.at[0], other),
    )
    for copy in ahead:
        copy.start()
    kv_finish(FWD)
    attention(FWD)
    gather_relay(GRAD)
    loads[9].wait()
    scatter_first(FWD, out_product(FWD), rows_all(cx.at[FWD]))
    gather_finish(GRAD)

    og_rows = ag[GRAD].reshape(TOK, D)
    for h in range(2):
        cgs[h * TOK : (h + 1) * TOK] = dot_nt(
            og_rows, wo[BACK, h * HD : (h + 1) * HD, :]
        ).astype(bf16)
    q_gain, k_gain = gain(qg, BACK), gain(kg, BACK)

    R1, R2, R3, R4, R5 = 0, 1, 2, 3, 4
    OWN, ONE, FOUR = 0, 1, 2

    def grad_block(i, d):
        if i == 0:
            return dot_tn(dss[:, d * TOK : (d + 1) * TOK], qs[BACK])
        return dot_tn(pl_s[:, d * TOK : (d + 1) * TOK], cgs[...])

    def g_send(d, e, se, device, cond, i):
        send(rcopy(gs.at[i, d - 1], gr.at[e, i], gss.at[se, i], gsr.at[e, i], device), cond)

    def g_add(e, k, cond, i):
        arrive(gr.at[e, i], gsr.at[e, i], cond)

        @pl.when(cond)
        def _():
            gacc[i, k] = gacc[i, k] + gr[e, i].astype(f32)

    def g_cross(i, d, far, cond):
        for h, device in enumerate((y_dn, y_up)):
            send(rcopy(gs.at[i, d - 1, TH[h]], grr.at[far, i], gsc.at[far, i, h],
                       gcr.at[far, i], device), cond)

    def g_relay(i, far):
        cond = z <= 1 if far else None
        e = R5 if far else R4
        buf = grr.at[far, i]
        arrive(buf, gcr.at[far, i], cond)
        for h, (role, device) in enumerate(((relay_k, y_dn), (relay_v, y_up))):
            send(rcopy(buf, gr.at[e, i, TH[h]], gsx.at[far, i], gsh.at[far, i, h], device),
                 role & cond if far else role)

    def g_halves(i, far, cond):
        for h in range(2):
            arrive(gr.at[R5 if far else R4, i, TH[h]], gsh.at[far, i, h], cond)

    def g_forward(i):
        cond = lo & (z <= 1)
        g_halves(i, 1, cond)
        ahead_cond = cond if i else lo & (z == 1)
        send(rcopy(gr.at[R5, i], gr.at[R5, i], gss.at[7, i], gsr.at[R5, i], z_op), ahead_cond)
        if i == 0:
            for h in range(2):
                send(rcopy(gr.at[R5, 0, TH[h]], gr.at[R3, 0, TH[h]], gsz.at[h], gsy.at[0, h], z_up),
                     lo & (z == 0))

    def g_forward_again():
        cond = lo & (z == 1)
        for h in range(2):
            part = gr.at[R3, 0, TH[h]]
            arrive(part, gsy.at[0, h], cond)
            send(rcopy(part, gr.at[R5, 0, TH[h]], gsz.at[h], gsy.at[1, h], z_up), cond)

    def g_first(i):
        gs[i, 1] = grad_block(i, 2).astype(bf16)
        g_cross(i, 2, 1, hi & (z <= 1))
        g_send(2, R2, 0, z_dn, z >= 2, i)
        gs[i, 2] = grad_block(i, 3).astype(bf16)
        g_send(3, R3, 2, z_up, (z == 3) | hi, i)
        gacc[i, ONE] = grad_block(i, 1)
        gs[i, 0] = gacc[i, ONE].astype(bf16)
        g_send(1, R1, 3, z_dn, (z == 3) | (hi & (z == 0)), i)
        gacc[i, FOUR] = grad_block(i, 4)
        gacc[i, OWN] = grad_block(i, 0)

    def g_middle(i):
        g_add(R2, ONE, mid, i)

        @pl.when(mid)
        def _():
            gs[i, 0] = gacc[i, ONE].astype(bf16)
        g_send(1, R1, 3, z_dn, mid, i)

    def g_third(i):
        g_add(R3, FOUR, hi & (z >= 1), i)
        g_add(R1, FOUR, hi & (z == 3), i)
        gs[i, 3] = gacc[i, FOUR].astype(bf16)
        g_cross(i, 4, 0, hi)

    early = len(drains)
    g_first(1)

    for ci in range(2):
        rows = chunk_rows(ci)
        near, far = tops[rows, :], sums[rows, :]
        ws = [pw[rows, block_cols(d)] * (far if d == 2 else near) for d in range(5)]
        wgs = [dot_nt(cgs[rows, :], kvs[BACK, 1, d]) for d in range(5)]
        delta = sum_of([w * wg for w, wg in zip(ws, wgs)])
        for d in range(5):
            dss[rows, block_cols(d)] = (ws[d] * (wgs[d] - delta)).astype(bf16)

    g_first(0)
    g_middle(1)
    g_relay(1, 1)
    g_third(1)
    scatter_second(FWD)
    g_middle(0)
    g_relay(0, 1)
    g_third(0)

    for h in range(2):
        rows = slice(h * TOK, (h + 1) * TOK)
        dq = dot(dss[rows, :], kvs[BACK, 0].reshape(5 * TOK, HD)) * (HD ** -0.5)
        low = rms_back(
            qraw[rows], rope_back(dq, cos_ref[...], sin_ref[...]), q_gain
        ).astype(bf16)
        lq[:, :, h * HD : (h + 1) * HD] = low.reshape(8, ROWS, HD)
    query_low = rows_all(lq)[:, : 2 * HD]
    for n in range(NCH):
        hq[:, cols(n)] = dot_nt(query_low, wq[BACK, n * CW : (n + 1) * CW, :])

    g_forward(1)
    g_relay(1, 0)
    g_forward(0)
    scatter_relay(FWD)
    g_relay(0, 0)
    g_forward_again()
    for copy in ahead:
        copy.wait_send()
    flush(0, early)
    sent(0, 0, 6)
    sent(1, 0, 4)
    fwd_proj = scatter_finish(FWD)
    x_fwd = sti[plan[0, 0]].astype(f32)
    fo[...] = (x_fwd + fwd_proj * rms_of(fwd_proj) * gain(og, FWD)).astype(bf16)
    send(rcopy(fo, act_out, swap_s.at[1], swap_r.at[1], other))
    for i in (1, 0):
        g_add(R1, OWN, z < 3, i)
        g_add(R3, OWN, z == 0, i)
        g_halves(i, 0, lo)

        @pl.when(lo)
        def _():
            gacc[i, OWN] = gacc[i, OWN] + gr[R4, i].astype(f32)
        if i:
            g_add(R5, OWN, lo & (z >= 2), i)
        else:
            for h in range(2):
                arrive(gr.at[R5, 0, TH[h]], gsy.at[1, h], lo & (z == 2))
            arrive(gr.at[R5, 0], gsr.at[R5, 0], lo & (z == 3))

            @pl.when(lo & (z >= 2))
            def _():
                gacc[0, OWN] = gacc[0, OWN] + gr[R5, 0].astype(f32)
    key_low = rms_back(
        kraw[...], rope_back(gacc[0, 0], cos_ref[...], sin_ref[...]), k_gain
    ).astype(bf16)
    lq[:, :, 2 * HD : 3 * HD] = key_low.reshape(8, ROWS, HD)
    lq[:, :, 3 * HD :] = gacc[1, 0].astype(bf16).reshape(8, ROWS, HD)

    scatter_first(2, hidden_product, rows_all(lq), lambda n: scatter_second(2, (n,)))
    scatter_second(2, range(NCH - 3, NCH))
    scatter_relay(2)
    flush(0, len(drains))
    sent(1, 0, 6)
    sent(2, 0, 2)
    for n in range(NCH):
        hidden = scatter_part(2, n)
        gb[:, cols(n)] = (hidden * ig[pl.ds(legs[BACK], 1), cols(n)]).astype(bf16)
        send(rcopy(gb.at[:, cols(n)], g_out.at[:, cols(n)],
                   swap_s.at[3 + n], swap_r.at[3 + n], other))
    arrive(xi_out.at[0], swap_r.at[2])
    arrive(xi_out.at[1], swap_r.at[0])
    for n in range(NCH):
        arrive(g_out.at[:, cols(n)], swap_r.at[3 + n])
    arrive(act_out, swap_r.at[1])
    flush(0, len(drains))
    sent(2, 0, 6)


def hand_on(act_in, g_in, xi_in, act_out, grad_out, act, g, xi, lsem):
    ins = [
        pltpu.make_async_copy(src, dst, lsem.at[k])
        for k, (src, dst) in enumerate(((xi_in, xi), (g_in, g), (act_in, act)))
    ]
    outs = [
        pltpu.make_async_copy(src, dst, lsem.at[3 + k])
        for k, (src, dst) in enumerate(((act, act_out), (g, grad_out)))
    ]
    for copy in ins:
        copy.start()
    ins[0].wait()
    ins[2].wait()
    outs[0].start()
    x = xi[0].astype(f32)
    scale = rms_of(x)
    ins[1].wait()
    grad = g[...].astype(f32)
    centred = grad - x * (scale * scale * jnp.mean(grad * x, axis=-1, keepdims=True))
    g[...] = (xi[1].astype(f32) + scale * centred).astype(bf16)
    outs[1].start()
    for copy in outs:
        copy.wait()


def per_device(
    stash_inputs, stash_grads, plan, query_weight, key_weight, value_weight, out_weight,
    input_gain, output_gain, query_gain, key_gain,
):
    hbm = pl.BlockSpec(memory_space=pl.ANY)
    smem = pl.BlockSpec(memory_space=pltpu.SMEM)
    V = pltpu.VMEM
    sem = pltpu.SemaphoreType.DMA
    act, g, xi = pl.pallas_call(
        kernel,
        out_shape=(jax.ShapeDtypeStruct((ROWS, D), bf16),) * 2
        + (jax.ShapeDtypeStruct((2, ROWS, D), bf16),),
        in_specs=[smem] + [hbm] * 10,
        out_specs=(hbm,) * 3,
        scratch_shapes=[
            V((2, D, 2 * HD), bf16), V((2, D, HD), bf16), V((2, D, HD), bf16), V((2, 2 * HD, D), bf16),
            V((4, ROWS, D), bf16), V((4, ROWS, D), bf16),
            V((3, 8, ROWS, D), bf16),
            V((2, 2 * TOK, HD), bf16), V((2 * TOK, HD), f32), V((TOK, HD), f32),
            V((2, 2, 5, TOK, HD), bf16), V((2, 2, TOK, HD), bf16), V((2, 2, TOK // 2, HD), bf16),
            V((2, 8, ROWS, 2 * HD), bf16),
            V((2 * TOK, 5 * TOK), f32), V((2 * TOK, 5 * TOK), bf16), V((2 * TOK, 5 * TOK), bf16),
            V((2 * TOK, HD), bf16),
            V((4, ROWS, D), bf16), V((3, 4, ROWS, D), bf16), V((2, 3, ROWS, D), bf16),
            V((3, 2, ROWS // 2, D), bf16), V((3, 2, ROWS, D), bf16), V((2, ROWS, D), f32),
            V((2, 4, TOK, HD), bf16), V((5, 2, TOK, HD), bf16), V((2, 3, TOK, HD), f32),
            V((8, ROWS, 4 * HD), bf16),
            V((ROWS, D), bf16), V((ROWS, D), bf16), V((TOK, HD // 2), f32), V((TOK, HD // 2), f32),
            V((2 * 4 * ROWS, D), f32), V((ROWS, D), bf16),
            V((2, D), f32), V((2, D), f32), V((2, HD), f32), V((2, HD), f32),
            V((2 * TOK, 1), f32), V((2 * TOK, 1), f32),
            sem((15,)), sem((3,)), sem((3, 7)), sem((3, 7)), sem((3, NCH, 4)),
            sem((2, 12)), sem((2, 10, 2)), sem((8, 2)), sem((5, 2)),
            sem((2, 2, 2)), sem((2, 2)), sem((2, 2)), sem((2, 2, 2)), sem((2, 2)), sem((2,)), sem((3 + NCH,)), sem((3 + NCH,)),
        ],
        compiler_params=pltpu.CompilerParams(
            collective_id=0, has_side_effects=True, vmem_limit_bytes=67043328
        ),
    )(
        plan, input_gain[0], output_gain[0], query_gain[0],
        key_gain[0], stash_inputs[0], stash_grads[0], query_weight[0], key_weight[0],
        value_weight[0], out_weight[0],
    )
    act, grad = pl.pallas_call(
        hand_on,
        out_shape=(jax.ShapeDtypeStruct((ROWS, D), bf16),) * 2,
        in_specs=[hbm] * 3,
        out_specs=(hbm, hbm),
        scratch_shapes=[V((ROWS, D), bf16), V((ROWS, D), bf16), V((2, ROWS, D), bf16), sem((5,))],
    )(act, g, xi)
    return act[None], grad[None]


def solution(mesh):
    return jax.shard_map(
        per_device,
        mesh=mesh,
        in_specs=(
            P("segment", None, ("ctx", "tp"), None),
            P("segment", None, ("ctx", "tp"), None),
            P("segment", None),
            P("segment", None, None, "tp"),
            P("segment", None, None, "tp"),
            P("segment", None, None, "tp"),
            P("segment", None, "tp", None),
            P("segment", None, None),
            P("segment", None, None),
            P("segment", None, None),
            P("segment", None, None),
        ),
        out_specs=(P("segment", ("ctx", "tp"), None), P("segment", ("ctx", "tp"), None)),
        check_vma=False,
    )
```
